32 devices in a mesh: grp: 4 (over y, x), tile: 8 (over z, core).
Axes of the slice: x: 2, y: 2, z: 4, core: 2. Of those that a mesh axis runs over, the one named last changes fastest.
Arguments:
- pool_input: float32 [32, 512, 256], P('grp', 'tile'), may hold values from 0 to 20
- weight_first: bfloat16 [3, 3, 256, 512], replicated, may hold values from -0.125 to 0.125
- weight_second: bfloat16 [3, 3, 512, 512], replicated, may hold values from -0.09375 to 0.09375
- targets: float32 [2, 512, 512], replicated, may hold values from -0.3 to 0.3
Outputs:
- image_grad: float32 [32, 512, 256], P('grp', 'tile')
The draws below stay inside these ranges and needn't reach their ends.
All inputs are finite; a program needn't handle non-finite values.
Results may differ from the reference program's by a relative error of at most 0.0028.
Values may be sent and summed in bfloat16 or wider, within the bound.
No kernel may reach another device: no remote copies, remote signals or barrier semaphores. Data moves between devices by JAX's collectives and lax.ppermute only.
A program may use at most 64 MiB of HBM per device.

```python
import jax
import jax.numpy as jnp
from jax import lax

C0 = 256
C1 = 512
H = 32
W = 512


def draw_pool_input(key, part):
    key_rough = jax.random.fold_in(key, 11)
    key_base = jax.random.fold_in(key, 12)
    ramp = 0.6 + 1.2 * jnp.arange(W, dtype=jnp.float32) / W
    rough = jnp.exp(jax.random.uniform(key_rough, (H, W, 1), jnp.float32, -0.7, 0.7))
    base = jnp.abs(jax.random.normal(key_base, (H, W, C0), jnp.float32))
    return jnp.clip(base * ramp[None, :, None] * rough, 0.0, 20.0)


def gaussian(stream_key, dims, spread, limit, kind=jnp.bfloat16):
    entries = spread * jax.random.normal(stream_key, dims, jnp.float32)
    return jnp.clip(entries, min=-limit, max=limit).astype(kind)


def setup_inputs(seed: int = 0) -> dict:
    seeds = jax.random.split(jax.random.key(seed), 5)
    return {
        "pool_input": draw_pool_input(jax.random.fold_in(seeds[4], 71), 0),
        "weight_first": gaussian(seeds[1], (3, 3, C0, C1), (9 * C0) ** -0.5, 0.125),
        "weight_second": gaussian(seeds[2], (3, 3, C1, C1), (9 * C1) ** -0.5, 0.09375),
        "targets": gaussian(seeds[3], (2, C1, C1), 0.05, 0.3, jnp.float32),
    }


GELU_SCALE = 0.7978845608
GELU_CUBIC = 0.044715


def gelu_value(values):
    return 0.5 * values * (1.0 + jnp.tanh(GELU_SCALE * (values + GELU_CUBIC * values ** 3)))


def gelu_slope(values):
    hyper = jnp.tanh(GELU_SCALE * (values + GELU_CUBIC * values ** 3))
    return 0.5 * (1.0 + hyper) + 0.5 * values * (1.0 - hyper * hyper) * GELU_SCALE * (1.0 + 3.0 * GELU_CUBIC * values * values)


def conv_fwd(padded, weight, height, breadth):
    summed = None
    for row_shift in range(3):
        for col_shift in range(3):
            window = padded[row_shift:row_shift + height, col_shift:col_shift + breadth, :].reshape(height * breadth, -1)
            product = jnp.dot(window, weight[row_shift, col_shift], preferred_element_type=jnp.float32)
            summed = product if summed is None else summed + product
    return summed.reshape(height, breadth, -1)


def conv_back(padded, weight, height, breadth):
    summed = None
    for row_shift in range(3):
        for col_shift in range(3):
            window = padded[2 - row_shift:2 - row_shift + height, 2 - col_shift:2 - col_shift + breadth, :].reshape(height * breadth, -1)
            product = lax.dot_general(window, weight[row_shift, col_shift], (((1,), (1,)), ((), ())), preferred_element_type=jnp.float32)
            summed = product if summed is None else summed + product
    return summed.reshape(height, breadth, -1)


def pad_one(values):
    return jnp.pad(values, ((1, 1), (1, 1), (0, 0)))


def push_back(feature, target):
    positions = H * W
    flat = feature.reshape(positions, -1)
    centred = flat - jnp.sum(flat, axis=0) / positions
    gram_matrix = lax.dot_general(centred, centred, (((0,), (0,)), ((), ())), precision=lax.Precision.HIGHEST, preferred_element_type=jnp.float32) / positions
    mismatch = gram_matrix - target
    symmetric = (mismatch + mismatch.T) * 0.5
    return jnp.dot(centred, symmetric, precision=lax.Precision.HIGHEST, preferred_element_type=jnp.float32).reshape(H, W, -1)


def reference(pool_input, weight_first, weight_second, targets):
    pool_bf = pool_input.astype(jnp.bfloat16)
    pre_first = conv_fwd(pad_one(pool_bf), weight_first, H, W)
    act_first = gelu_value(pre_first)
    pre_second = conv_fwd(pad_one(act_first.astype(jnp.bfloat16)), weight_second, H, W)
    act_second = gelu_value(pre_second)
    push_first = push_back(act_first, targets[0])
    push_second = push_back(act_second, targets[1])
    grad_second = (push_second * gelu_slope(pre_second)).astype(jnp.bfloat16)
    flow_first = push_first + conv_back(pad_one(grad_second), weight_second, H, W)
    grad_first = (flow_first * gelu_slope(pre_first)).astype(jnp.bfloat16)
    return conv_back(pad_one(grad_first), weight_first, H, W)
```

```python
import jax
import jax.numpy as jnp
from jax import lax
from jax.sharding import PartitionSpec as P

GELU_SCALE = 0.7978845608
GELU_CUBIC = 0.044715
REACH = 4
BLOCK = 128
BF = jnp.bfloat16
F32 = jnp.float32


def gelu_pair(values):
    hyper = jnp.tanh(GELU_SCALE * (values + GELU_CUBIC * values * values * values))
    act = 0.5 * values * (1.0 + hyper)
    slope = 0.5 * (1.0 + hyper) + 0.5 * values * (1.0 - hyper * hyper) * GELU_SCALE * (
        1.0 + 3.0 * GELU_CUBIC * values * values
    )
    return act, slope


def taps(padded, weight, back):
    height, breadth = padded.shape[0] - 2, padded.shape[1] - 2
    summed = None
    for a in range(3):
        for b in range(3):
            window = padded[a : a + height, b : b + breadth, :].reshape(height * breadth, -1)
            kernel = weight[2 - a, 2 - b] if back else weight[a, b]
            dims = (((1,), (1 if back else 0,)), ((), ()))
            product = lax.dot_general(window, kernel, dims, preferred_element_type=F32)
            summed = product if summed is None else summed + product
    return summed.reshape(height, breadth, -1)


def halo(pool, tiles, groups, core):
    right, left = pool[:, -REACH:], pool[:, :REACH]
    swap = [(i, i ^ 1) for i in range(tiles)]
    cross = [(i, i + 1) for i in range(1, tiles - 1, 2)]
    cross = cross + [(j, i) for i, j in cross]
    far = lax.ppermute(jnp.where(core == 0, left, right), "tile", cross)
    near = lax.ppermute(jnp.where(core == 0, right, left), "tile", swap)
    pool = jnp.concatenate(
        [jnp.where(core == 0, far, near), pool, jnp.where(core == 0, near, far)], axis=1
    )
    up = [(i, i + 1) for i in range(groups - 1)]
    down = [(j, i) for i, j in up]
    above = lax.ppermute(pool[-REACH:], "grp", up)
    below = lax.ppermute(pool[:REACH], "grp", down)
    return jnp.concatenate([above, pool, below], axis=0)


def pairs(width):
    blocks = width // BLOCK
    return [(i, j) for i in range(blocks) for j in range(i, blocks)]


def pack(matrix):
    width = matrix.shape[0]
    return jnp.concatenate(
        [
            matrix[i * BLOCK : (i + 1) * BLOCK, j * BLOCK : (j + 1) * BLOCK]
            for i, j in pairs(width)
        ],
        axis=0,
    )


def unpack(packed, width):
    blocks = width // BLOCK
    table = {}
    for n, (i, j) in enumerate(pairs(width)):
        table[i, j] = packed[n * BLOCK : (n + 1) * BLOCK]
        if i != j:
            table[j, i] = table[i, j].T
    return jnp.concatenate(
        [jnp.concatenate([table[i, j] for j in range(blocks)], axis=1) for i in range(blocks)],
        axis=0,
    )


def split(mean):
    high = mean.astype(BF)
    low = (mean - high.astype(F32)).astype(BF)
    rows = jnp.concatenate([high.reshape(-1, BLOCK), low.reshape(-1, BLOCK)], axis=0)
    return jnp.pad(rows, ((0, -rows.shape[0] % 16), (0, 0)))


def join(rows, width):
    half = width // BLOCK
    rows = rows.astype(F32)
    return (rows[:half] + rows[half : 2 * half]).reshape(-1)


def spread(means, count):
    centre = sum(means) / len(means)
    away = jnp.stack(means) - centre
    scatter = lax.dot_general(
        away, away, (((0,), (0,)), ((), ())), precision=lax.Precision.HIGHEST
    )
    return centre, pack(scatter * count)


def local(pool_input, weight_first, weight_second, targets):
    height, breadth = pool_input.shape[0], pool_input.shape[1]
    width = weight_first.shape[3]
    groups, tiles = lax.axis_size("grp"), lax.axis_size("tile")
    row, tile = lax.axis_index("grp"), lax.axis_index("tile")
    core = tile % 2
    cells = height * breadth
    positions = cells * groups * tiles

    def inside(rim):
        i = row * height - rim + jnp.arange(height + 2 * rim)
        j = tile * breadth - rim + jnp.arange(breadth + 2 * rim)
        i = (i >= 0) & (i < height * groups)
        j = (j >= 0) & (j < breadth * tiles)
        return (i[:, None] & j[None, :])[:, :, None]

    padded = halo(pool_input.astype(BF), tiles, groups, core)
    act_first, slope_first = gelu_pair(taps(padded, weight_first, False))
    first_bf = jnp.where(inside(3), act_first, 0.0).astype(BF)
    act_second, slope_second = gelu_pair(taps(first_bf, weight_second, False))

    def stats(act, rim):
        own = act[rim:-rim, rim:-rim].reshape(cells, width)
        mean = jnp.sum(own, axis=0) / cells
        own = (own - mean).astype(BF)
        return mean, pack(
            lax.dot_general(own, own, (((0,), (0,)), ((), ())), preferred_element_type=F32)
        )

    mean_first, gram_first = stats(act_first, 3)
    mean_second, gram_second = stats(act_second, 2)
    first_core = core == 0
    mean = jnp.where(first_core, mean_first, mean_second)
    gram = jnp.where(first_core, gram_first, gram_second)

    def message(part, vector):
        return jnp.concatenate([part.astype(BF), split(vector)], axis=0)

    swap = [(i, i ^ 1) for i in range(tiles)]
    sent = message(
        jnp.where(first_core, gram_second, gram_first),
        jnp.where(first_core, mean_second, mean_first),
    )
    got = lax.ppermute(sent, "tile", swap)
    rows = gram.shape[0]
    centre, extra = spread([mean, join(got[rows:], width)], cells)
    gram = gram + got[:rows].astype(F32) + extra
    chunk = rows // groups
    share = lax.dynamic_slice_in_dim(gram, row * chunk, chunk, 0)
    means, parts = [centre], [share]
    for k in range(1, groups):
        part = lax.dynamic_slice_in_dim(gram, (row ^ k) * chunk, chunk, 0)
        got = lax.ppermute(message(part, centre), "grp", [(i, i ^ k) for i in range(groups)])
        parts.append(got[:chunk].astype(F32))
        means.append(join(got[chunk:], width))
    centre, extra = spread(means, cells * 2)
    share = sum(parts) + lax.dynamic_slice_in_dim(extra, row * chunk, chunk, 0)
    sent = message(share, centre)
    means, parts = [centre], [share]
    for k in range(1, tiles // 2):
        got = lax.ppermute(sent, "tile", [(i, i ^ (2 * k)) for i in range(tiles)])
        parts.append(got[:chunk].astype(F32))
        means.append(join(got[chunk:], width))
    centre, extra = spread(means, cells * 2 * groups)
    share = sum(parts) + lax.dynamic_slice_in_dim(extra, row * chunk, chunk, 0)
    goal = [pack((t + t.T) * 0.5) for t in targets]
    goal = lax.dynamic_slice_in_dim(jnp.where(first_core, goal[0], goal[1]), row * chunk, chunk, 0)
    share = (share / positions - goal).astype(BF)
    whole = jnp.zeros((rows, BLOCK), BF)
    whole = lax.dynamic_update_slice_in_dim(whole, share, row * chunk, 0)
    for k in range(1, groups):
        got = lax.ppermute(share, "grp", [(i, i ^ k) for i in range(groups)])
        whole = lax.dynamic_update_slice_in_dim(whole, got, (row ^ k) * chunk, 0)
    mine = jnp.concatenate([whole, split(centre)], axis=0)
    other = lax.ppermute(mine, "tile", swap)

    def recentre(act, table):
        cen = act - join(table[rows:], width)
        flat = cen.reshape(-1, width).astype(BF)
        push = jnp.dot(flat, unpack(table[:rows], width), preferred_element_type=F32)
        return push.reshape(act.shape)

    push_second = recentre(act_second, jnp.where(first_core, other, mine))
    push_first = recentre(act_first[2:-2, 2:-2], jnp.where(first_core, mine, other))
    grad_second = jnp.where(inside(2), push_second * slope_second, 0.0).astype(BF)
    flow_first = push_first + taps(grad_second, weight_second, True)
    slope_first = slope_first[2:-2, 2:-2]
    grad_first = jnp.where(inside(1), flow_first * slope_first, 0.0).astype(BF)
    return taps(grad_first, weight_first, True)


def solution(mesh):
    return jax.shard_map(
        local,
        mesh=mesh,
        in_specs=(P("grp", "tile", None), P(), P(), P()),
        out_specs=P("grp", "tile", None),
        check_vma=False,
    )
```

```python
import functools

import jax
import jax.numpy as jnp
from jax import lax
from jax.experimental import pallas as pl
from jax.experimental.pallas import tpu as pltpu
from jax.sharding import PartitionSpec as P

GELU_SCALE = 0.7978845608
GELU_CUBIC = 0.044715
REACH = 4
BLOCK = 128
EXTRA = 16
BF = jnp.bfloat16
F32 = jnp.float32
VMEM = pl.BlockSpec(memory_space=pltpu.VMEM)
SMEM = pl.BlockSpec(memory_space=pltpu.SMEM)
MIB = 2**20


def gelu_pair(values):
    square = values * values
    hyper = jnp.tanh(GELU_SCALE * (values + GELU_CUBIC * values * square))
    half = 0.5 * (1.0 + hyper)
    slope = half + 0.5 * values * (1.0 - hyper * hyper) * (
        GELU_SCALE + 3.0 * GELU_SCALE * GELU_CUBIC * square
    )
    return values * half, slope


def pairs(width):
    blocks = width // BLOCK
    return [(i, j) for i in range(blocks) for j in range(i, blocks)]


def wide(mask, width):
    return jnp.concatenate([mask] * (width // BLOCK), axis=1)


def fill_mask(mask_ref, place_ref, rim, pitch, limits):
    rows = mask_ref.shape[0] // pitch
    col = lax.broadcasted_iota(jnp.int32, (pitch, BLOCK), 0) + (place_ref[2] - rim)
    inside = jnp.where((col >= 0) & (col < limits[1]), 1.0, 0.0).astype(F32)
    for r in range(rows):
        row = place_ref[1] - rim + r
        ok = jnp.where((row >= 0) & (row < limits[0]), 1.0, 0.0).astype(F32)
        mask_ref[r * pitch : (r + 1) * pitch, :] = inside * ok


def shifted(ref, base, step, offset):
    return ref[pl.ds(base, step + 8), :][offset : offset + step]


def spread_taps(flat_ref, base, out_ref, at, step):
    depth = flat_ref.shape[1]
    whole = flat_ref[pl.ds(base, step + 8), :]
    for b in range(3):
        out_ref[pl.ds(at, step), b * depth : (b + 1) * depth] = whole[b : b + step].astype(BF)


def conv(taps_ref, base, weight_ref, pitch, step):
    lhs = jnp.concatenate(
        [taps_ref[pl.ds(base + a * pitch, step), :] for a in range(3)], axis=1
    )
    return jnp.dot(lhs, weight_ref[...], preferred_element_type=F32)


def tiles_of(start, stop, step, body):
    def one(t, carry):
        body(pl.multiple_of(start + t * step, 16))
        return carry

    lax.fori_loop(0, (stop - start) // step, one, 0)


def put_mean(rows_ref, mean, parts):
    blocks = mean.shape[1] // BLOCK
    high = mean.astype(BF).astype(F32)
    for p, row in enumerate((high, mean - high) if parts == 2 else (mean,)):
        for j in range(blocks):
            at = p * blocks + j
            rows_ref[at : at + 1, :] = row[:, j * BLOCK : (j + 1) * BLOCK]


def get_mean(rows, blocks, parts):
    rows = rows.astype(F32)
    found = rows[:blocks] + rows[blocks : 2 * blocks] if parts == 2 else rows[:blocks]
    return jnp.concatenate([found[j : j + 1] for j in range(blocks)], axis=1)


def spread(means, count, left_ref, right_ref, emit):
    centre = means[0]
    for mean in means[1:]:
        centre = centre + mean
    centre = centre * (1.0 / len(means))
    left_ref[...] = jnp.zeros(left_ref.shape, F32)
    right_ref[...] = jnp.zeros(right_ref.shape, F32)
    for n, mean in enumerate(means):
        away = mean - centre
        high = away.astype(BF).astype(F32)
        low = away - high
        for q, (lhs, rhs) in enumerate(((high, high), (high, low), (low, high))):
            at = 3 * n + q
            left_ref[at : at + 1, :] = lhs
            right_ref[at : at + 1, :] = rhs
    lhs, rhs = left_ref[...].astype(BF), right_ref[...].astype(BF)
    for n, (i, j) in enumerate(pairs(lhs.shape[1])):
        product = lax.dot_general(
            lhs[:, i * BLOCK : (i + 1) * BLOCK],
            rhs[:, j * BLOCK : (j + 1) * BLOCK],
            (((0,), (0,)), ((), ())),
            preferred_element_type=F32,
        )
        emit(n, product * float(count))
    return centre


def front(dims, place, pool, far, near, above, below, w1, w2, *rest):
    (act1, slope1, act2, slope2, keep, mine, sent) = rest[:7]
    (flat, taps1, taps2, own, gram, stat, mask) = rest[7:]
    height, breadth, pitch, limits = dims
    step = 2 * pitch
    width = w1.shape[1]
    blocks = width // BLOCK
    flat[...] = jnp.zeros(flat.shape, F32)
    left_core = place[0] == 0
    for r in range(height):
        at = (r + REACH) * pitch
        one, two = far[r].astype(F32), near[r].astype(F32)
        flat[at : at + REACH, :] = jnp.where(left_core, one, two)
        flat[at + REACH : at + REACH + breadth, :] = pool[r]
        flat[at + REACH + breadth : at + 2 * REACH + breadth, :] = jnp.where(left_core, two, one)
    for r in range(REACH):
        at = r * pitch
        flat[at : at + breadth + 2 * REACH, :] = above[r].astype(F32)
        at = (r + REACH + height) * pitch
        flat[at : at + breadth + 2 * REACH, :] = below[r].astype(F32)
    fill_mask(mask, place, 3, pitch, limits)
    tiles_of(
        0, (height + 8) * pitch, step, lambda at: spread_taps(flat, at, taps1, at, step)
    )

    def first(at):
        act, slope = gelu_pair(conv(taps1, at, w1, pitch, step))
        act1[pl.ds(at, step), :] = act * wide(mask[pl.ds(at, step), :], width)
        slope1[pl.ds(at, step), :] = slope

    rows1 = (height + 6) * pitch
    act1[rows1:, :] = jnp.zeros((act1.shape[0] - rows1, width), F32)
    tiles_of(0, rows1, step, first)
    tiles_of(step, rows1 - step, step, lambda at: spread_taps(act1, at, taps2, at, step))

    def second(at):
        act, slope = gelu_pair(conv(taps2, at, w2, pitch, step))
        act2[pl.ds(at - step, step), :] = act
        slope2[pl.ds(at - step, step), :] = slope

    tiles_of(step, step + height * pitch, step, second)
    cells = height * breadth
    for layer, (act, offset) in enumerate(((act1, 3 * pitch + 3), (act2, 2))):
        total = jnp.zeros((8, width), F32)
        for r in range(height):
            cut = act[offset + r * pitch : offset + r * pitch + breadth, :]
            own[r * breadth : (r + 1) * breadth, :] = cut
            total = total + jnp.sum(cut.reshape(breadth // 8, 8, width), axis=0)
        mean = jnp.sum(total, axis=0, keepdims=True) * (1.0 / cells)
        centred = (own[...] - mean).astype(BF)
        n = 0
        for i in range(blocks):
            panel = lax.dot_general(
                centred[:, i * BLOCK : (i + 1) * BLOCK],
                centred[:, i * BLOCK :],
                (((0,), (0,)), ((), ())),
                preferred_element_type=F32,
            )
            for j in range(i, blocks):
                gram[layer, n * BLOCK : (n + 1) * BLOCK, :] = panel[
                    :, (j - i) * BLOCK : (j - i + 1) * BLOCK
                ]
                n += 1
        stat[layer] = jnp.zeros(stat.shape[1:], F32)
        put_mean(stat.at[layer, 0:EXTRA], mean, 2)
        put_mean(stat.at[layer, EXTRA : 2 * EXTRA], mean, 1)
    rows = keep.shape[0]
    keep[...] = gram[place[0]]
    mine[...] = stat[place[0], EXTRA : EXTRA + 8, :]
    sent[0:rows, :] = gram[1 - place[0]].astype(BF)
    sent[rows:, :] = stat[1 - place[0], 0:EXTRA, :].astype(BF)


def ring(dims, act1, w2, act2, slope2, taps2):
    height, _, pitch, _ = dims
    step = 2 * pitch
    for n, start in enumerate((0, (height + 2) * pitch)):
        for q in range(2):
            spread_taps(act1, start + q * step, taps2, q * step, step)
        act, slope = gelu_pair(conv(taps2, 0, w2, pitch, step))
        act2[n * step : (n + 1) * step, :] = act
        slope2[n * step : (n + 1) * step, :] = slope


def write_message(ref, part, rows_ref, centre):
    count = part.shape[0]
    rows_ref[...] = jnp.zeros(rows_ref.shape, F32)
    put_mean(rows_ref, centre, 2)
    ref[0:count, :] = part.astype(BF)
    ref[count:, :] = rows_ref[...].astype(BF)


def merge_pair(dims, place, keep, mine, got, share, centre_out, *rest):
    count, groups, blocks = dims
    messages, (full, left, right, rows_ref) = rest[: groups - 1], rest[groups - 1 :]
    rows = keep.shape[0]
    chunk = rows // groups

    def emit(n, product):
        at = slice(n * BLOCK, (n + 1) * BLOCK)
        full[at, :] = keep[at, :] + got[at, :].astype(F32) + product

    means = [get_mean(mine[...], blocks, 1), get_mean(got[rows:, :], blocks, 2)]
    centre = spread(means, count, left, right, emit)
    centre_out[...] = jnp.zeros(centre_out.shape, F32)
    put_mean(centre_out, centre, 1)
    for k, ref in enumerate(messages, 1):
        at = pl.multiple_of((place[3] ^ k) * chunk, 16)
        write_message(ref, full[pl.ds(at, chunk), :], rows_ref, centre)
    share[...] = full[pl.ds(pl.multiple_of(place[3] * chunk, 16), chunk), :]


def merge_many(dims, final, place, share, mine, *rest):
    count, members, blocks = dims
    gots, rest = rest[: members - 1], rest[members - 1 :]
    chunk = share.shape[0]
    full, left, right, rows_ref = rest[-4:]

    def emit(n, product):
        full[n * BLOCK : (n + 1) * BLOCK, :] = product

    means = [get_mean(mine[...], blocks, 1)]
    means += [get_mean(got[chunk:, :], blocks, 2) for got in gots]
    centre = spread(means, count, left, right, emit)
    total = share[...] + full[pl.ds(pl.multiple_of(place[3] * chunk, 16), chunk), :]
    for got in gots:
        total = total + got[0:chunk, :].astype(F32)
    if final is None:
        out, centre_out, sent = rest[:3]
        out[...] = total
        centre_out[...] = jnp.zeros(centre_out.shape, F32)
        put_mean(centre_out, centre, 1)
        write_message(sent, total, rows_ref, centre)
    else:
        goal, sent, centre_out = rest[:3]
        rows_ref[...] = jnp.zeros(rows_ref.shape, F32)
        put_mean(rows_ref, centre, 2)
        centre_out[...] = rows_ref[...].astype(BF)
        sent[...] = (total * (1.0 / final) - goal[...]).astype(BF)


def assemble(place, share, centre, *rest):
    gots, out = rest[:-1], rest[-1]
    chunk = share.shape[0]
    for k, ref in enumerate((share,) + tuple(gots)):
        out[pl.ds(pl.multiple_of((place[3] ^ k) * chunk, 16), chunk), :] = ref[...]
    rows = chunk * (len(gots) + 1)
    out[rows:, :] = centre[...]


def back(dims, place, act1, slope1, act2, slope2, act2r, slope2r, mine, other, w2, w1, out, *scratch):
    (flat2, taps2, flat1, taps1, first_m, second_m, table, mask) = scratch
    height, breadth, pitch, limits = dims
    step = 2 * pitch
    width = act1.shape[1]
    blocks = width // BLOCK
    packed = table.shape[1] - EXTRA
    table[place[0]] = mine[...]
    table[1 - place[0]] = other[...]
    means = []
    for layer, ref in enumerate((first_m, second_m)):
        for n, (i, j) in enumerate(pairs(width)):
            block = table[layer, n * BLOCK : (n + 1) * BLOCK, :]
            ref[i * BLOCK : (i + 1) * BLOCK, j * BLOCK : (j + 1) * BLOCK] = block
            if i != j:
                ref[j * BLOCK : (j + 1) * BLOCK, i * BLOCK : (i + 1) * BLOCK] = (
                    block.astype(F32).T.astype(BF)
                )
        means.append(get_mean(table[layer, packed:, :], blocks, 2))
    fill_mask(mask, place, 3, pitch, limits)

    def second(act, slope, at, to):
        centred = (act[pl.ds(at, step), :] - means[1]).astype(BF)
        push = jnp.dot(centred, second_m[...], preferred_element_type=F32)
        allow = wide(shifted(mask, to + pitch, step, 1), width)
        flat2[pl.ds(to, step), :] = push * slope[pl.ds(at, step), :] * allow

    rows2 = (height + 4) * pitch
    flat2[rows2:, :] = jnp.zeros((flat2.shape[0] - rows2, width), F32)
    second(act2r, slope2r, 0, 0)
    second(act2r, slope2r, step, rows2 - step)
    tiles_of(
        0, height * pitch, step, lambda at: second(act2, slope2, at, pl.multiple_of(at + step, 16))
    )
    tiles_of(0, rows2, step, lambda at: spread_taps(flat2, at, taps2, at, step))
    rows1 = (height + 2) * pitch
    flat1[rows1:, :] = jnp.zeros((flat1.shape[0] - rows1, width), F32)

    def first(at):
        near = pl.multiple_of(at + 2 * pitch, 16)
        centred = (shifted(act1, near, step, 2) - means[0]).astype(BF)
        flow = conv(taps2, at, w2, pitch, step) + jnp.dot(
            centred, first_m[...], preferred_element_type=F32
        )
        allow = wide(shifted(mask, near, step, 2), width)
        flat1[pl.ds(at, step), :] = flow * shifted(slope1, near, step, 2) * allow

    tiles_of(0, rows1, step, first)
    tiles_of(0, rows1, step, lambda at: spread_taps(flat1, at, taps1, at, step))

    def last(t, carry):
        got = conv(taps1, pl.multiple_of(t * step, 16), w1, pitch, step)
        out[2 * t] = got[0:breadth]
        out[2 * t + 1] = got[pitch : pitch + breadth]
        return carry

    lax.fori_loop(0, height // 2, last, 0)


def call(body, ins, outs, scratch, flops=0, limit=None, name=None):
    moved = sum(x.size * x.dtype.itemsize for x in ins) + sum(
        x.size * x.dtype.itemsize for x in outs
    )
    return pl.pallas_call(
        body,
        out_shape=tuple(outs),
        in_specs=[SMEM if x.dtype == jnp.int32 else VMEM for x in ins],
        out_specs=tuple(VMEM for _ in outs),
        scratch_shapes=scratch,
        compiler_params=pltpu.CompilerParams(vmem_limit_bytes=(limit or 8) * MIB),
        cost_estimate=pl.CostEstimate(flops=flops, bytes_accessed=moved, transcendentals=0),
        name=name,
    )(*ins)


def shape(dims, dtype):
    return jax.ShapeDtypeStruct(dims, dtype)


def transposed(weight):
    flipped = weight[::-1, ::-1].transpose(0, 1, 3, 2)
    return flipped.reshape(-1, weight.shape[2])


def local(pool_input, weight_first, weight_second, targets):
    height, breadth, depth = pool_input.shape
    width = weight_first.shape[3]
    groups, tiles = lax.axis_size("grp"), lax.axis_size("tile")
    chips = tiles // 2
    row, tile = lax.axis_index("grp"), lax.axis_index("tile")
    core = tile % 2
    cells = height * breadth
    positions = cells * groups * tiles
    pitch = -(-(breadth + 2 * REACH) // 16) * 16
    step = 2 * pitch
    blocks = width // BLOCK
    place = jnp.stack([core, row * height, tile * breadth, row]).astype(jnp.int32)
    dims = (height, breadth, pitch, (height * groups, breadth * tiles))
    swap = [(i, i ^ 1) for i in range(tiles)]
    cross = [(i, i + 1) for i in range(1, tiles - 1, 2)]
    cross = cross + [(j, i) for i, j in cross]

    first_core = core == 0
    right = pool_input[:, -REACH:].astype(BF)
    left = pool_input[:, :REACH].astype(BF)
    far = lax.ppermute(jnp.where(first_core, left, right), "tile", cross)
    near = lax.ppermute(jnp.where(first_core, right, left), "tile", swap)

    def band(part):
        rows = slice(0, REACH) if part == 0 else slice(height - REACH, height)
        one, two = far[rows], near[rows]
        middle = pool_input[rows].astype(BF)
        return jnp.concatenate(
            [jnp.where(first_core, one, two), middle, jnp.where(first_core, two, one)], axis=1
        )

    up = [(i, i + 1) for i in range(groups - 1)]
    down = [(j, i) for i, j in up]
    above = lax.ppermute(band(1), "grp", up)
    below = lax.ppermute(band(0), "grp", down)

    rows0, rows1, rows2 = ((height + n) * pitch for n in (8, 6, 0))
    packed = len(pairs(width)) * BLOCK
    w1 = weight_first.reshape(-1, width)
    w2 = weight_second.reshape(-1, width)
    act1, slope1, act2, slope2, keep, mine, sent = call(
        functools.partial(front, dims),
        [place, pool_input, far, near, above, below, w1, w2],
        [
            shape((rows1 + 16, width), F32),
            shape((rows1, width), F32),
            shape((rows2, width), F32),
            shape((rows2, width), F32),
            shape((packed, BLOCK), F32),
            shape((8, BLOCK), F32),
            shape((packed + EXTRA, BLOCK), BF),
        ],
        [
            pltpu.VMEM((rows0 + 16, depth), F32),
            pltpu.VMEM((rows0, 3 * depth), BF),
            pltpu.VMEM((rows1, 3 * width), BF),
            pltpu.VMEM((cells, width), F32),
            pltpu.VMEM((2, packed, BLOCK), F32),
            pltpu.VMEM((2, 2 * EXTRA, BLOCK), F32),
            pltpu.VMEM((rows1, BLOCK), F32),
        ],
        flops=2 * 9 * width * (rows1 * depth + rows2 * width),
        limit=30,
        name="front",
    )
    act2r, slope2r = call(
        functools.partial(ring, dims),
        [act1, w2],
        [shape((2 * step, width), F32)] * 2,
        [pltpu.VMEM((2 * step, 3 * width), BF)],
        flops=2 * 9 * width * width * 2 * step,
        limit=16,
        name="ring",
    )
    goal = jnp.where(first_core, targets[0], targets[1])
    goal = (goal + goal.T) * 0.5
    goal = jnp.concatenate(
        [
            goal[i * BLOCK : (i + 1) * BLOCK, j * BLOCK : (j + 1) * BLOCK]
            for i, j in pairs(width)
        ],
        axis=0,
    )
    chunk = packed // groups
    goal = lax.dynamic_slice_in_dim(goal, row * chunk, chunk, 0)

    def helpers(members):
        deep = -(-3 * members // 16) * 16
        return [
            pltpu.VMEM((packed, BLOCK), F32),
            pltpu.VMEM((deep, width), F32),
            pltpu.VMEM((deep, width), F32),
            pltpu.VMEM((EXTRA, BLOCK), F32),
        ]

    message = shape((chunk + EXTRA, BLOCK), BF)
    part, centre = shape((chunk, BLOCK), F32), shape((8, BLOCK), F32)
    got = lax.ppermute(sent, "tile", swap)
    share, mean, *sents = call(
        functools.partial(merge_pair, (cells, groups, blocks)),
        [place, keep, mine, got],
        [part, centre] + [message] * (groups - 1),
        helpers(2),
        name="merge_cores",
    )
    gots = [
        lax.ppermute(sents[k - 1], "grp", [(i, i ^ k) for i in range(groups)])
        for k in range(1, groups)
    ]
    share, mean, sent = call(
        functools.partial(merge_many, (2 * cells, groups, blocks), None),
        [place, share, mean] + gots,
        [part, centre, message],
        helpers(groups),
        name="merge_groups",
    )
    gots = [
        lax.ppermute(sent, "tile", [(i, i ^ (2 * k)) for i in range(tiles)])
        for k in range(1, chips)
    ]
    share, mean = call(
        functools.partial(merge_many, (2 * groups * cells, chips, blocks), positions),
        [place, share, mean] + gots + [goal],
        [shape((chunk, BLOCK), BF), shape((EXTRA, BLOCK), BF)],
        helpers(chips),
        name="merge_chips",
    )
    gots = [
        lax.ppermute(share, "grp", [(i, i ^ k) for i in range(groups)])
        for k in range(1, groups)
    ]
    table = shape((packed + EXTRA, BLOCK), BF)
    (mine,) = call(assemble, [place, share, mean] + gots, [table], [], name="assemble")
    other = lax.ppermute(mine, "tile", swap)
    rows_b, rows_d = (height + 4) * pitch, (height + 2) * pitch
    (out,) = call(
        functools.partial(back, dims),
        [place, act1, slope1, act2, slope2, act2r, slope2r, mine, other]
        + [transposed(weight_second), transposed(weight_first)],
        [shape(pool_input.shape, F32)],
        [
            pltpu.VMEM((rows_b + 16, width), F32),
            pltpu.VMEM((rows_b, 3 * width), BF),
            pltpu.VMEM((rows_d + 16, width), F32),
            pltpu.VMEM((rows_d, 3 * width), BF),
            pltpu.VMEM((width, width), BF),
            pltpu.VMEM((width, width), BF),
            pltpu.VMEM((2, packed + EXTRA, BLOCK), BF),
            pltpu.VMEM((rows1, BLOCK), F32),
        ],
        flops=2 * 9 * width * (rows_d * width + rows2 * depth),
        limit=32,
        name="back",
    )
    return out


def solution(mesh):
    return jax.shard_map(
        local,
        mesh=mesh,
        in_specs=(P("grp", "tile", None), P(), P(), P()),
        out_specs=P("grp", "tile", None),
        check_vma=False,
    )
```

```python
import functools

import jax
import jax.numpy as jnp
from jax import lax
from jax.experimental import pallas as pl
from jax.experimental.pallas import tpu as pltpu
from jax.sharding import PartitionSpec as P

GELU_SCALE = 0.7978845608
GELU_CUBIC = 0.044715
REACH = 4
BLOCK = 128
EXTRA = 16
BF = jnp.bfloat16
F32 = jnp.float32
VMEM = pl.BlockSpec(memory_space=pltpu.VMEM)
SMEM = pl.BlockSpec(memory_space=pltpu.SMEM)
MIB = 2**20


def gelu_pair(values):
    square = values * values
    hyper = jnp.tanh(GELU_SCALE * (values + GELU_CUBIC * values * square))
    half = 0.5 * (1.0 + hyper)
    slope = half + 0.5 * values * (1.0 - hyper * hyper) * (
        GELU_SCALE + 3.0 * GELU_SCALE * GELU_CUBIC * square
    )
    return values * half, slope


def pairs(width):
    blocks = width // BLOCK
    return [(i, j) for i in range(blocks) for j in range(i, blocks)]


def wide(mask, width):
    return jnp.concatenate([mask] * (width // BLOCK), axis=1)


def fill_mask(mask_ref, place_ref, rim, pitch, limits):
    rows = mask_ref.shape[0] // pitch
    col = lax.broadcasted_iota(jnp.int32, (pitch, BLOCK), 0) + (place_ref[2] - rim)
    inside = jnp.where((col >= 0) & (col < limits[1]), 1.0, 0.0).astype(F32)
    for r in range(rows):
        row = place_ref[1] - rim + r
        ok = jnp.where((row >= 0) & (row < limits[0]), 1.0, 0.0).astype(F32)
        mask_ref[r * pitch : (r + 1) * pitch, :] = inside * ok


def shifted(ref, base, step, offset):
    return ref[pl.ds(base, step + 8), :][offset : offset + step]


def spread_taps(flat_ref, base, out_ref, at, step):
    depth = flat_ref.shape[1]
    whole = flat_ref[pl.ds(base, step + 8), :]
    for b in range(3):
        out_ref[pl.ds(at, step), b * depth : (b + 1) * depth] = whole[b : b + step].astype(BF)


def conv(taps_ref, base, weight_ref, pitch, step):
    lhs = jnp.concatenate(
        [taps_ref[pl.ds(base + a * pitch, step), :] for a in range(3)], axis=1
    )
    return jnp.dot(lhs, weight_ref[...], preferred_element_type=F32)


def tiles_of(start, stop, step, body):
    def one(t, carry):
        body(pl.multiple_of(start + t * step, 16))
        return carry

    lax.fori_loop(0, (stop - start) // step, one, 0)


def put_mean(rows_ref, mean, parts):
    blocks = mean.shape[1] // BLOCK
    high = mean.astype(BF).astype(F32)
    for p, row in enumerate((high, mean - high) if parts == 2 else (mean,)):
        for j in range(blocks):
            at = p * blocks + j
            rows_ref[at : at + 1, :] = row[:, j * BLOCK : (j + 1) * BLOCK]


def get_mean(rows, blocks, parts):
    rows = rows.astype(F32)
    found = rows[:blocks] + rows[blocks : 2 * blocks] if parts == 2 else rows[:blocks]
    return jnp.concatenate([found[j : j + 1] for j in range(blocks)], axis=1)


def spread(means, count, left_ref, right_ref, emit):
    centre = means[0]
    for mean in means[1:]:
        centre = centre + mean
    centre = centre * (1.0 / len(means))
    left_ref[...] = jnp.zeros(left_ref.shape, F32)
    right_ref[...] = jnp.zeros(right_ref.shape, F32)
    for n, mean in enumerate(means):
        away = mean - centre
        high = away.astype(BF).astype(F32)
        low = away - high
        for q, (lhs, rhs) in enumerate(((high, high), (high, low), (low, high))):
            at = 3 * n + q
            left_ref[at : at + 1, :] = lhs
            right_ref[at : at + 1, :] = rhs
    lhs, rhs = left_ref[...].astype(BF), right_ref[...].astype(BF)
    for n, (i, j) in enumerate(pairs(lhs.shape[1])):
        product = lax.dot_general(
            lhs[:, i * BLOCK : (i + 1) * BLOCK],
            rhs[:, j * BLOCK : (j + 1) * BLOCK],
            (((0,), (0,)), ((), ())),
            preferred_element_type=F32,
        )
        emit(n, product * float(count))
    return centre


def front(dims, place, pool, far, near, above, below, w1, w2, *rest):
    (act1, slope1, act2, slope2, keep, mine, sent) = rest[:7]
    (flat, taps1, taps2, own, gram, stat, mask) = rest[7:]
    height, breadth, pitch, limits = dims
    step = 2 * pitch
    width = w1.shape[1]
    blocks = width // BLOCK
    flat[...] = jnp.zeros(flat.shape, F32)
    left_core = place[0] == 0
    for r in range(height):
        at = (r + REACH) * pitch
        one, two = far[r].astype(F32), near[r].astype(F32)
        flat[at : at + REACH, :] = jnp.where(left_core, one, two)
        flat[at + REACH : at + REACH + breadth, :] = pool[r]
        flat[at + REACH + breadth : at + 2 * REACH + breadth, :] = jnp.where(left_core, two, one)
    for r in range(REACH):
        at = r * pitch
        flat[at : at + breadth + 2 * REACH, :] = above[r].astype(F32)
        at = (r + REACH + height) * pitch
        flat[at : at + breadth + 2 * REACH, :] = below[r].astype(F32)
    fill_mask(mask, place, 3, pitch, limits)
    tiles_of(
        0, (height + 8) * pitch, step, lambda at: spread_taps(flat, at, taps1, at, step)
    )

    def first(at):
        act, slope = gelu_pair(conv(taps1, at, w1, pitch, step))
        act1[pl.ds(at, step), :] = act * wide(mask[pl.ds(at, step), :], width)
        slope1[pl.ds(at, step), :] = slope

    rows1 = (height + 6) * pitch
    act1[rows1:, :] = jnp.zeros((act1.shape[0] - rows1, width), F32)
    tiles_of(0, rows1, step, first)
    tiles_of(step, rows1 - step, step, lambda at: spread_taps(act1, at, taps2, at, step))

    def second(at):
        act, slope = gelu_pair(conv(taps2, at, w2, pitch, step))
        act2[pl.ds(at - step, step), :] = act
        slope2[pl.ds(at - step, step), :] = slope

    tiles_of(step, step + height * pitch, step, second)
    cells = height * breadth
    for layer, (act, offset) in enumerate(((act1, 3 * pitch + 3), (act2, 2))):
        total = jnp.zeros((8, width), F32)
        for r in range(height):
            cut = act[offset + r * pitch : offset + r * pitch + breadth, :]
            own[r * breadth : (r + 1) * breadth, :] = cut
            total = total + jnp.sum(cut.reshape(breadth // 8, 8, width), axis=0)
        mean = jnp.sum(total, axis=0, keepdims=True) * (1.0 / cells)
        centred = (own[...] - mean).astype(BF)
        n = 0
        for i in range(blocks):
            panel = lax.dot_general(
                centred[:, i * BLOCK : (i + 1) * BLOCK],
                centred[:, i * BLOCK :],
                (((0,), (0,)), ((), ())),
                preferred_element_type=F32,
            )
            for j in range(i, blocks):
                gram[layer, n * BLOCK : (n + 1) * BLOCK, :] = panel[
                    :, (j - i) * BLOCK : (j - i + 1) * BLOCK
                ]
                n += 1
        stat[layer] = jnp.zeros(stat.shape[1:], F32)
        put_mean(stat.at[layer, 0:EXTRA], mean, 2)
        put_mean(stat.at[layer, EXTRA : 2 * EXTRA], mean, 1)
    rows = keep.shape[0]
    keep[...] = gram[place[0]]
    mine[...] = stat[place[0], EXTRA : EXTRA + 8, :]
    sent[0:rows, :] = gram[1 - place[0]].astype(BF)
    sent[rows:, :] = stat[1 - place[0], 0:EXTRA, :].astype(BF)


def ring(dims, act1, w2, act2, slope2, taps2):
    height, _, pitch, _ = dims
    step = 2 * pitch
    for n, start in enumerate((0, (height + 2) * pitch)):
        for q in range(2):
            spread_taps(act1, start + q * step, taps2, q * step, step)
        act, slope = gelu_pair(conv(taps2, 0, w2, pitch, step))
        act2[n * step : (n + 1) * step, :] = act
        slope2[n * step : (n + 1) * step, :] = slope


def write_message(ref, part, rows_ref, centre):
    count = part.shape[0]
    rows_ref[...] = jnp.zeros(rows_ref.shape, F32)
    put_mean(rows_ref, centre, 2)
    ref[0:count, :] = part.astype(BF)
    ref[count:, :] = rows_ref[...].astype(BF)


def merge_pair(dims, place, keep, mine, got, share, centre_out, *rest):
    count, groups, blocks = dims
    messages, (full, left, right, rows_ref) = rest[: groups - 1], rest[groups - 1 :]
    rows = keep.shape[0]
    chunk = rows // groups

    def emit(n, product):
        at = slice(n * BLOCK, (n + 1) * BLOCK)
        full[at, :] = keep[at, :] + got[at, :].astype(F32) + product

    means = [get_mean(mine[...], blocks, 1), get_mean(got[rows:, :], blocks, 2)]
    centre = spread(means, count, left, right, emit)
    centre_out[...] = jnp.zeros(centre_out.shape, F32)
    put_mean(centre_out, centre, 1)
    for k, ref in enumerate(messages, 1):
        at = pl.multiple_of((place[3] ^ k) * chunk, 16)
        write_message(ref, full[pl.ds(at, chunk), :], rows_ref, centre)
    share[...] = full[pl.ds(pl.multiple_of(place[3] * chunk, 16), chunk), :]


def merge_many(dims, final, place, share, mine, *rest):
    count, members, blocks = dims
    gots, rest = rest[: members - 1], rest[members - 1 :]
    chunk = share.shape[0]
    full, left, right, rows_ref = rest[-4:]

    def emit(n, product):
        full[n * BLOCK : (n + 1) * BLOCK, :] = product

    means = [get_mean(mine[...], blocks, 1)]
    means += [get_mean(got[chunk:, :], blocks, 2) for got in gots]
    centre = spread(means, count, left, right, emit)
    total = share[...] + full[pl.ds(pl.multiple_of(place[3] * chunk, 16), chunk), :]
    for got in gots:
        total = total + got[0:chunk, :].astype(F32)
    if final is None:
        out, centre_out, sent = rest[:3]
        out[...] = total
        centre_out[...] = jnp.zeros(centre_out.shape, F32)
        put_mean(centre_out, centre, 1)
        write_message(sent, total, rows_ref, centre)
    else:
        goal, sent, centre_out = rest[:3]
        rows_ref[...] = jnp.zeros(rows_ref.shape, F32)
        put_mean(rows_ref, centre, 2)
        centre_out[...] = rows_ref[...].astype(BF)
        sent[...] = (total * (1.0 / final) - goal[...]).astype(BF)


def assemble(place, share, centre, *rest):
    gots, out = rest[:-1], rest[-1]
    chunk = share.shape[0]
    for k, ref in enumerate((share,) + tuple(gots)):
        out[pl.ds(pl.multiple_of((place[3] ^ k) * chunk, 16), chunk), :] = ref[...]
    rows = chunk * (len(gots) + 1)
    out[rows:, :] = centre[...]


def back(dims, place, act1, slope1, act2, slope2, act2r, slope2r, mine, other, w2, w1, out, *scratch):
    (flat2, taps2, flat1, taps1, first_m, second_m, table, mask) = scratch
    height, breadth, pitch, limits = dims
    step = 2 * pitch
    width = act1.shape[1]
    blocks = width // BLOCK
    packed = table.shape[1] - EXTRA
    table[place[0]] = mine[...]
    table[1 - place[0]] = other[...]
    means = []
    for layer, ref in enumerate((first_m, second_m)):
        for n, (i, j) in enumerate(pairs(width)):
            block = table[layer, n * BLOCK : (n + 1) * BLOCK, :]
            ref[i * BLOCK : (i + 1) * BLOCK, j * BLOCK : (j + 1) * BLOCK] = block
            if i != j:
                ref[j * BLOCK : (j + 1) * BLOCK, i * BLOCK : (i + 1) * BLOCK] = (
                    block.astype(F32).T.astype(BF)
                )
        means.append(get_mean(table[layer, packed:, :], blocks, 2))
    fill_mask(mask, place, 3, pitch, limits)

    def second(act, slope, at, to):
        centred = (act[pl.ds(at, step), :] - means[1]).astype(BF)
        push = jnp.dot(centred, second_m[...], preferred_element_type=F32)
        allow = wide(shifted(mask, to + pitch, step, 1), width)
        flat2[pl.ds(to, step), :] = push * slope[pl.ds(at, step), :] * allow

    rows2 = (height + 4) * pitch
    flat2[rows2:, :] = jnp.zeros((flat2.shape[0] - rows2, width), F32)
    second(act2r, slope2r, 0, 0)
    second(act2r, slope2r, step, rows2 - step)
    tiles_of(
        0, height * pitch, step, lambda at: second(act2, slope2, at, pl.multiple_of(at + step, 16))
    )
    tiles_of(0, rows2, step, lambda at: spread_taps(flat2, at, taps2, at, step))
    rows1 = (height + 2) * pitch
    flat1[rows1:, :] = jnp.zeros((flat1.shape[0] - rows1, width), F32)

    def first(at):
        near = pl.multiple_of(at + 2 * pitch, 16)
        centred = (shifted(act1, near, step, 2) - means[0]).astype(BF)
        flow = conv(taps2, at, w2, pitch, step) + jnp.dot(
            centred, first_m[...], preferred_element_type=F32
        )
        allow = wide(shifted(mask, near, step, 2), width)
        flat1[pl.ds(at, step), :] = flow * shifted(slope1, near, step, 2) * allow

    tiles_of(0, rows1, step, first)
    tiles_of(0, rows1, step, lambda at: spread_taps(flat1, at, taps1, at, step))

    def last(t, carry):
        got = conv(taps1, pl.multiple_of(t * step, 16), w1, pitch, step)
        out[2 * t] = got[0:breadth]
        out[2 * t + 1] = got[pitch : pitch + breadth]
        return carry

    lax.fori_loop(0, height // 2, last, 0)


def edges(place, pool, far, near):
    breadth = pool.shape[1]
    left_core = place[0] == 0
    left = pool[:, 0:REACH, :]
    right = pool[:, breadth - REACH : breadth, :]
    far[...] = jnp.where(left_core, left, right).astype(BF)
    near[...] = jnp.where(left_core, right, left).astype(BF)


def bands(place, pool, far, near, above, below, row):
    height, breadth, _ = pool.shape
    left_core = place[0] == 0
    for start, ref in ((height - REACH, above), (0, below)):
        for r in range(REACH):
            one, two = far[start + r].astype(F32), near[start + r].astype(F32)
            row[0:REACH, :] = jnp.where(left_core, one, two)
            row[REACH : REACH + breadth, :] = pool[start + r]
            row[REACH + breadth :, :] = jnp.where(left_core, two, one)
            ref[r] = row[...].astype(BF)


def flip(weight, out):
    taps, _, width = weight.shape

    def one(t, carry):
        at = pl.multiple_of(t * width, 16)
        out[pl.ds(at, width), :] = weight[taps - 1 - t].T
        return carry

    lax.fori_loop(0, taps, one, 0)


def aim(place, targets, goal, full):
    core = place[0]
    chunk = goal.shape[0]
    for n, (i, j) in enumerate(pairs(targets.shape[1])):
        rows, cols = slice(i * BLOCK, (i + 1) * BLOCK), slice(j * BLOCK, (j + 1) * BLOCK)
        block = (targets[core, rows, cols] + targets[core, cols, rows].T) * 0.5
        full[n * BLOCK : (n + 1) * BLOCK, :] = block
    goal[...] = full[pl.ds(pl.multiple_of(place[3] * chunk, 16), chunk), :]


def call(body, ins, outs, scratch, flops=0, limit=None, name=None):
    moved = sum(x.size * x.dtype.itemsize for x in ins) + sum(
        x.size * x.dtype.itemsize for x in outs
    )
    return pl.pallas_call(
        body,
        out_shape=tuple(outs),
        in_specs=[SMEM if x.dtype == jnp.int32 else VMEM for x in ins],
        out_specs=tuple(VMEM for _ in outs),
        scratch_shapes=scratch,
        compiler_params=pltpu.CompilerParams(vmem_limit_bytes=(limit or 8) * MIB),
        cost_estimate=pl.CostEstimate(flops=flops, bytes_accessed=moved, transcendentals=0),
        name=name,
    )(*ins)


def shape(dims, dtype):
    return jax.ShapeDtypeStruct(dims, dtype)


def local(pool_input, weight_first, weight_second, targets):
    height, breadth, depth = pool_input.shape
    width = weight_first.shape[3]
    groups, tiles = lax.axis_size("grp"), lax.axis_size("tile")
    chips = tiles // 2
    row, tile = lax.axis_index("grp"), lax.axis_index("tile")
    core = tile % 2
    cells = height * breadth
    positions = cells * groups * tiles
    pitch = -(-(breadth + 2 * REACH) // 16) * 16
    step = 2 * pitch
    blocks = width // BLOCK
    place = jnp.stack([core, row * height, tile * breadth, row]).astype(jnp.int32)
    dims = (height, breadth, pitch, (height * groups, breadth * tiles))
    swap = [(i, i ^ 1) for i in range(tiles)]
    cross = [(i, i + 1) for i in range(1, tiles - 1, 2)]
    cross = cross + [(j, i) for i, j in cross]

    rim = shape((height, REACH, depth), BF)
    far, near = call(edges, [place, pool_input], [rim] * 2, [], name="edges")
    far = lax.ppermute(far, "tile", cross)
    near = lax.ppermute(near, "tile", swap)
    band = shape((REACH, breadth + 2 * REACH, depth), BF)
    above, below = call(
        bands,
        [place, pool_input, far, near],
        [band] * 2,
        [pltpu.VMEM((breadth + 2 * REACH, depth), F32)],
        name="bands",
    )
    up = [(i, i + 1) for i in range(groups - 1)]
    down = [(j, i) for i, j in up]
    above = lax.ppermute(above, "grp", up)
    below = lax.ppermute(below, "grp", down)

    rows0, rows1, rows2 = ((height + n) * pitch for n in (8, 6, 0))
    packed = len(pairs(width)) * BLOCK
    w1 = weight_first.reshape(-1, width)
    w2 = weight_second.reshape(-1, width)
    act1, slope1, act2, slope2, keep, mine, sent = call(
        functools.partial(front, dims),
        [place, pool_input, far, near, above, below, w1, w2],
        [
            shape((rows1 + 16, width), F32),
            shape((rows1, width), F32),
            shape((rows2, width), F32),
            shape((rows2, width), F32),
            shape((packed, BLOCK), F32),
            shape((8, BLOCK), F32),
            shape((packed + EXTRA, BLOCK), BF),
        ],
        [
            pltpu.VMEM((rows0 + 16, depth), F32),
            pltpu.VMEM((rows0, 3 * depth), BF),
            pltpu.VMEM((rows1, 3 * width), BF),
            pltpu.VMEM((cells, width), F32),
            pltpu.VMEM((2, packed, BLOCK), F32),
            pltpu.VMEM((2, 2 * EXTRA, BLOCK), F32),
            pltpu.VMEM((rows1, BLOCK), F32),
        ],
        flops=2 * 9 * width * (rows1 * depth + rows2 * width),
        limit=30,
        name="front",
    )
    act2r, slope2r = call(
        functools.partial(ring, dims),
        [act1, w2],
        [shape((2 * step, width), F32)] * 2,
        [pltpu.VMEM((2 * step, 3 * width), BF)],
        flops=2 * 9 * width * width * 2 * step,
        limit=16,
        name="ring",
    )
    chunk = packed // groups
    (goal,) = call(
        aim,
        [place, targets],
        [shape((chunk, BLOCK), F32)],
        [pltpu.VMEM((packed, BLOCK), F32)],
        flops=2 * 10**8,
        name="aim",
    )
    backs = []
    for weight in (weight_second, weight_first):
        taps, inner = 9, weight.shape[2]
        (turned,) = call(
            flip,
            [weight.reshape(taps, inner, width)],
            [shape((taps * width, inner), BF)],
            [],
            flops=2 * 10**9,
            limit=16,
            name="flip",
        )
        backs.append(turned)

    def helpers(members):
        deep = -(-3 * members // 16) * 16
        return [
            pltpu.VMEM((packed, BLOCK), F32),
            pltpu.VMEM((deep, width), F32),
            pltpu.VMEM((deep, width), F32),
            pltpu.VMEM((EXTRA, BLOCK), F32),
        ]

    message = shape((chunk + EXTRA, BLOCK), BF)
    part, centre = shape((chunk, BLOCK), F32), shape((8, BLOCK), F32)
    got = lax.ppermute(sent, "tile", swap)
    share, mean, *sents = call(
        functools.partial(merge_pair, (cells, groups, blocks)),
        [place, keep, mine, got],
        [part, centre] + [message] * (groups - 1),
        helpers(2),
        name="merge_cores",
    )
    gots = [
        lax.ppermute(sents[k - 1], "grp", [(i, i ^ k) for i in range(groups)])
        for k in range(1, groups)
    ]
    share, mean, sent = call(
        functools.partial(merge_many, (2 * cells, groups, blocks), None),
        [place, share, mean] + gots,
        [part, centre, message],
        helpers(groups),
        name="merge_groups",
    )
    gots = [
        lax.ppermute(sent, "tile", [(i, i ^ (2 * k)) for i in range(tiles)])
        for k in range(1, chips)
    ]
    share, mean = call(
        functools.partial(merge_many, (2 * groups * cells, chips, blocks), positions),
        [place, share, mean] + gots + [goal],
        [shape((chunk, BLOCK), BF), shape((EXTRA, BLOCK), BF)],
        helpers(chips),
        name="merge_chips",
    )
    gots = [
        lax.ppermute(share, "grp", [(i, i ^ k) for i in range(groups)])
        for k in range(1, groups)
    ]
    table = shape((packed + EXTRA, BLOCK), BF)
    (mine,) = call(assemble, [place, share, mean] + gots, [table], [], name="assemble")
    other = lax.ppermute(mine, "tile", swap)
    rows_b, rows_d = (height + 4) * pitch, (height + 2) * pitch
    (out,) = call(
        functools.partial(back, dims),
        [place, act1, slope1, act2, slope2, act2r, slope2r, mine, other]
        + backs,
        [shape(pool_input.shape, F32)],
        [
            pltpu.VMEM((rows_b + 16, width), F32),
            pltpu.VMEM((rows_b, 3 * width), BF),
            pltpu.VMEM((rows_d + 16, width), F32),
            pltpu.VMEM((rows_d, 3 * width), BF),
            pltpu.VMEM((width, width), BF),
            pltpu.VMEM((width, width), BF),
            pltpu.VMEM((2, packed + EXTRA, BLOCK), BF),
            pltpu.VMEM((rows1, BLOCK), F32),
        ],
        flops=2 * 9 * width * (rows_d * width + rows2 * depth),
        limit=32,
        name="back",
    )
    return out


def solution(mesh):
    return jax.shard_map(
        local,
        mesh=mesh,
        in_specs=(P("grp", "tile", None), P(), P(), P()),
        out_specs=P("grp", "tile", None),
        check_vma=False,
    )
```

```python
import functools

import jax
import jax.numpy as jnp
from jax import lax
from jax.experimental import pallas as pl
from jax.experimental.pallas import tpu as pltpu
from jax.sharding import PartitionSpec as P


GELU_SCALE = 0.7978845608
GELU_CUBIC = 0.044715
REACH = 4
BLOCK = 128
EXTRA = 16
BF = jnp.bfloat16
F32 = jnp.float32
VMEM = pl.BlockSpec(memory_space=pltpu.VMEM)
SMEM = pl.BlockSpec(memory_space=pltpu.SMEM)
MIB = 2**20


def gelu_pair(values):
    square = values * values
    hyper = jnp.tanh(GELU_SCALE * (values + GELU_CUBIC * values * square))
    half = 0.5 * (1.0 + hyper)
    slope = half + 0.5 * values * (1.0 - hyper * hyper) * (
        GELU_SCALE + 3.0 * GELU_SCALE * GELU_CUBIC * square
    )
    return values * half, slope


def pairs(width):
    blocks = width // BLOCK
    return [(i, j) for i in range(blocks) for j in range(i, blocks)]


def wide(mask, width):
    return jnp.concatenate([mask] * (width // BLOCK), axis=1)


def fill_mask(mask_ref, place_ref, rim, pitch, limits):
    rows = mask_ref.shape[0] // pitch
    col = lax.broadcasted_iota(jnp.int32, (pitch, BLOCK), 0) + (place_ref[2] - rim)
    inside = jnp.where((col >= 0) & (col < limits[1]), 1.0, 0.0).astype(F32)
    for r in range(rows):
        row = place_ref[1] - rim + r
        ok = jnp.where((row >= 0) & (row < limits[0]), 1.0, 0.0).astype(F32)
        mask_ref[r * pitch : (r + 1) * pitch, :] = inside * ok


def shifted(ref, base, step, offset):
    return ref[pl.ds(base, step + 8), :][offset : offset + step]


def spread_taps(flat_ref, base, out_ref, at, step):
    depth = flat_ref.shape[1]
    whole = flat_ref[pl.ds(base, step + 8), :]
    for b in range(3):
        out_ref[pl.ds(at, step), b * depth : (b + 1) * depth] = whole[b : b + step].astype(BF)


def conv(taps_ref, base, weight_ref, pitch, step):
    lhs = jnp.concatenate(
        [taps_ref[pl.ds(base + a * pitch, step), :] for a in range(3)], axis=1
    )
    return jnp.dot(lhs, weight_ref[...], preferred_element_type=F32)


def tiles_of(start, stop, step, body):
    def one(t, carry):
        body(pl.multiple_of(start + t * step, 16))
        return carry

    lax.fori_loop(0, (stop - start) // step, one, 0)


def put_mean(rows_ref, mean, parts):
    blocks = mean.shape[1] // BLOCK
    high = mean.astype(BF).astype(F32)
    for p, row in enumerate((high, mean - high) if parts == 2 else (mean,)):
        for j in range(blocks):
            at = p * blocks + j
            rows_ref[at : at + 1, :] = row[:, j * BLOCK : (j + 1) * BLOCK]


def get_mean(rows, blocks, parts):
    rows = rows.astype(F32)
    found = rows[:blocks] + rows[blocks : 2 * blocks] if parts == 2 else rows[:blocks]
    return jnp.concatenate([found[j : j + 1] for j in range(blocks)], axis=1)


def spread(means, count, left_ref, right_ref, emit):
    centre = means[0]
    for mean in means[1:]:
        centre = centre + mean
    centre = centre * (1.0 / len(means))
    left_ref[...] = jnp.zeros(left_ref.shape, F32)
    right_ref[...] = jnp.zeros(right_ref.shape, F32)
    for n, mean in enumerate(means):
        away = mean - centre
        high = away.astype(BF).astype(F32)
        low = away - high
        for q, (lhs, rhs) in enumerate(((high, high), (high, low), (low, high))):
            at = 3 * n + q
            left_ref[at : at + 1, :] = lhs
            right_ref[at : at + 1, :] = rhs
    lhs, rhs = left_ref[...].astype(BF), right_ref[...].astype(BF)
    for n, (i, j) in enumerate(pairs(lhs.shape[1])):
        product = lax.dot_general(
            lhs[:, i * BLOCK : (i + 1) * BLOCK],
            rhs[:, j * BLOCK : (j + 1) * BLOCK],
            (((0,), (0,)), ((), ())),
            preferred_element_type=F32,
        )
        emit(n, product * float(count))
    return centre


def front(dims, place, pool, far, near, above, below, w1, w2, *rest):
    (act1, slope1, act2, slope2, keep, mine, sent) = rest[:7]
    (flat, taps1, taps2, own, gram, stat, mask) = rest[7:]
    height, breadth, pitch, limits = dims
    step = 2 * pitch
    width = w1.shape[1]
    blocks = width // BLOCK
    flat[...] = jnp.zeros(flat.shape, F32)
    left_core = place[0] == 0
    for r in range(height):
        at = (r + REACH) * pitch
        one, two = far[r].astype(F32), near[r].astype(F32)
        flat[at : at + REACH, :] = jnp.where(left_core, one, two)
        flat[at + REACH : at + REACH + breadth, :] = pool[r]
        flat[at + REACH + breadth : at + 2 * REACH + breadth, :] = jnp.where(left_core, two, one)
    for r in range(REACH):
        at = r * pitch
        flat[at : at + breadth + 2 * REACH, :] = above[r].astype(F32)
        at = (r + REACH + height) * pitch
        flat[at : at + breadth + 2 * REACH, :] = below[r].astype(F32)
    fill_mask(mask, place, 3, pitch, limits)
    tiles_of(
        0, (height + 8) * pitch, step, lambda at: spread_taps(flat, at, taps1, at, step)
    )

    def first(at):
        act, slope = gelu_pair(conv(taps1, at, w1, pitch, step))
        act1[pl.ds(at, step), :] = act * wide(mask[pl.ds(at, step), :], width)
        slope1[pl.ds(at, step), :] = slope

    rows1 = (height + 6) * pitch
    act1[rows1:, :] = jnp.zeros((act1.shape[0] - rows1, width), F32)
    tiles_of(0, rows1, step, first)
    tiles_of(step, rows1 - step, step, lambda at: spread_taps(act1, at, taps2, at, step))

    def second(at):
        act, slope = gelu_pair(conv(taps2, at, w2, pitch, step))
        act2[pl.ds(at - step, step), :] = act
        slope2[pl.ds(at - step, step), :] = slope

    tiles_of(step, step + height * pitch, step, second)
    cells = height * breadth
    for layer, (act, offset) in enumerate(((act1, 3 * pitch + 3), (act2, 2))):
        total = jnp.zeros((8, width), F32)
        for r in range(height):
            cut = act[offset + r * pitch : offset + r * pitch + breadth, :]
            own[r * breadth : (r + 1) * breadth, :] = cut
            total = total + jnp.sum(cut.reshape(breadth // 8, 8, width), axis=0)
        mean = jnp.sum(total, axis=0, keepdims=True) * (1.0 / cells)
        centred = (own[...] - mean).astype(BF)
        n = 0
        for i in range(blocks):
            panel = lax.dot_general(
                centred[:, i * BLOCK : (i + 1) * BLOCK],
                centred[:, i * BLOCK :],
                (((0,), (0,)), ((), ())),
                preferred_element_type=F32,
            )
            for j in range(i, blocks):
                gram[layer, n * BLOCK : (n + 1) * BLOCK, :] = panel[
                    :, (j - i) * BLOCK : (j - i + 1) * BLOCK
                ]
                n += 1
        stat[layer] = jnp.zeros(stat.shape[1:], F32)
        put_mean(stat.at[layer, 0:EXTRA], mean, 2)
        put_mean(stat.at[layer, EXTRA : 2 * EXTRA], mean, 1)
    rows = keep.shape[0]
    keep[...] = gram[place[0]]
    mine[...] = stat[place[0], EXTRA : EXTRA + 8, :]
    sent[0:rows, :] = gram[1 - place[0]].astype(BF)
    sent[rows:, :] = stat[1 - place[0], 0:EXTRA, :].astype(BF)


def ring(dims, act1, w2, act2, slope2, taps2):
    height, _, pitch, _ = dims
    step = 2 * pitch
    for n, start in enumerate((0, (height + 2) * pitch)):
        for q in range(2):
            spread_taps(act1, start + q * step, taps2, q * step, step)
        act, slope = gelu_pair(conv(taps2, 0, w2, pitch, step))
        act2[n * step : (n + 1) * step, :] = act
        slope2[n * step : (n + 1) * step, :] = slope


def write_message(ref, part, rows_ref, centre):
    count = part.shape[0]
    rows_ref[...] = jnp.zeros(rows_ref.shape, F32)
    put_mean(rows_ref, centre, 2)
    ref[0:count, :] = part.astype(BF)
    ref[count:, :] = rows_ref[...].astype(BF)


def merge_pair(dims, place, keep, mine, got, share, centre_out, *rest):
    count, groups, blocks = dims
    messages, (full, left, right, rows_ref) = rest[: groups - 1], rest[groups - 1 :]
    rows = keep.shape[0]
    chunk = rows // groups

    def emit(n, product):
        at = slice(n * BLOCK, (n + 1) * BLOCK)
        full[at, :] = keep[at, :] + got[at, :].astype(F32) + product

    means = [get_mean(mine[...], blocks, 1), get_mean(got[rows:, :], blocks, 2)]
    centre = spread(means, count, left, right, emit)
    centre_out[...] = jnp.zeros(centre_out.shape, F32)
    put_mean(centre_out, centre, 1)
    for k, ref in enumerate(messages, 1):
        at = pl.multiple_of((place[3] ^ k) * chunk, 16)
        write_message(ref, full[pl.ds(at, chunk), :], rows_ref, centre)
    share[...] = full[pl.ds(pl.multiple_of(place[3] * chunk, 16), chunk), :]


def merge_many(dims, final, place, share, mine, *rest):
    count, members, blocks = dims
    gots, rest = rest[: members - 1], rest[members - 1 :]
    chunk = share.shape[0]
    full, left, right, rows_ref = rest[-4:]

    def emit(n, product):
        full[n * BLOCK : (n + 1) * BLOCK, :] = product

    means = [get_mean(mine[...], blocks, 1)]
    means += [get_mean(got[chunk:, :], blocks, 2) for got in gots]
    centre = spread(means, count, left, right, emit)
    total = share[...] + full[pl.ds(pl.multiple_of(place[3] * chunk, 16), chunk), :]
    for got in gots:
        total = total + got[0:chunk, :].astype(F32)
    if final is None:
        out, centre_out, sent = rest[:3]
        out[...] = total
        centre_out[...] = jnp.zeros(centre_out.shape, F32)
        put_mean(centre_out, centre, 1)
        write_message(sent, total, rows_ref, centre)
    else:
        goal, sent, centre_out = rest[:3]
        rows_ref[...] = jnp.zeros(rows_ref.shape, F32)
        put_mean(rows_ref, centre, 2)
        centre_out[...] = rows_ref[...].astype(BF)
        sent[...] = (total * (1.0 / final) - goal[...]).astype(BF)


def assemble(place, share, centre, *rest):
    gots, out = rest[:-1], rest[-1]
    chunk = share.shape[0]
    for k, ref in enumerate((share,) + tuple(gots)):
        out[pl.ds(pl.multiple_of((place[3] ^ k) * chunk, 16), chunk), :] = ref[...]
    rows = chunk * (len(gots) + 1)
    out[rows:, :] = centre[...]


def back(dims, place, act1, slope1, act2, slope2, act2r, slope2r, mine, other, w2, w1, out, *scratch):
    (flat2, taps2, flat1, taps1, first_m, second_m, table, mask) = scratch
    height, breadth, pitch, limits = dims
    step = 2 * pitch
    width = act1.shape[1]
    blocks = width // BLOCK
    packed = table.shape[1] - EXTRA
    table[place[0]] = mine[...]
    table[1 - place[0]] = other[...]
    means = []
    for layer, ref in enumerate((first_m, second_m)):
        for n, (i, j) in enumerate(pairs(width)):
            block = table[layer, n * BLOCK : (n + 1) * BLOCK, :]
            ref[i * BLOCK : (i + 1) * BLOCK, j * BLOCK : (j + 1) * BLOCK] = block
            if i != j:
                ref[j * BLOCK : (j + 1) * BLOCK, i * BLOCK : (i + 1) * BLOCK] = (
                    block.astype(F32).T.astype(BF)
                )
        means.append(get_mean(table[layer, packed:, :], blocks, 2))
    fill_mask(mask, place, 3, pitch, limits)

    def second(act, slope, at, to):
        centred = (act[pl.ds(at, step), :] - means[1]).astype(BF)
        push = jnp.dot(centred, second_m[...], preferred_element_type=F32)
        allow = wide(shifted(mask, to + pitch, step, 1), width)
        flat2[pl.ds(to, step), :] = push * slope[pl.ds(at, step), :] * allow

    rows2 = (height + 4) * pitch
    flat2[rows2:, :] = jnp.zeros((flat2.shape[0] - rows2, width), F32)
    second(act2r, slope2r, 0, 0)
    second(act2r, slope2r, step, rows2 - step)
    tiles_of(
        0, height * pitch, step, lambda at: second(act2, slope2, at, pl.multiple_of(at + step, 16))
    )
    tiles_of(0, rows2, step, lambda at: spread_taps(flat2, at, taps2, at, step))
    rows1 = (height + 2) * pitch
    flat1[rows1:, :] = jnp.zeros((flat1.shape[0] - rows1, width), F32)

    def first(at):
        near = pl.multiple_of(at + 2 * pitch, 16)
        centred = (shifted(act1, near, step, 2) - means[0]).astype(BF)
        flow = conv(taps2, at, w2, pitch, step) + jnp.dot(
            centred, first_m[...], preferred_element_type=F32
        )
        allow = wide(shifted(mask, near, step, 2), width)
        flat1[pl.ds(at, step), :] = flow * shifted(slope1, near, step, 2) * allow

    tiles_of(0, rows1, step, first)
    tiles_of(0, rows1, step, lambda at: spread_taps(flat1, at, taps1, at, step))

    def last(t, carry):
        got = conv(taps1, pl.multiple_of(t * step, 16), w1, pitch, step)
        out[2 * t] = got[0:breadth]
        out[2 * t + 1] = got[pitch : pitch + breadth]
        return carry

    lax.fori_loop(0, height // 2, last, 0)


def edges(place, pool, far, near):
    breadth = pool.shape[1]
    left_core = place[0] == 0
    left = pool[:, 0:REACH, :]
    right = pool[:, breadth - REACH : breadth, :]
    far[...] = jnp.where(left_core, left, right).astype(BF)
    near[...] = jnp.where(left_core, right, left).astype(BF)


def bands(place, pool, far, near, above, below, row):
    height, breadth, _ = pool.shape
    left_core = place[0] == 0
    for start, ref in ((height - REACH, above), (0, below)):
        for r in range(REACH):
            one, two = far[start + r].astype(F32), near[start + r].astype(F32)
            row[0:REACH, :] = jnp.where(left_core, one, two)
            row[REACH : REACH + breadth, :] = pool[start + r]
            row[REACH + breadth :, :] = jnp.where(left_core, two, one)
            ref[r] = row[...].astype(BF)


def flip(weight, out):
    taps, _, width = weight.shape

    def one(t, carry):
        at = pl.multiple_of(t * width, 16)
        out[pl.ds(at, width), :] = weight[taps - 1 - t].T
        return carry

    lax.fori_loop(0, taps, one, 0)


def aim(place, targets, goal, full):
    core = place[0]
    chunk = goal.shape[0]
    for n, (i, j) in enumerate(pairs(targets.shape[1])):
        rows, cols = slice(i * BLOCK, (i + 1) * BLOCK), slice(j * BLOCK, (j + 1) * BLOCK)
        block = (targets[core, rows, cols] + targets[core, cols, rows].T) * 0.5
        full[n * BLOCK : (n + 1) * BLOCK, :] = block
    goal[...] = full[pl.ds(pl.multiple_of(place[3] * chunk, 16), chunk), :]


def call(body, ins, outs, scratch, flops=0, limit=None):
    moved = sum(x.size * x.dtype.itemsize for x in ins) + sum(
        x.size * x.dtype.itemsize for x in outs
    )
    return pl.pallas_call(
        body,
        out_shape=tuple(outs),
        in_specs=[SMEM if x.dtype == jnp.int32 else VMEM for x in ins],
        out_specs=tuple(VMEM for _ in outs),
        scratch_shapes=scratch,
        compiler_params=pltpu.CompilerParams(vmem_limit_bytes=(limit or 8) * MIB),
        cost_estimate=pl.CostEstimate(flops=flops, bytes_accessed=moved, transcendentals=0),
    )(*ins)


def shape(dims, dtype):
    return jax.ShapeDtypeStruct(dims, dtype)


def local(pool_input, weight_first, weight_second, targets):
    height, breadth, depth = pool_input.shape
    width = weight_first.shape[3]
    groups, tiles = lax.axis_size("grp"), lax.axis_size("tile")
    chips = tiles // 2
    row, tile = lax.axis_index("grp"), lax.axis_index("tile")
    core = tile % 2
    cells = height * breadth
    positions = cells * groups * tiles
    pitch = -(-(breadth + 2 * REACH) // 16) * 16
    step = 2 * pitch
    blocks = width // BLOCK
    place = jnp.stack([core, row * height, tile * breadth, row]).astype(jnp.int32)
    dims = (height, breadth, pitch, (height * groups, breadth * tiles))
    swap = [(i, i ^ 1) for i in range(tiles)]
    cross = [(i, i + 1) for i in range(1, tiles - 1, 2)]
    cross = cross + [(j, i) for i, j in cross]

    rim = shape((height, REACH, depth), BF)
    far, near = call(edges, [place, pool_input], [rim] * 2, [])
    far = lax.ppermute(far, "tile", cross)
    near = lax.ppermute(near, "tile", swap)
    band = shape((REACH, breadth + 2 * REACH, depth), BF)
    above, below = call(
        bands,
        [place, pool_input, far, near],
        [band] * 2,
        [pltpu.VMEM((breadth + 2 * REACH, depth), F32)],
    )
    up = [(i, i + 1) for i in range(groups - 1)]
    down = [(j, i) for i, j in up]
    above = lax.ppermute(above, "grp", up)
    below = lax.ppermute(below, "grp", down)

    rows0, rows1, rows2 = ((height + n) * pitch for n in (8, 6, 0))
    packed = len(pairs(width)) * BLOCK
    w1 = weight_first.reshape(-1, width)
    w2 = weight_second.reshape(-1, width)
    act1, slope1, act2, slope2, keep, mine, sent = call(
        functools.partial(front, dims),
        [place, pool_input, far, near, above, below, w1, w2],
        [
            shape((rows1 + 16, width), F32),
            shape((rows1, width), F32),
            shape((rows2, width), F32),
            shape((rows2, width), F32),
            shape((packed, BLOCK), F32),
            shape((8, BLOCK), F32),
            shape((packed + EXTRA, BLOCK), BF),
        ],
        [
            pltpu.VMEM((rows0 + 16, depth), F32),
            pltpu.VMEM((rows0, 3 * depth), BF),
            pltpu.VMEM((rows1, 3 * width), BF),
            pltpu.VMEM((cells, width), F32),
            pltpu.VMEM((2, packed, BLOCK), F32),
            pltpu.VMEM((2, 2 * EXTRA, BLOCK), F32),
            pltpu.VMEM((rows1, BLOCK), F32),
        ],
        flops=2 * 9 * width * (rows1 * depth + rows2 * width),
        limit=30,
    )
    act2r, slope2r = call(
        functools.partial(ring, dims),
        [act1, w2],
        [shape((2 * step, width), F32)] * 2,
        [pltpu.VMEM((2 * step, 3 * width), BF)],
        flops=2 * 9 * width * width * 2 * step,
        limit=16,
    )
    chunk = packed // groups
    (goal,) = call(
        aim,
        [place, targets],
        [shape((chunk, BLOCK), F32)],
        [pltpu.VMEM((packed, BLOCK), F32)],
        flops=2 * 10**8,
    )
    backs = []
    for weight in (weight_second, weight_first):
        taps, inner = 9, weight.shape[2]
        (turned,) = call(
            flip,
            [weight.reshape(taps, inner, width)],
            [shape((taps * width, inner), BF)],
            [],
            flops=2 * 10**9,
            limit=16,
        )
        backs.append(turned)

    def helpers(members):
        deep = -(-3 * members // 16) * 16
        return [
            pltpu.VMEM((packed, BLOCK), F32),
            pltpu.VMEM((deep, width), F32),
            pltpu.VMEM((deep, width), F32),
            pltpu.VMEM((EXTRA, BLOCK), F32),
        ]

    message = shape((chunk + EXTRA, BLOCK), BF)
    part, centre = shape((chunk, BLOCK), F32), shape((8, BLOCK), F32)
    got = lax.ppermute(sent, "tile", swap)
    share, mean, *sents = call(
        functools.partial(merge_pair, (cells, groups, blocks)),
        [place, keep, mine, got],
        [part, centre] + [message] * (groups - 1),
        helpers(2),
    )
    gots = [
        lax.ppermute(sents[k - 1], "grp", [(i, i ^ k) for i in range(groups)])
        for k in range(1, groups)
    ]
    share, mean, sent = call(
        functools.partial(merge_many, (2 * cells, groups, blocks), None),
        [place, share, mean] + gots,
        [part, centre, message],
        helpers(groups),
    )
    gots = [
        lax.ppermute(sent, "tile", [(i, i ^ (2 * k)) for i in range(tiles)])
        for k in range(1, chips)
    ]
    share, mean = call(
        functools.partial(merge_many, (2 * groups * cells, chips, blocks), positions),
        [place, share, mean] + gots + [goal],
        [shape((chunk, BLOCK), BF), shape((EXTRA, BLOCK), BF)],
        helpers(chips),
    )
    gots = [
        lax.ppermute(share, "grp", [(i, i ^ k) for i in range(groups)])
        for k in range(1, groups)
    ]
    table = shape((packed + EXTRA, BLOCK), BF)
    (mine,) = call(assemble, [place, share, mean] + gots, [table], [])
    other = lax.ppermute(mine, "tile", swap)
    rows_b, rows_d = (height + 4) * pitch, (height + 2) * pitch
    (out,) = call(
        functools.partial(back, dims),
        [place, act1, slope1, act2, slope2, act2r, slope2r, mine, other]
        + backs,
        [shape(pool_input.shape, F32)],
        [
            pltpu.VMEM((rows_b + 16, width), F32),
            pltpu.VMEM((rows_b, 3 * width), BF),
            pltpu.VMEM((rows_d + 16, width), F32),
            pltpu.VMEM((rows_d, 3 * width), BF),
            pltpu.VMEM((width, width), BF),
            pltpu.VMEM((width, width), BF),
            pltpu.VMEM((2, packed + EXTRA, BLOCK), BF),
            pltpu.VMEM((rows1, BLOCK), F32),
        ],
        flops=2 * 9 * width * (rows_d * width + rows2 * depth),
        limit=32,
    )
    return out


def solution(mesh):
    return jax.shard_map(
        local,
        mesh=mesh,
        in_specs=(P("grp", "tile", None), P(), P(), P()),
        out_specs=P("grp", "tile", None),
        check_vma=False,
    )
```

```python
import functools

import jax
import jax.numpy as jnp
from jax import lax
from jax.experimental import pallas as pl
from jax.experimental.pallas import tpu as pltpu
from jax.sharding import PartitionSpec as P


GELU_SCALE = 0.7978845608
GELU_CUBIC = 0.044715
REACH = 4
BLOCK = 128
EXTRA = 16
BF = jnp.bfloat16
F32 = jnp.float32
VMEM = pl.BlockSpec(memory_space=pltpu.VMEM)
SMEM = pl.BlockSpec(memory_space=pltpu.SMEM)
MIB = 2**20


def gelu_pair(values):
    square = values * values
    hyper = jnp.tanh(GELU_SCALE * (values + GELU_CUBIC * values * square))
    half = 0.5 * (1.0 + hyper)
    slope = half + 0.5 * values * (1.0 - hyper * hyper) * (
        GELU_SCALE + 3.0 * GELU_SCALE * GELU_CUBIC * square
    )
    return values * half, slope


def pairs(width):
    blocks = width // BLOCK
    return [(i, j) for i in range(blocks) for j in range(i, blocks)]


def wide(mask, width):
    return jnp.concatenate([mask] * (width // BLOCK), axis=1)


def columns(groups):
    n = lax.broadcasted_iota(jnp.int32, (groups * 16, BLOCK), 0)
    return (n & 15) * groups + (n >> 4)


def span(groups, low, high):
    col = columns(groups)
    return jnp.where((col >= low) & (col < high), 1.0, 0.0).astype(F32)


def pair_mask(inside, place, limits, row):
    parts = []
    for r in range(2):
        at = place[1] + row + r
        parts.append(inside * jnp.where((at >= 0) & (at < limits[0]), 1.0, 0.0).astype(F32))
    return jnp.concatenate(parts, axis=0)


def roll_group(value):
    return [pltpu.roll(value[n * 16 : (n + 1) * 16], 15, 0) for n in range(2)]


def write_taps(ref, row, value, groups, lanes=slice(None)):
    at, pitch = row * (groups + 2) * 16, groups * 16
    ref[at : at + pitch, lanes] = value.astype(BF)
    for n, block in enumerate(roll_group(value)):
        ref[at + pitch + n * 16 : at + pitch + (n + 1) * 16, lanes] = block.astype(BF)


def fold_row(ref, row, buf_ref, at, groups):
    base = row * (groups + 2) * 16
    for n in range(groups + 2):
        for p in range(buf_ref.shape[0]):
            ref[base + n * 16 : base + (n + 1) * 16, p * BLOCK : (p + 1) * BLOCK] = buf_ref[
                p, pl.ds(at + n, 16, stride=groups), :
            ].astype(BF)


def put_row(buf_ref, at, value):
    for p in range(buf_ref.shape[0]):
        buf_ref[p, at : at + value.shape[0], :] = value[:, p * BLOCK : (p + 1) * BLOCK]


def clear_rows(buf_ref, start, stop):
    for p in range(buf_ref.shape[0]):
        buf_ref[p, start:stop, :] = jnp.zeros((stop - start, BLOCK), F32)


def conv(find, weight_ref, groups, lanes):
    pitch, pieces = groups * 16, []
    for a in range(3):
        for b in range(3):
            both = []
            for r in range(2):
                ref, row = find(r + a)
                at = (row * (groups + 2) + b) * 16
                both.append(ref[at : at + pitch, :])
            pieces.append(jnp.concatenate(both, axis=0))
    lhs = jnp.concatenate(pieces, axis=1)
    return jnp.dot(lhs, weight_ref[:, lanes], preferred_element_type=F32)


def halves(width):
    half = 2 * BLOCK
    return [slice(n, n + half) for n in range(0, width, half)]


def first_rows(find, w1, taps_ref, row, act, slope, at, groups, mask):
    width, pitch = w1.shape[1], groups * 16
    for lanes in halves(width):
        value, tilt = gelu_pair(conv(find, w1, groups, lanes))
        value = value * wide(mask, 2 * BLOCK)
        for r in range(2):
            one = value[r * pitch : (r + 1) * pitch]
            write_taps(taps_ref, row + r, one, groups, lanes)
            if act is None:
                continue
            two = tilt[r * pitch : (r + 1) * pitch]
            base = at + r * pitch
            for ref, part in ((act, one), (slope, two)):
                ref[base : base + pitch - 32, lanes] = part[32:]
                for n, block in enumerate(roll_group(part)):
                    to = base + pitch - 32 + n * 16
                    ref[to : to + 16, lanes] = block


def second_rows(find, w2, act, slope, at, groups):
    step = groups * 32
    for lanes in halves(w2.shape[1]):
        value, tilt = gelu_pair(conv(find, w2, groups, lanes))
        act[at : at + step, lanes] = value
        slope[at : at + step, lanes] = tilt


def put_mean(rows_ref, mean, parts):
    blocks = mean.shape[1] // BLOCK
    high = mean.astype(BF).astype(F32)
    for p, row in enumerate((high, mean - high) if parts == 2 else (mean,)):
        for j in range(blocks):
            at = p * blocks + j
            rows_ref[at : at + 1, :] = row[:, j * BLOCK : (j + 1) * BLOCK]


def get_mean(rows, blocks, parts):
    rows = rows.astype(F32)
    found = rows[:blocks] + rows[blocks : 2 * blocks] if parts == 2 else rows[:blocks]
    return jnp.concatenate([found[j : j + 1] for j in range(blocks)], axis=1)


def spread(means, count, left_ref, right_ref, emit):
    centre = means[0]
    for mean in means[1:]:
        centre = centre + mean
    centre = centre * (1.0 / len(means))
    left_ref[...] = jnp.zeros(left_ref.shape, F32)
    right_ref[...] = jnp.zeros(right_ref.shape, F32)
    for n, mean in enumerate(means):
        away = mean - centre
        high = away.astype(BF).astype(F32)
        low = away - high
        for q, (lhs, rhs) in enumerate(((high, high), (high, low), (low, high))):
            at = 3 * n + q
            left_ref[at : at + 1, :] = lhs
            right_ref[at : at + 1, :] = rhs
    lhs, rhs = left_ref[...].astype(BF), right_ref[...].astype(BF)
    for n, (i, j) in enumerate(pairs(lhs.shape[1])):
        product = lax.dot_general(
            lhs[:, i * BLOCK : (i + 1) * BLOCK],
            rhs[:, j * BLOCK : (j + 1) * BLOCK],
            (((0,), (0,)), ((), ())),
            preferred_element_type=F32,
        )
        emit(n, product * float(count))
    return centre


def middle(dims, place, pool, far, near, w1, w2, taps1, taps2, act1, slope1, act2, slope2, buf):
    height, breadth, groups, limits = dims
    pitch = groups * 16
    left_core = place[0] == 0
    space = buf.shape[1] // height
    for r in range(height):
        at = r * space
        one, two = far[r].astype(F32), near[r].astype(F32)
        put_row(buf, at, jnp.where(left_core, one, two))
        put_row(buf, at + REACH, pool[r])
        put_row(buf, at + REACH + breadth, jnp.where(left_core, two, one))
        clear_rows(buf, at + 2 * REACH + breadth, at + space)
        fold_row(taps1, r, buf, at, groups)
    low = 3 - place[2]
    inside = span(groups, low, low + limits[1])
    for t in range(0, height - 2, 2):
        mask = pair_mask(inside, place, limits, t + 1)
        first_rows(
            lambda r: (taps1, t + r), w1, taps2, t, act1, slope1, t * pitch, groups, mask
        )
    for t in range(0, height - 4, 2):
        second_rows(lambda r: (taps2, t + r), w2, act2, slope2, t * pitch, groups)


def rim_taps(ref, rows, buf, groups):
    space = buf.shape[1] // len(rows)
    for n, (source, r) in enumerate(rows):
        breadth = source.shape[1]
        at = n * space
        put_row(buf, at, source[r].astype(F32))
        clear_rows(buf, at + breadth, at + space)
        fold_row(ref, n, buf, at, groups)


def front(dims, place, above, below, taps1, taps2, act1, act2, w1, w2, *rest):
    (taps2b, act1b, slope1b, act2b, slope2b, keep, mine, sent) = rest[:8]
    (rim, buf, gram, stat) = rest[8:]
    height, breadth, groups, limits = dims
    pitch = groups * 16
    width = w1.shape[1]
    blocks = width // BLOCK
    rim_taps(rim, [(above, 2), (above, 3), (below, 0), (below, 1)], buf, groups)
    low = 3 - place[2]
    inside = span(groups, low, low + limits[1])
    last = height - 2
    finds = (
        lambda r: (rim, r) if r < 2 else (taps1, r - 2),
        lambda r: (taps1, last + r) if r < 2 else (rim, r),
    )
    for n, row in enumerate((-1, height - 1)):
        mask = pair_mask(inside, place, limits, row)
        first_rows(
            finds[n], w1, taps2b, 2 * n, act1b, slope1b, 2 * n * pitch, groups, mask
        )
    last = height - 4
    finds = (
        lambda r: (taps2b, r) if r < 2 else (taps2, r - 2),
        lambda r: (taps2, last + r) if r < 2 else (taps2b, r),
    )
    for n in range(2):
        second_rows(finds[n], w2, act2b, slope2b, 2 * n * pitch, groups)
    cells = height * breadth
    first_parts = [(act1b, pitch, 2 * pitch), (act1, 0, (height - 2) * pitch)]
    second_parts = [(act2b, 0, 4 * pitch), (act2, 0, (height - 4) * pitch)]
    for layer, (parts, offset) in enumerate(((first_parts, 1), (second_parts, 2))):
        own = wide(span(groups, offset, offset + breadth), width)
        total = jnp.zeros((pitch, width), F32)
        for ref, start, count in parts:
            for at in range(start, start + count, pitch):
                total = total + ref[at : at + pitch, :]
        mean = jnp.sum(total * own, axis=0, keepdims=True) * (1.0 / cells)
        centred = jnp.concatenate(
            [
                ((ref[at : at + pitch, :] - mean) * own).astype(BF)
                for ref, start, count in parts
                for at in range(start, start + count, pitch)
            ],
            axis=0,
        )
        n = 0
        for i in range(blocks):
            panel = lax.dot_general(
                centred[:, i * BLOCK : (i + 1) * BLOCK],
                centred[:, i * BLOCK :],
                (((0,), (0,)), ((), ())),
                preferred_element_type=F32,
            )
            for j in range(i, blocks):
                gram[layer, n * BLOCK : (n + 1) * BLOCK, :] = panel[
                    :, (j - i) * BLOCK : (j - i + 1) * BLOCK
                ]
                n += 1
        stat[layer] = jnp.zeros(stat.shape[1:], F32)
        put_mean(stat.at[layer, 0:EXTRA], mean, 2)
        put_mean(stat.at[layer, EXTRA : 2 * EXTRA], mean, 1)
    rows = keep.shape[0]
    keep[...] = gram[place[0]]
    mine[...] = stat[place[0], EXTRA : EXTRA + 8, :]
    sent[0:rows, :] = gram[1 - place[0]].astype(BF)
    sent[rows:, :] = stat[1 - place[0], 0:EXTRA, :].astype(BF)


def ring(dims, place, above, below, taps2b, w1, w2, act2, slope2, rim, outer, buf):
    height, _, groups, limits = dims
    low = 3 - place[2]
    inside = span(groups, low, low + limits[1])
    finds = (
        lambda r: (outer, r) if r < 2 else (taps2b, r - 2),
        lambda r: (taps2b, 2 + r) if r < 2 else (outer, r),
    )
    for n, (source, row) in enumerate(((above, -3), (below, height + 1))):
        rim_taps(rim, [(source, r) for r in range(REACH)], buf, groups)
        mask = pair_mask(inside, place, limits, row)
        first_rows(lambda r: (rim, r), w1, outer, 2 * n, None, None, 0, groups, mask)
        second_rows(finds[n], w2, act2, slope2, 2 * n * groups * 16, groups)


def write_message(ref, part, rows_ref, centre):
    count = part.shape[0]
    rows_ref[...] = jnp.zeros(rows_ref.shape, F32)
    put_mean(rows_ref, centre, 2)
    ref[0:count, :] = part.astype(BF)
    ref[count:, :] = rows_ref[...].astype(BF)


def merge_pair(dims, place, keep, mine, got, share, centre_out, *rest):
    count, groups, blocks = dims
    messages, (full, left, right, rows_ref) = rest[: groups - 1], rest[groups - 1 :]
    rows = keep.shape[0]
    chunk = rows // groups

    def emit(n, product):
        at = slice(n * BLOCK, (n + 1) * BLOCK)
        full[at, :] = keep[at, :] + got[at, :].astype(F32) + product

    means = [get_mean(mine[...], blocks, 1), get_mean(got[rows:, :], blocks, 2)]
    centre = spread(means, count, left, right, emit)
    centre_out[...] = jnp.zeros(centre_out.shape, F32)
    put_mean(centre_out, centre, 1)
    for k, ref in enumerate(messages, 1):
        at = pl.multiple_of((place[3] ^ k) * chunk, 16)
        write_message(ref, full[pl.ds(at, chunk), :], rows_ref, centre)
    share[...] = full[pl.ds(pl.multiple_of(place[3] * chunk, 16), chunk), :]


def merge_many(dims, final, place, share, mine, *rest):
    count, members, blocks = dims
    gots, rest = rest[: members - 1], rest[members - 1 :]
    chunk = share.shape[0]
    full, left, right, rows_ref = rest[-4:]

    def emit(n, product):
        full[n * BLOCK : (n + 1) * BLOCK, :] = product

    means = [get_mean(mine[...], blocks, 1)]
    means += [get_mean(got[chunk:, :], blocks, 2) for got in gots]
    centre = spread(means, count, left, right, emit)
    total = share[...] + full[pl.ds(pl.multiple_of(place[3] * chunk, 16), chunk), :]
    for got in gots:
        total = total + got[0:chunk, :].astype(F32)
    if final is None:
        out, centre_out, sent = rest[:3]
        out[...] = total
        centre_out[...] = jnp.zeros(centre_out.shape, F32)
        put_mean(centre_out, centre, 1)
        write_message(sent, total, rows_ref, centre)
    else:
        goal, sent, centre_out = rest[:3]
        rows_ref[...] = jnp.zeros(rows_ref.shape, F32)
        put_mean(rows_ref, centre, 2)
        centre_out[...] = rows_ref[...].astype(BF)
        sent[...] = (total * (1.0 / final) - goal[...]).astype(BF)


def assemble(place, share, centre, *rest):
    gots, out = rest[:-1], rest[-1]
    chunk = share.shape[0]
    for k, ref in enumerate((share,) + tuple(gots)):
        out[pl.ds(pl.multiple_of((place[3] ^ k) * chunk, 16), chunk), :] = ref[...]
    rows = chunk * (len(gots) + 1)
    out[rows:, :] = centre[...]


def back(dims, place, *rest):
    (act1, slope1, act1b, slope1b, act2, slope2, act2b, slope2b, act2r, slope2r) = rest[:10]
    (mine, other, w2, w1, out, taps2, taps1, first_m, second_m, table, buf) = rest[10:]
    height, breadth, groups, limits = dims
    pitch = groups * 16
    step = 2 * pitch
    width = act1.shape[1]
    blocks = width // BLOCK
    packed = table.shape[1] - EXTRA
    table[place[0]] = mine[...]
    table[1 - place[0]] = other[...]
    means = []
    for layer, ref in enumerate((first_m, second_m)):
        for n, (i, j) in enumerate(pairs(width)):
            block = table[layer, n * BLOCK : (n + 1) * BLOCK, :]
            ref[i * BLOCK : (i + 1) * BLOCK, j * BLOCK : (j + 1) * BLOCK] = block
            if i != j:
                ref[j * BLOCK : (j + 1) * BLOCK, i * BLOCK : (i + 1) * BLOCK] = block.T
        means.append(get_mean(table[layer, packed:, :], blocks, 2))
    low = 2 - place[2]
    inside = span(groups, low, low + limits[1])
    tiles = [(act2r, slope2r, 0), (act2b, slope2b, 0)]
    tiles += [(act2, slope2, t * pitch) for t in range(0, height - 4, 2)]
    tiles += [(act2b, slope2b, step), (act2r, slope2r, step)]
    for t, (act, slope, at) in enumerate(tiles):
        centred = (act[at : at + step, :] - means[1]).astype(BF)
        mask = wide(pair_mask(inside, place, limits, 2 * t - 2), 2 * BLOCK)
        for lanes in halves(width):
            push = jnp.dot(centred, second_m[:, lanes], preferred_element_type=F32)
            grad = push * slope[at : at + step, lanes] * mask
            for r in range(2):
                write_taps(taps2, 2 * t + r, grad[r * pitch : (r + 1) * pitch], groups, lanes)
    low = 1 - place[2]
    inside = span(groups, low, low + limits[1])
    tiles = [(act1b, slope1b, 0)]
    tiles += [(act1, slope1, t * pitch) for t in range(0, height - 2, 2)]
    tiles += [(act1b, slope1b, step)]
    for t, (act, slope, at) in enumerate(tiles):
        centred = (act[at : at + step, :] - means[0]).astype(BF)
        mask = wide(pair_mask(inside, place, limits, 2 * t - 1), 2 * BLOCK)
        for lanes in halves(width):
            flow = conv(lambda r: (taps2, 2 * t + r), w2, groups, lanes) + jnp.dot(
                centred, first_m[:, lanes], preferred_element_type=F32
            )
            grad = flow * slope[at : at + step, lanes] * mask
            for r in range(2):
                write_taps(taps1, 2 * t + r, grad[r * pitch : (r + 1) * pitch], groups, lanes)
    for t in range(0, height, 2):
        got = conv(lambda r: (taps1, t + r), w1, groups, slice(None))
        for r in range(2):
            at = (t + r) * pitch
            for n in range(groups):
                part = got[r * pitch + n * 16 : r * pitch + (n + 1) * 16]
                for p in range(buf.shape[0]):
                    lanes = slice(p * BLOCK, (p + 1) * BLOCK)
                    buf[p, pl.ds(at + n, 16, stride=groups), :] = part[:, lanes]
            for p in range(buf.shape[0]):
                lanes = slice(p * BLOCK, (p + 1) * BLOCK)
                out[t + r, :, lanes] = buf[p, at : at + breadth, :]


def edges(place, pool, far, near):
    breadth = pool.shape[1]
    left_core = place[0] == 0
    left = pool[:, 0:REACH, :]
    right = pool[:, breadth - REACH : breadth, :]
    far[...] = jnp.where(left_core, left, right).astype(BF)
    near[...] = jnp.where(left_core, right, left).astype(BF)


def bands(place, pool, far, near, above, below, row):
    height, breadth, _ = pool.shape
    left_core = place[0] == 0
    for start, ref in ((height - REACH, above), (0, below)):
        for r in range(REACH):
            one, two = far[start + r].astype(F32), near[start + r].astype(F32)
            row[0:REACH, :] = jnp.where(left_core, one, two)
            row[REACH : REACH + breadth, :] = pool[start + r]
            row[REACH + breadth :, :] = jnp.where(left_core, two, one)
            ref[r] = row[...].astype(BF)


def flip(weight, out):
    taps, _, width = weight.shape

    def one(t, carry):
        at = pl.multiple_of(t * width, 16)
        out[pl.ds(at, width), :] = weight[taps - 1 - t].T
        return carry

    lax.fori_loop(0, taps, one, 0)


def aim(place, targets, goal, full):
    core = place[0]
    chunk = goal.shape[0]
    for n, (i, j) in enumerate(pairs(targets.shape[1])):
        rows, cols = slice(i * BLOCK, (i + 1) * BLOCK), slice(j * BLOCK, (j + 1) * BLOCK)
        block = (targets[core, rows, cols] + targets[core, cols, rows].T) * 0.5
        full[n * BLOCK : (n + 1) * BLOCK, :] = block
    goal[...] = full[pl.ds(pl.multiple_of(place[3] * chunk, 16), chunk), :]


def call(body, ins, outs, scratch, flops=0, limit=None):
    moved = sum(x.size * x.dtype.itemsize for x in ins) + sum(
        x.size * x.dtype.itemsize for x in outs
    )
    return pl.pallas_call(
        body,
        out_shape=tuple(outs),
        in_specs=[SMEM if x.dtype == jnp.int32 else VMEM for x in ins],
        out_specs=tuple(VMEM for _ in outs),
        scratch_shapes=scratch,
        compiler_params=pltpu.CompilerParams(vmem_limit_bytes=(limit or 8) * MIB),
        cost_estimate=pl.CostEstimate(flops=flops, bytes_accessed=moved, transcendentals=0),
    )(*ins)


def shape(dims, dtype):
    return jax.ShapeDtypeStruct(dims, dtype)


def local(pool_input, weight_first, weight_second, targets):
    height, breadth, depth = pool_input.shape
    width = weight_first.shape[3]
    groups, tiles = lax.axis_size("grp"), lax.axis_size("tile")
    chips = tiles // 2
    row, tile = lax.axis_index("grp"), lax.axis_index("tile")
    core = tile % 2
    cells = height * breadth
    positions = cells * groups * tiles
    fold = -(-(breadth + 2 * REACH) // 16)
    pitch, wider = fold * 16, (fold + 2) * 16
    blocks = width // BLOCK
    place = jnp.stack([core, row * height, tile * breadth, row]).astype(jnp.int32)
    dims = (height, breadth, fold, (height * groups, breadth * tiles))
    swap = [(i, i ^ 1) for i in range(tiles)]
    cross = [(i, i + 1) for i in range(1, tiles - 1, 2)]
    cross = cross + [(j, i) for i, j in cross]

    rim = shape((height, REACH, depth), BF)
    far, near = call(edges, [place, pool_input], [rim] * 2, [])
    far = lax.ppermute(far, "tile", cross)
    near = lax.ppermute(near, "tile", swap)
    band = shape((REACH, breadth + 2 * REACH, depth), BF)
    above, below = call(
        bands,
        [place, pool_input, far, near],
        [band] * 2,
        [pltpu.VMEM((breadth + 2 * REACH, depth), F32)],
    )
    up = [(i, i + 1) for i in range(groups - 1)]
    down = [(j, i) for i, j in up]
    above = lax.ppermute(above, "grp", up)
    below = lax.ppermute(below, "grp", down)

    packed = len(pairs(width)) * BLOCK
    w1 = weight_first.reshape(-1, width)
    w2 = weight_second.reshape(-1, width)
    space = (fold * 15 + fold + 2 + 7) // 8 * 8

    def maps(rows):
        return [shape((rows * pitch, width), F32)] * 2

    def cost(rows_first, rows_second):
        return 2 * 9 * width * pitch * (rows_first * depth + rows_second * width)

    taps1, taps2, act1, slope1, act2, slope2 = call(
        functools.partial(middle, dims),
        [place, pool_input, far, near, w1, w2],
        [shape((height * wider, depth), BF), shape(((height - 2) * wider, width), BF)]
        + maps(height - 2)
        + maps(height - 4),
        [pltpu.VMEM((depth // BLOCK, height * space, BLOCK), F32)],
        flops=cost(height - 2, height - 4),
        limit=24,
    )
    taps2b, act1b, slope1b, act2b, slope2b, keep, mine, sent = call(
        functools.partial(front, dims),
        [place, above, below, taps1, taps2, act1, act2, w1, w2],
        [shape((4 * wider, width), BF)]
        + maps(4)
        + maps(4)
        + [
            shape((packed, BLOCK), F32),
            shape((8, BLOCK), F32),
            shape((packed + EXTRA, BLOCK), BF),
        ],
        [
            pltpu.VMEM((4 * wider, depth), BF),
            pltpu.VMEM((depth // BLOCK, 4 * space, BLOCK), F32),
            pltpu.VMEM((2, packed, BLOCK), F32),
            pltpu.VMEM((2, 2 * EXTRA, BLOCK), F32),
        ],
        flops=cost(4, 4),
        limit=24,
    )
    act2r, slope2r = call(
        functools.partial(ring, dims),
        [place, above, below, taps2b, w1, w2],
        maps(4),
        [
            pltpu.VMEM((4 * wider, depth), BF),
            pltpu.VMEM((4 * wider, width), BF),
            pltpu.VMEM((depth // BLOCK, 4 * space, BLOCK), F32),
        ],
        flops=cost(4, 4),
        limit=16,
    )
    chunk = packed // groups
    (goal,) = call(
        aim,
        [place, targets],
        [shape((chunk, BLOCK), F32)],
        [pltpu.VMEM((packed, BLOCK), F32)],
        flops=2 * 10**8,
    )

    def turned(weight):
        inner = weight.shape[2]
        (out,) = call(
            flip,
            [weight.reshape(9, inner, width)],
            [shape((9 * width, inner), BF)],
            [],
            flops=2 * 10**9,
            limit=16,
        )
        return out

    back2 = turned(weight_second)
    back1 = turned(weight_first)

    def helpers(members):
        deep = -(-3 * members // 16) * 16
        return [
            pltpu.VMEM((packed, BLOCK), F32),
            pltpu.VMEM((deep, width), F32),
            pltpu.VMEM((deep, width), F32),
            pltpu.VMEM((EXTRA, BLOCK), F32),
        ]

    message = shape((chunk + EXTRA, BLOCK), BF)
    part, centre = shape((chunk, BLOCK), F32), shape((8, BLOCK), F32)
    got = lax.ppermute(sent, "tile", swap)
    share, mean, *sents = call(
        functools.partial(merge_pair, (cells, groups, blocks)),
        [place, keep, mine, got],
        [part, centre] + [message] * (groups - 1),
        helpers(2),
    )
    gots = [
        lax.ppermute(sents[k - 1], "grp", [(i, i ^ k) for i in range(groups)])
        for k in range(1, groups)
    ]
    share, mean, sent = call(
        functools.partial(merge_many, (2 * cells, groups, blocks), None),
        [place, share, mean] + gots,
        [part, centre, message],
        helpers(groups),
    )
    gots = [
        lax.ppermute(sent, "tile", [(i, i ^ (2 * k)) for i in range(tiles)])
        for k in range(1, chips)
    ]
    share, mean = call(
        functools.partial(merge_many, (2 * groups * cells, chips, blocks), positions),
        [place, share, mean] + gots + [goal],
        [shape((chunk, BLOCK), BF), shape((EXTRA, BLOCK), BF)],
        helpers(chips),
    )
    gots = [
        lax.ppermute(share, "grp", [(i, i ^ k) for i in range(groups)])
        for k in range(1, groups)
    ]
    table = shape((packed + EXTRA, BLOCK), BF)
    (mine,) = call(assemble, [place, share, mean] + gots, [table], [])
    other = lax.ppermute(mine, "tile", swap)
    maps_in = [act1, slope1, act1b, slope1b, act2, slope2, act2b, slope2b, act2r, slope2r]
    (out,) = call(
        functools.partial(back, dims),
        [place] + maps_in + [mine, other, back2, back1],
        [shape(pool_input.shape, F32)],
        [
            pltpu.VMEM(((height + 4) * wider, width), BF),
            pltpu.VMEM(((height + 2) * wider, width), BF),
            pltpu.VMEM((width, width), BF),
            pltpu.VMEM((width, width), BF),
            pltpu.VMEM((2, packed + EXTRA, BLOCK), BF),
            pltpu.VMEM((depth // BLOCK, height * pitch, BLOCK), F32),
        ],
        flops=2 * 9 * width * pitch * ((height + 2) * width + height * depth),
        limit=32,
    )
    return out


def solution(mesh):
    return jax.shard_map(
        local,
        mesh=mesh,
        in_specs=(P("grp", "tile", None), P(), P(), P()),
        out_specs=P("grp", "tile", None),
        check_vma=False,
    )
```

```python
import functools

import jax
import jax.numpy as jnp
from jax import lax
from jax.experimental import pallas as pl
from jax.experimental.pallas import tpu as pltpu
from jax.sharding import PartitionSpec as P


GELU_SCALE = 0.7978845608
GELU_CUBIC = 0.044715
REACH = 4
BLOCK = 128
EXTRA = 16
BF = jnp.bfloat16
F32 = jnp.float32
VMEM = pl.BlockSpec(memory_space=pltpu.VMEM)
SMEM = pl.BlockSpec(memory_space=pltpu.SMEM)
HBM = pl.BlockSpec(memory_space=pltpu.HBM)
MIB = 2**20


def gelu_pair(values):
    square = values * values
    hyper = jnp.tanh(GELU_SCALE * (values + GELU_CUBIC * values * square))
    half = 0.5 * (1.0 + hyper)
    slope = half + 0.5 * values * (1.0 - hyper * hyper) * (
        GELU_SCALE + 3.0 * GELU_SCALE * GELU_CUBIC * square
    )
    return values * half, slope


def pairs(width):
    blocks = width // BLOCK
    return [(i, j) for i in range(blocks) for j in range(i, blocks)]


def wide(mask, width):
    return jnp.concatenate([mask] * (width // BLOCK), axis=1)


def columns(groups):
    n = lax.broadcasted_iota(jnp.int32, (groups * 16, BLOCK), 0)
    return (n & 15) * groups + (n >> 4)


def span(groups, low, high):
    col = columns(groups)
    return jnp.where((col >= low) & (col < high), 1.0, 0.0).astype(F32)


def pair_mask(inside, place, limits, row):
    parts = []
    for r in range(2):
        at = place[1] + row + r
        parts.append(inside * jnp.where((at >= 0) & (at < limits[0]), 1.0, 0.0).astype(F32))
    return jnp.concatenate(parts, axis=0)


def roll_group(value):
    return [pltpu.roll(value[n * 16 : (n + 1) * 16], 15, 0) for n in range(2)]


def write_taps(ref, row, value, groups, lanes=slice(None)):
    at, pitch = row * (groups + 2) * 16, groups * 16
    ref[at : at + pitch, lanes] = value.astype(BF)
    for n, block in enumerate(roll_group(value)):
        ref[at + pitch + n * 16 : at + pitch + (n + 1) * 16, lanes] = block.astype(BF)


def fold_row(ref, row, buf_ref, at, groups):
    base = row * (groups + 2) * 16
    for n in range(groups + 2):
        for p in range(buf_ref.shape[0]):
            ref[base + n * 16 : base + (n + 1) * 16, p * BLOCK : (p + 1) * BLOCK] = buf_ref[
                p, pl.ds(at + n, 16, stride=groups), :
            ].astype(BF)


def put_row(buf_ref, at, value):
    for p in range(buf_ref.shape[0]):
        buf_ref[p, at : at + value.shape[0], :] = value[:, p * BLOCK : (p + 1) * BLOCK]


def clear_rows(buf_ref, start, stop):
    for p in range(buf_ref.shape[0]):
        buf_ref[p, start:stop, :] = jnp.zeros((stop - start, BLOCK), F32)


def conv(find, weight_ref, groups, lanes):
    pitch, pieces = groups * 16, []
    for a in range(3):
        for b in range(3):
            both = []
            for r in range(2):
                ref, row = find(r + a)
                at = (row * (groups + 2) + b) * 16
                both.append(ref[at : at + pitch, :])
            pieces.append(jnp.concatenate(both, axis=0))
    lhs = jnp.concatenate(pieces, axis=1)
    return jnp.dot(lhs, weight_ref[:, lanes], preferred_element_type=F32)


def halves(width):
    half = 2 * BLOCK
    return [slice(n, n + half) for n in range(0, width, half)]


def first_rows(find, w1, taps_ref, row, act, slope, at, groups, mask):
    width, pitch = w1.shape[1], groups * 16
    for lanes in halves(width):
        value, tilt = gelu_pair(conv(find, w1, groups, lanes))
        value = value * wide(mask, 2 * BLOCK)
        for r in range(2):
            one = value[r * pitch : (r + 1) * pitch]
            write_taps(taps_ref, row + r, one, groups, lanes)
            if act is None:
                continue
            two = tilt[r * pitch : (r + 1) * pitch]
            base = at + r * pitch
            for ref, part in ((act, one), (slope, two)):
                ref[base : base + pitch - 32, lanes] = part[32:]
                for n, block in enumerate(roll_group(part)):
                    to = base + pitch - 32 + n * 16
                    ref[to : to + 16, lanes] = block


def second_rows(find, w2, act, slope, at, groups):
    step = groups * 32
    for lanes in halves(w2.shape[1]):
        value, tilt = gelu_pair(conv(find, w2, groups, lanes))
        act[at : at + step, lanes] = value
        slope[at : at + step, lanes] = tilt


def put_mean(rows_ref, mean, parts):
    blocks = mean.shape[1] // BLOCK
    high = mean.astype(BF).astype(F32)
    for p, row in enumerate((high, mean - high) if parts == 2 else (mean,)):
        for j in range(blocks):
            at = p * blocks + j
            rows_ref[at : at + 1, :] = row[:, j * BLOCK : (j + 1) * BLOCK]


def get_mean(rows, blocks, parts):
    rows = rows.astype(F32)
    found = rows[:blocks] + rows[blocks : 2 * blocks] if parts == 2 else rows[:blocks]
    return jnp.concatenate([found[j : j + 1] for j in range(blocks)], axis=1)


def spread(means, count, left_ref, right_ref, emit):
    centre = means[0]
    for mean in means[1:]:
        centre = centre + mean
    centre = centre * (1.0 / len(means))
    left_ref[...] = jnp.zeros(left_ref.shape, F32)
    right_ref[...] = jnp.zeros(right_ref.shape, F32)
    for n, mean in enumerate(means):
        away = mean - centre
        high = away.astype(BF).astype(F32)
        low = away - high
        for q, (lhs, rhs) in enumerate(((high, high), (high, low), (low, high))):
            at = 3 * n + q
            left_ref[at : at + 1, :] = lhs
            right_ref[at : at + 1, :] = rhs
    lhs, rhs = left_ref[...].astype(BF), right_ref[...].astype(BF)
    for n, (i, j) in enumerate(pairs(lhs.shape[1])):
        product = lax.dot_general(
            lhs[:, i * BLOCK : (i + 1) * BLOCK],
            rhs[:, j * BLOCK : (j + 1) * BLOCK],
            (((0,), (0,)), ((), ())),
            preferred_element_type=F32,
        )
        emit(n, product * float(count))
    return centre


def middle(dims, place, pool, far, near, w1_hbm, w2_hbm, *rest):
    taps1, taps2, act1, slope1, act2, slope2, w1, w2, buf, sems = rest
    height, breadth, groups, limits = dims
    loads = [
        pltpu.make_async_copy(w1_hbm, w1, sems.at[0]),
        pltpu.make_async_copy(w2_hbm, w2, sems.at[1]),
    ]
    for load in loads:
        load.start()
    pitch = groups * 16
    left_core = place[0] == 0
    space = buf.shape[1] // height
    for r in range(height):
        at = r * space
        one, two = far[r].astype(F32), near[r].astype(F32)
        put_row(buf, at, jnp.where(left_core, one, two))
        put_row(buf, at + REACH, pool[r])
        put_row(buf, at + REACH + breadth, jnp.where(left_core, two, one))
        clear_rows(buf, at + 2 * REACH + breadth, at + space)
        fold_row(taps1, r, buf, at, groups)
    low = 3 - place[2]
    inside = span(groups, low, low + limits[1])
    loads[0].wait()
    for t in range(0, height - 2, 2):
        mask = pair_mask(inside, place, limits, t + 1)
        first_rows(
            lambda r: (taps1, t + r), w1, taps2, t, act1, slope1, t * pitch, groups, mask
        )
    loads[1].wait()
    for t in range(0, height - 4, 2):
        second_rows(lambda r: (taps2, t + r), w2, act2, slope2, t * pitch, groups)


def rim_taps(ref, rows, place, buf, groups):
    space = buf.shape[1] // len(rows)
    even = (place[3] & 1) == 0
    for n, (one, two, r) in enumerate(rows):
        breadth = one.shape[1]
        at = n * space
        put_row(buf, at, jnp.where(even, one[r].astype(F32), two[r].astype(F32)))
        clear_rows(buf, at + breadth, at + space)
        fold_row(ref, n, buf, at, groups)


def front(dims, place, even, odd, taps1, taps2, act1, act2, w1, w2, *rest):
    (taps2b, act1b, slope1b, act2b, slope2b, keep, mine, sent) = rest[:8]
    (rim, buf, gram, stat) = rest[8:]
    height, breadth, groups, limits = dims
    pitch = groups * 16
    width = w1.shape[1]
    blocks = width // BLOCK
    rows = [(odd, even, REACH - 2), (odd, even, REACH - 1), (even, odd, 0), (even, odd, 1)]
    rim_taps(rim, rows, place, buf, groups)
    low = 3 - place[2]
    inside = span(groups, low, low + limits[1])
    last = height - 2
    finds = (
        lambda r: (rim, r) if r < 2 else (taps1, r - 2),
        lambda r: (taps1, last + r) if r < 2 else (rim, r),
    )
    for n, row in enumerate((-1, height - 1)):
        mask = pair_mask(inside, place, limits, row)
        first_rows(
            finds[n], w1, taps2b, 2 * n, act1b, slope1b, 2 * n * pitch, groups, mask
        )
    last = height - 4
    finds = (
        lambda r: (taps2b, r) if r < 2 else (taps2, r - 2),
        lambda r: (taps2, last + r) if r < 2 else (taps2b, r),
    )
    for n in range(2):
        second_rows(finds[n], w2, act2b, slope2b, 2 * n * pitch, groups)
    cells = height * breadth
    first_parts = [(act1b, pitch, 2 * pitch), (act1, 0, (height - 2) * pitch)]
    second_parts = [(act2b, 0, 4 * pitch), (act2, 0, (height - 4) * pitch)]
    for layer, (parts, offset) in enumerate(((first_parts, 1), (second_parts, 2))):
        own = wide(span(groups, offset, offset + breadth), width)
        total = jnp.zeros((pitch, width), F32)
        for ref, start, count in parts:
            for at in range(start, start + count, pitch):
                total = total + ref[at : at + pitch, :]
        mean = jnp.sum(total * own, axis=0, keepdims=True) * (1.0 / cells)
        centred = jnp.concatenate(
            [
                ((ref[at : at + pitch, :] - mean) * own).astype(BF)
                for ref, start, count in parts
                for at in range(start, start + count, pitch)
            ],
            axis=0,
        )
        n = 0
        for i in range(blocks):
            panel = lax.dot_general(
                centred[:, i * BLOCK : (i + 1) * BLOCK],
                centred[:, i * BLOCK :],
                (((0,), (0,)), ((), ())),
                preferred_element_type=F32,
            )
            for j in range(i, blocks):
                gram[layer, n * BLOCK : (n + 1) * BLOCK, :] = panel[
                    :, (j - i) * BLOCK : (j - i + 1) * BLOCK
                ]
                n += 1
        stat[layer] = jnp.zeros(stat.shape[1:], F32)
        put_mean(stat.at[layer, 0:EXTRA], mean, 2)
        put_mean(stat.at[layer, EXTRA : 2 * EXTRA], mean, 1)
    rows = keep.shape[0]
    keep[...] = gram[place[0]]
    mine[...] = stat[place[0], EXTRA : EXTRA + 8, :]
    sent[0:rows, :] = gram[1 - place[0]].astype(BF)
    sent[rows:, :] = stat[1 - place[0], 0:EXTRA, :].astype(BF)


def ring(dims, place, even, odd, taps2b, w1, w2, act2, slope2, rim, outer, buf):
    height, _, groups, limits = dims
    low = 3 - place[2]
    inside = span(groups, low, low + limits[1])
    finds = (
        lambda r: (outer, r) if r < 2 else (taps2b, r - 2),
        lambda r: (taps2b, 2 + r) if r < 2 else (outer, r),
    )
    for n, (one, two, row) in enumerate(((odd, even, -3), (even, odd, height + 1))):
        rim_taps(rim, [(one, two, r) for r in range(REACH)], place, buf, groups)
        mask = pair_mask(inside, place, limits, row)
        first_rows(lambda r: (rim, r), w1, outer, 2 * n, None, None, 0, groups, mask)
        second_rows(finds[n], w2, act2, slope2, 2 * n * groups * 16, groups)


def write_message(ref, part, rows_ref, centre):
    count = part.shape[0]
    rows_ref[...] = jnp.zeros(rows_ref.shape, F32)
    put_mean(rows_ref, centre, 2)
    ref[0:count, :] = part.astype(BF)
    ref[count:, :] = rows_ref[...].astype(BF)


def merge_pair(dims, place, keep, mine, got, share, centre_out, *rest):
    count, groups, blocks = dims
    messages, (full, left, right, rows_ref) = rest[: groups - 1], rest[groups - 1 :]
    rows = keep.shape[0]
    chunk = rows // groups

    def emit(n, product):
        at = slice(n * BLOCK, (n + 1) * BLOCK)
        full[at, :] = keep[at, :] + got[at, :].astype(F32) + product

    means = [get_mean(mine[...], blocks, 1), get_mean(got[rows:, :], blocks, 2)]
    centre = spread(means, count, left, right, emit)
    centre_out[...] = jnp.zeros(centre_out.shape, F32)
    put_mean(centre_out, centre, 1)
    for k, ref in enumerate(messages, 1):
        at = pl.multiple_of((place[3] ^ k) * chunk, 16)
        write_message(ref, full[pl.ds(at, chunk), :], rows_ref, centre)
    share[...] = full[pl.ds(pl.multiple_of(place[3] * chunk, 16), chunk), :]


def merge_many(dims, final, place, share, mine, *rest):
    count, members, blocks = dims
    gots, rest = rest[: members - 1], rest[members - 1 :]
    chunk = share.shape[0]
    full, left, right, rows_ref = rest[-4:]

    def emit(n, product):
        full[n * BLOCK : (n + 1) * BLOCK, :] = product

    means = [get_mean(mine[...], blocks, 1)]
    means += [get_mean(got[chunk:, :], blocks, 2) for got in gots]
    centre = spread(means, count, left, right, emit)
    total = share[...] + full[pl.ds(pl.multiple_of(place[3] * chunk, 16), chunk), :]
    for got in gots:
        total = total + got[0:chunk, :].astype(F32)
    if final is None:
        out, centre_out, sent = rest[:3]
        out[...] = total
        centre_out[...] = jnp.zeros(centre_out.shape, F32)
        put_mean(centre_out, centre, 1)
        write_message(sent, total, rows_ref, centre)
    else:
        goal, sent, centre_out = rest[:3]
        rows_ref[...] = jnp.zeros(rows_ref.shape, F32)
        put_mean(rows_ref, centre, 2)
        centre_out[...] = rows_ref[...].astype(BF)
        sent[...] = (total * (1.0 / final) - goal[...]).astype(BF)


def assemble(place, share, centre, *rest):
    gots, out = rest[:-1], rest[-1]
    chunk = share.shape[0]
    for k, ref in enumerate((share,) + tuple(gots)):
        out[pl.ds(pl.multiple_of((place[3] ^ k) * chunk, 16), chunk), :] = ref[...]
    rows = chunk * (len(gots) + 1)
    out[rows:, :] = centre[...]


def back(dims, place, *rest):
    (act1, slope1, act1b, slope1b, act2, slope2, act2b, slope2b, act2r, slope2r) = rest[:10]
    (mine, other, w2, w1, out, taps2, taps1, first_m, second_m, table, buf) = rest[10:]
    height, breadth, groups, limits = dims
    pitch = groups * 16
    step = 2 * pitch
    width = act1.shape[1]
    blocks = width // BLOCK
    packed = table.shape[1] - EXTRA
    table[place[0]] = mine[...]
    table[1 - place[0]] = other[...]
    means = []
    for layer, ref in enumerate((first_m, second_m)):
        for n, (i, j) in enumerate(pairs(width)):
            block = table[layer, n * BLOCK : (n + 1) * BLOCK, :]
            ref[i * BLOCK : (i + 1) * BLOCK, j * BLOCK : (j + 1) * BLOCK] = block
            if i != j:
                ref[j * BLOCK : (j + 1) * BLOCK, i * BLOCK : (i + 1) * BLOCK] = block.T
        means.append(get_mean(table[layer, packed:, :], blocks, 2))
    low = 2 - place[2]
    inside = span(groups, low, low + limits[1])
    tiles = [(act2r, slope2r, 0), (act2b, slope2b, 0)]
    tiles += [(act2, slope2, t * pitch) for t in range(0, height - 4, 2)]
    tiles += [(act2b, slope2b, step), (act2r, slope2r, step)]
    for t, (act, slope, at) in enumerate(tiles):
        centred = (act[at : at + step, :] - means[1]).astype(BF)
        mask = wide(pair_mask(inside, place, limits, 2 * t - 2), 2 * BLOCK)
        for lanes in halves(width):
            push = jnp.dot(centred, second_m[:, lanes], preferred_element_type=F32)
            grad = push * slope[at : at + step, lanes] * mask
            for r in range(2):
                write_taps(taps2, 2 * t + r, grad[r * pitch : (r + 1) * pitch], groups, lanes)
    low = 1 - place[2]
    inside = span(groups, low, low + limits[1])
    tiles = [(act1b, slope1b, 0)]
    tiles += [(act1, slope1, t * pitch) for t in range(0, height - 2, 2)]
    tiles += [(act1b, slope1b, step)]
    for t, (act, slope, at) in enumerate(tiles):
        centred = (act[at : at + step, :] - means[0]).astype(BF)
        mask = wide(pair_mask(inside, place, limits, 2 * t - 1), 2 * BLOCK)
        for lanes in halves(width):
            flow = conv(lambda r: (taps2, 2 * t + r), w2, groups, lanes) + jnp.dot(
                centred, first_m[:, lanes], preferred_element_type=F32
            )
            grad = flow * slope[at : at + step, lanes] * mask
            for r in range(2):
                write_taps(taps1, 2 * t + r, grad[r * pitch : (r + 1) * pitch], groups, lanes)
    for t in range(0, height, 2):
        got = conv(lambda r: (taps1, t + r), w1, groups, slice(None))
        for r in range(2):
            at = (t + r) * pitch
            for n in range(groups):
                part = got[r * pitch + n * 16 : r * pitch + (n + 1) * 16]
                for p in range(buf.shape[0]):
                    lanes = slice(p * BLOCK, (p + 1) * BLOCK)
                    buf[p, pl.ds(at + n, 16, stride=groups), :] = part[:, lanes]
            for p in range(buf.shape[0]):
                lanes = slice(p * BLOCK, (p + 1) * BLOCK)
                out[t + r, :, lanes] = buf[p, at : at + breadth, :]


def edges(place, pool_hbm, pool, far, near, sem):
    load = pltpu.make_async_copy(pool_hbm, pool, sem)
    load.start()
    load.wait()
    breadth = pool.shape[1]
    left_core = place[0] == 0
    left = pool[:, 0:REACH, :]
    right = pool[:, breadth - REACH : breadth, :]
    far[...] = jnp.where(left_core, left, right).astype(BF)
    near[...] = jnp.where(left_core, right, left).astype(BF)


def bands(place, pool, far, near, even, odd, row):
    height, breadth, _ = pool.shape
    left_core = place[0] == 0
    odd_row = place[3] & 1
    for start, ref in ((1 - odd_row, even), (odd_row, odd)):
        for r in range(REACH):
            at = start * (height - REACH) + r
            one, two = far[at].astype(F32), near[at].astype(F32)
            row[0:REACH, :] = jnp.where(left_core, one, two)
            row[REACH : REACH + breadth, :] = pool[at]
            row[REACH + breadth :, :] = jnp.where(left_core, two, one)
            ref[r] = row[...].astype(BF)


def flip(weight, out):
    taps, _, width = weight.shape

    def one(t, carry):
        at = pl.multiple_of(t * width, 16)
        out[pl.ds(at, width), :] = weight[taps - 1 - t].T
        return carry

    lax.fori_loop(0, taps, one, 0)


def aim(place, targets, goal, full):
    core = place[0]
    chunk = goal.shape[0]
    for n, (i, j) in enumerate(pairs(targets.shape[1])):
        rows, cols = slice(i * BLOCK, (i + 1) * BLOCK), slice(j * BLOCK, (j + 1) * BLOCK)
        block = (targets[core, rows, cols] + targets[core, cols, rows].T) * 0.5
        full[n * BLOCK : (n + 1) * BLOCK, :] = block
    goal[...] = full[pl.ds(pl.multiple_of(place[3] * chunk, 16), chunk), :]


def call(body, ins, outs, scratch, flops=0, limit=None, far=()):
    ins = [
        pltpu.with_memory_space_constraint(x, pltpu.HBM) if n in far else x
        for n, x in enumerate(ins)
    ]
    moved = sum(x.size * x.dtype.itemsize for x in ins) + sum(
        x.size * x.dtype.itemsize for x in outs
    )
    return pl.pallas_call(
        body,
        out_shape=tuple(outs),
        in_specs=[
            HBM if n in far else SMEM if x.dtype == jnp.int32 else VMEM for n, x in enumerate(ins)
        ],
        out_specs=tuple(VMEM for _ in outs),
        scratch_shapes=scratch,
        compiler_params=pltpu.CompilerParams(vmem_limit_bytes=(limit or 8) * MIB),
        cost_estimate=pl.CostEstimate(flops=flops, bytes_accessed=moved, transcendentals=0),
    )(*ins)


def shape(dims, dtype):
    return jax.ShapeDtypeStruct(dims, dtype)


def local(pool_input, weight_first, weight_second, targets):
    height, breadth, depth = pool_input.shape
    width = weight_first.shape[3]
    groups, tiles = lax.axis_size("grp"), lax.axis_size("tile")
    chips = tiles // 2
    row, tile = lax.axis_index("grp"), lax.axis_index("tile")
    core = tile % 2
    cells = height * breadth
    positions = cells * groups * tiles
    fold = -(-(breadth + 2 * REACH) // 16)
    pitch, wider = fold * 16, (fold + 2) * 16
    blocks = width // BLOCK
    place = jnp.stack([core, row * height, tile * breadth, row]).astype(jnp.int32)
    dims = (height, breadth, fold, (height * groups, breadth * tiles))
    swap = [(i, i ^ 1) for i in range(tiles)]
    cross = [(i, i + 1) for i in range(1, tiles - 1, 2)]
    cross = cross + [(j, i) for i, j in cross]

    rim = shape((height, REACH, depth), BF)
    pool, far, near = call(
        edges,
        [place, pool_input],
        [shape(pool_input.shape, F32)] + [rim] * 2,
        [pltpu.SemaphoreType.DMA],
        far=(1,),
    )
    far = lax.ppermute(far, "tile", cross)
    near = lax.ppermute(near, "tile", swap)
    band = shape((REACH, breadth + 2 * REACH, depth), BF)
    even, odd = call(
        bands, [place, pool, far, near], [band] * 2, [pltpu.VMEM((breadth + 2 * REACH, depth), F32)]
    )

    def couples(start):
        ways = [(i, i + 1) for i in range(start, groups - 1, 2)]
        return ways + [(j, i) for i, j in ways]

    even = lax.ppermute(even, "grp", couples(0))
    odd = lax.ppermute(odd, "grp", couples(1))

    packed = len(pairs(width)) * BLOCK
    space = (fold * 15 + fold + 2 + 7) // 8 * 8

    def maps(rows):
        return [shape((rows * pitch, width), F32)] * 2

    def cost(rows_first, rows_second):
        return 2 * 9 * width * pitch * (rows_first * depth + rows_second * width)

    taps1, taps2, act1, slope1, act2, slope2, w1, w2 = call(
        functools.partial(middle, dims),
        [place, pool, far, near]
        + [weight_first.reshape(-1, width), weight_second.reshape(-1, width)],
        [shape((height * wider, depth), BF), shape(((height - 2) * wider, width), BF)]
        + maps(height - 2)
        + maps(height - 4)
        + [shape((9 * depth, width), BF), shape((9 * width, width), BF)],
        [pltpu.VMEM((depth // BLOCK, height * space, BLOCK), F32), pltpu.SemaphoreType.DMA((2,))],
        flops=cost(height - 2, height - 4),
        limit=24,
        far=(4, 5),
    )
    taps2b, act1b, slope1b, act2b, slope2b, keep, mine, sent = call(
        functools.partial(front, dims),
        [place, even, odd, taps1, taps2, act1, act2, w1, w2],
        [shape((4 * wider, width), BF)]
        + maps(4)
        + maps(4)
        + [
            shape((packed, BLOCK), F32),
            shape((8, BLOCK), F32),
            shape((packed + EXTRA, BLOCK), BF),
        ],
        [
            pltpu.VMEM((4 * wider, depth), BF),
            pltpu.VMEM((depth // BLOCK, 4 * space, BLOCK), F32),
            pltpu.VMEM((2, packed, BLOCK), F32),
            pltpu.VMEM((2, 2 * EXTRA, BLOCK), F32),
        ],
        flops=cost(4, 4),
        limit=24,
    )
    act2r, slope2r = call(
        functools.partial(ring, dims),
        [place, even, odd, taps2b, w1, w2],
        maps(4),
        [
            pltpu.VMEM((4 * wider, depth), BF),
            pltpu.VMEM((4 * wider, width), BF),
            pltpu.VMEM((depth // BLOCK, 4 * space, BLOCK), F32),
        ],
        flops=cost(4, 4),
        limit=16,
    )
    chunk = packed // groups
    (goal,) = call(
        aim,
        [place, targets],
        [shape((chunk, BLOCK), F32)],
        [pltpu.VMEM((packed, BLOCK), F32)],
        flops=2 * 10**8,
    )

    def turned(weight, inner):
        (out,) = call(
            flip,
            [weight.reshape(9, inner, width)],
            [shape((9 * width, inner), BF)],
            [],
            flops=2 * 10**9,
            limit=16,
        )
        return out

    back2 = turned(w2, width)
    back1 = turned(w1, depth)

    def helpers(members):
        deep = -(-3 * members // 16) * 16
        return [
            pltpu.VMEM((packed, BLOCK), F32),
            pltpu.VMEM((deep, width), F32),
            pltpu.VMEM((deep, width), F32),
            pltpu.VMEM((EXTRA, BLOCK), F32),
        ]

    message = shape((chunk + EXTRA, BLOCK), BF)
    part, centre = shape((chunk, BLOCK), F32), shape((8, BLOCK), F32)
    got = lax.ppermute(sent, "tile", swap)
    share, mean, *sents = call(
        functools.partial(merge_pair, (cells, groups, blocks)),
        [place, keep, mine, got],
        [part, centre] + [message] * (groups - 1),
        helpers(2),
    )
    gots = [
        lax.ppermute(sents[k - 1], "grp", [(i, i ^ k) for i in range(groups)])
        for k in range(1, groups)
    ]
    share, mean, sent = call(
        functools.partial(merge_many, (2 * cells, groups, blocks), None),
        [place, share, mean] + gots,
        [part, centre, message],
        helpers(groups),
    )
    gots = [
        lax.ppermute(sent, "tile", [(i, i ^ (2 * k)) for i in range(tiles)])
        for k in range(1, chips)
    ]
    share, mean = call(
        functools.partial(merge_many, (2 * groups * cells, chips, blocks), positions),
        [place, share, mean] + gots + [goal],
        [shape((chunk, BLOCK), BF), shape((EXTRA, BLOCK), BF)],
        helpers(chips),
    )
    gots = [
        lax.ppermute(share, "grp", [(i, i ^ k) for i in range(groups)])
        for k in range(1, groups)
    ]
    table = shape((packed + EXTRA, BLOCK), BF)
    (mine,) = call(assemble, [place, share, mean] + gots, [table], [])
    other = lax.ppermute(mine, "tile", swap)
    maps_in = [act1, slope1, act1b, slope1b, act2, slope2, act2b, slope2b, act2r, slope2r]
    (out,) = call(
        functools.partial(back, dims),
        [place] + maps_in + [mine, other, back2, back1],
        [shape(pool_input.shape, F32)],
        [
            pltpu.VMEM(((height + 4) * wider, width), BF),
            pltpu.VMEM(((height + 2) * wider, width), BF),
            pltpu.VMEM((width, width), BF),
            pltpu.VMEM((width, width), BF),
            pltpu.VMEM((2, packed + EXTRA, BLOCK), BF),
            pltpu.VMEM((depth // BLOCK, height * pitch, BLOCK), F32),
        ],
        flops=2 * 9 * width * pitch * ((height + 2) * width + height * depth),
        limit=32,
    )
    return out


def solution(mesh):
    return jax.shard_map(
        local,
        mesh=mesh,
        in_specs=(P("grp", "tile", None), P(), P(), P()),
        out_specs=P("grp", "tile", None),
        check_vma=False,
    )
```

```python
import functools

import jax
import jax.numpy as jnp
from jax import lax
from jax.experimental import pallas as pl
from jax.experimental.pallas import tpu as pltpu
from jax.sharding import PartitionSpec as P


GELU_SCALE = 0.7978845608
GELU_CUBIC = 0.044715
REACH = 4
BLOCK = 128
EXTRA = 16
BF = jnp.bfloat16
F32 = jnp.float32
VMEM = pl.BlockSpec(memory_space=pltpu.VMEM)
SMEM = pl.BlockSpec(memory_space=pltpu.SMEM)
HBM = pl.BlockSpec(memory_space=pltpu.HBM)
MIB = 2**20


def gelu_pair(values):
    square = values * values
    hyper = jnp.tanh(GELU_SCALE * (values + GELU_CUBIC * values * square))
    half = 0.5 * (1.0 + hyper)
    slope = half + 0.5 * values * (1.0 - hyper * hyper) * (
        GELU_SCALE + 3.0 * GELU_SCALE * GELU_CUBIC * square
    )
    return values * half, slope


def pairs(width):
    blocks = width // BLOCK
    return [(i, j) for i in range(blocks) for j in range(i, blocks)]


def wide(mask, width):
    return jnp.concatenate([mask] * (width // BLOCK), axis=1)


def columns(groups):
    n = lax.broadcasted_iota(jnp.int32, (groups * 16, BLOCK), 0)
    return (n & 15) * groups + (n >> 4)


def span(groups, low, high):
    col = columns(groups)
    return jnp.where((col >= low) & (col < high), 1.0, 0.0).astype(F32)


def pair_mask(inside, place, limits, row):
    parts = []
    for r in range(2):
        at = place[1] + row + r
        parts.append(inside * jnp.where((at >= 0) & (at < limits[0]), 1.0, 0.0).astype(F32))
    return jnp.concatenate(parts, axis=0)


def roll_group(value):
    return [pltpu.roll(value[n * 16 : (n + 1) * 16], 15, 0) for n in range(2)]


def write_taps(ref, row, value, groups, lanes=slice(None)):
    at, pitch = row * (groups + 2) * 16, groups * 16
    ref[at : at + pitch, lanes] = value.astype(BF)
    for n, block in enumerate(roll_group(value)):
        ref[at + pitch + n * 16 : at + pitch + (n + 1) * 16, lanes] = block.astype(BF)


def fold_row(ref, row, buf_ref, at, groups):
    base = row * (groups + 2) * 16
    for n in range(groups + 2):
        for p in range(buf_ref.shape[0]):
            ref[base + n * 16 : base + (n + 1) * 16, p * BLOCK : (p + 1) * BLOCK] = buf_ref[
                p, pl.ds(at + n, 16, stride=groups), :
            ].astype(BF)


def put_row(buf_ref, at, value):
    for p in range(buf_ref.shape[0]):
        buf_ref[p, at : at + value.shape[0], :] = value[:, p * BLOCK : (p + 1) * BLOCK]


def clear_rows(buf_ref, start, stop):
    for p in range(buf_ref.shape[0]):
        buf_ref[p, start:stop, :] = jnp.zeros((stop - start, BLOCK), F32)


def conv(find, weight_ref, groups, lanes):
    pitch, pieces = groups * 16, []
    for a in range(3):
        for b in range(3):
            both = []
            for r in range(2):
                ref, row = find(r + a)
                at = (row * (groups + 2) + b) * 16
                both.append(ref[at : at + pitch, :])
            pieces.append(jnp.concatenate(both, axis=0))
    lhs = jnp.concatenate(pieces, axis=1)
    return jnp.dot(lhs, weight_ref[:, lanes], preferred_element_type=F32)


def halves(width):
    half = 2 * BLOCK
    return [slice(n, n + half) for n in range(0, width, half)]


def first_rows(find, w1, taps_ref, row, act, slope, at, groups, mask):
    width, pitch = w1.shape[1], groups * 16
    for lanes in halves(width):
        value, tilt = gelu_pair(conv(find, w1, groups, lanes))
        value = value * wide(mask, 2 * BLOCK)
        for r in range(2):
            one = value[r * pitch : (r + 1) * pitch]
            write_taps(taps_ref, row + r, one, groups, lanes)
            if act is None:
                continue
            two = tilt[r * pitch : (r + 1) * pitch]
            base = at + r * pitch
            for ref, part in ((act, one), (slope, two)):
                ref[base : base + pitch - 32, lanes] = part[32:]
                for n, block in enumerate(roll_group(part)):
                    to = base + pitch - 32 + n * 16
                    ref[to : to + 16, lanes] = block


def second_rows(find, w2, act, slope, at, groups):
    step = groups * 32
    for lanes in halves(w2.shape[1]):
        value, tilt = gelu_pair(conv(find, w2, groups, lanes))
        act[at : at + step, lanes] = value
        slope[at : at + step, lanes] = tilt


def put_mean(rows_ref, mean, parts):
    blocks = mean.shape[1] // BLOCK
    high = mean.astype(BF).astype(F32)
    for p, row in enumerate((high, mean - high) if parts == 2 else (mean,)):
        for j in range(blocks):
            at = p * blocks + j
            rows_ref[at : at + 1, :] = row[:, j * BLOCK : (j + 1) * BLOCK]


def get_mean(rows, blocks, parts):
    rows = rows.astype(F32)
    found = rows[:blocks] + rows[blocks : 2 * blocks] if parts == 2 else rows[:blocks]
    return jnp.concatenate([found[j : j + 1] for j in range(blocks)], axis=1)


def panels(lhs, rhs, emit):
    width, n = lhs.shape[1], 0
    for i in range(0, width, BLOCK):
        panel = lax.dot_general(
            lhs[:, i : i + BLOCK],
            rhs[:, i:],
            (((0,), (0,)), ((), ())),
            preferred_element_type=F32,
        )
        for j in range(0, width - i, BLOCK):
            emit(n, panel[:, j : j + BLOCK])
            n += 1


def spread(means, count, left_ref, right_ref, emit):
    centre = means[0]
    for mean in means[1:]:
        centre = centre + mean
    centre = centre * (1.0 / len(means))
    left_ref[...] = jnp.zeros(left_ref.shape, F32)
    right_ref[...] = jnp.zeros(right_ref.shape, F32)
    for n, mean in enumerate(means):
        away = mean - centre
        high = away.astype(BF).astype(F32)
        low = away - high
        for q, (lhs, rhs) in enumerate(((high, high), (high, low), (low, high))):
            at = 3 * n + q
            left_ref[at : at + 1, :] = lhs
            right_ref[at : at + 1, :] = rhs
    lhs, rhs = left_ref[...].astype(BF), right_ref[...].astype(BF)
    panels(lhs, rhs, lambda n, block: emit(n, block * float(count)))
    return centre


def middle(dims, place, pool, far, near, w1, w2, *rest):
    taps1, taps2, act1, slope1, act2, slope2, buf = rest
    height, breadth, groups, limits = dims
    pitch = groups * 16
    left_core = place[0] == 0
    space = buf.shape[1] // height
    for r in range(height):
        at = r * space
        one, two = far[r].astype(F32), near[r].astype(F32)
        put_row(buf, at, jnp.where(left_core, one, two))
        put_row(buf, at + REACH, pool[r])
        put_row(buf, at + REACH + breadth, jnp.where(left_core, two, one))
        clear_rows(buf, at + 2 * REACH + breadth, at + space)
        fold_row(taps1, r, buf, at, groups)
    low = 3 - place[2]
    inside = span(groups, low, low + limits[1])
    for t in range(0, height - 2, 2):
        mask = pair_mask(inside, place, limits, t + 1)
        first_rows(
            lambda r: (taps1, t + r), w1, taps2, t, act1, slope1, t * pitch, groups, mask
        )
        if t >= 2:
            second_rows(
                lambda r: (taps2, t - 2 + r), w2, act2, slope2, (t - 2) * pitch, groups
            )


def rim_taps(ref, rows, place, buf, groups):
    space = buf.shape[1] // len(rows)
    even = (place[3] & 1) == 0
    for n, (one, two, r) in enumerate(rows):
        breadth = one.shape[1]
        at = n * space
        put_row(buf, at, jnp.where(even, one[r].astype(F32), two[r].astype(F32)))
        clear_rows(buf, at + breadth, at + space)
        fold_row(ref, n, buf, at, groups)


def front(dims, place, even, odd, taps1, taps2, act1, act2, w1, w2, *rest):
    (taps2b, act1b, slope1b, act2b, slope2b, keep, mine, sent) = rest[:8]
    (rim, buf, centred, stat) = rest[8:]
    height, breadth, groups, limits = dims
    pitch = groups * 16
    width = w1.shape[1]
    rows = [(odd, even, REACH - 2), (odd, even, REACH - 1), (even, odd, 0), (even, odd, 1)]
    rim_taps(rim, rows, place, buf, groups)
    low = 3 - place[2]
    inside = span(groups, low, low + limits[1])
    last = height - 2
    finds = (
        lambda r: (rim, r) if r < 2 else (taps1, r - 2),
        lambda r: (taps1, last + r) if r < 2 else (rim, r),
    )
    for n, row in enumerate((-1, height - 1)):
        mask = pair_mask(inside, place, limits, row)
        first_rows(
            finds[n], w1, taps2b, 2 * n, act1b, slope1b, 2 * n * pitch, groups, mask
        )
    last = height - 4
    finds = (
        lambda r: (taps2b, r) if r < 2 else (taps2, r - 2),
        lambda r: (taps2, last + r) if r < 2 else (taps2b, r),
    )
    for n in range(2):
        second_rows(finds[n], w2, act2b, slope2b, 2 * n * pitch, groups)
    cells = height * breadth
    first_parts = [(act1b, pitch, 2 * pitch), (act1, 0, (height - 2) * pitch)]
    second_parts = [(act2b, 0, 4 * pitch), (act2, 0, (height - 4) * pitch)]
    for layer, (parts, offset) in enumerate(((first_parts, 1), (second_parts, 2))):
        own = wide(span(groups, offset, offset + breadth), width)
        total = jnp.zeros((pitch, width), F32)
        for ref, start, count in parts:
            for at in range(start, start + count, pitch):
                total = total + ref[at : at + pitch, :]
        mean = jnp.sum(total * own, axis=0, keepdims=True) * (1.0 / cells)
        n = 0
        for ref, start, count in parts:
            for at in range(start, start + count, pitch):
                centred[layer, n : n + pitch, :] = ((ref[at : at + pitch, :] - mean) * own).astype(
                    BF
                )
                n += pitch
        stat[layer] = jnp.zeros(stat.shape[1:], F32)
        put_mean(stat.at[layer, 0:EXTRA], mean, 2)
        put_mean(stat.at[layer, EXTRA : 2 * EXTRA], mean, 1)
    rows = keep.shape[0]

    def give(n, block):
        sent[n * BLOCK : (n + 1) * BLOCK, :] = block.astype(BF)

    def hold(n, block):
        keep[n * BLOCK : (n + 1) * BLOCK, :] = block

    for layer, emit in ((1 - place[0], give), (place[0], hold)):
        panels(centred[layer], centred[layer], emit)
    mine[...] = stat[place[0], EXTRA : EXTRA + 8, :]
    sent[rows:, :] = stat[1 - place[0], 0:EXTRA, :].astype(BF)


def ring(dims, place, even, odd, taps2b, w1, w2, act2, slope2, rim, outer, buf):
    height, _, groups, limits = dims
    low = 3 - place[2]
    inside = span(groups, low, low + limits[1])
    finds = (
        lambda r: (outer, r) if r < 2 else (taps2b, r - 2),
        lambda r: (taps2b, 2 + r) if r < 2 else (outer, r),
    )
    for n, (one, two, row) in enumerate(((odd, even, -3), (even, odd, height + 1))):
        rim_taps(rim, [(one, two, r) for r in range(REACH)], place, buf, groups)
        mask = pair_mask(inside, place, limits, row)
        first_rows(lambda r: (rim, r), w1, outer, 2 * n, None, None, 0, groups, mask)
        second_rows(finds[n], w2, act2, slope2, 2 * n * groups * 16, groups)


def write_message(ref, part, rows_ref, centre):
    count = part.shape[0]
    rows_ref[...] = jnp.zeros(rows_ref.shape, F32)
    put_mean(rows_ref, centre, 2)
    ref[0:count, :] = part.astype(BF)
    ref[count:, :] = rows_ref[...].astype(BF)


def merge_pair(dims, place, keep, mine, got, share, centre_out, *rest):
    count, groups, blocks = dims
    messages, (full, left, right, rows_ref) = rest[: groups - 1], rest[groups - 1 :]
    rows = keep.shape[0]
    chunk = rows // groups

    def emit(n, product):
        at = slice(n * BLOCK, (n + 1) * BLOCK)
        full[at, :] = keep[at, :] + got[at, :].astype(F32) + product

    means = [get_mean(mine[...], blocks, 1), get_mean(got[rows:, :], blocks, 2)]
    centre = spread(means, count, left, right, emit)
    centre_out[...] = jnp.zeros(centre_out.shape, F32)
    put_mean(centre_out, centre, 1)
    for k, ref in enumerate(messages, 1):
        at = pl.multiple_of((place[3] ^ k) * chunk, 16)
        write_message(ref, full[pl.ds(at, chunk), :], rows_ref, centre)
    share[...] = full[pl.ds(pl.multiple_of(place[3] * chunk, 16), chunk), :]


def merge_many(dims, final, place, share, mine, *rest):
    count, members, blocks = dims
    gots, rest = rest[: members - 1], rest[members - 1 :]
    chunk = share.shape[0]
    full, left, right, rows_ref = rest[-4:]

    def emit(n, product):
        full[n * BLOCK : (n + 1) * BLOCK, :] = product

    means = [get_mean(mine[...], blocks, 1)]
    means += [get_mean(got[chunk:, :], blocks, 2) for got in gots]
    centre = spread(means, count, left, right, emit)
    total = share[...] + full[pl.ds(pl.multiple_of(place[3] * chunk, 16), chunk), :]
    for got in gots:
        total = total + got[0:chunk, :].astype(F32)
    if final is None:
        out, centre_out, sent = rest[:3]
        out[...] = total
        centre_out[...] = jnp.zeros(centre_out.shape, F32)
        put_mean(centre_out, centre, 1)
        write_message(sent, total, rows_ref, centre)
    else:
        goal, sent, centre_out = rest[:3]
        rows_ref[...] = jnp.zeros(rows_ref.shape, F32)
        put_mean(rows_ref, centre, 2)
        centre_out[...] = rows_ref[...].astype(BF)
        sent[...] = (total * (1.0 / final) - goal[...]).astype(BF)


def assemble(place, share, centre, *rest):
    gots, out = rest[:-1], rest[-1]
    chunk = share.shape[0]
    for k, ref in enumerate((share,) + tuple(gots)):
        out[pl.ds(pl.multiple_of((place[3] ^ k) * chunk, 16), chunk), :] = ref[...]
    rows = chunk * (len(gots) + 1)
    out[rows:, :] = centre[...]


def back(dims, place, *rest):
    (act1, slope1, act1b, slope1b, act2, slope2, act2b, slope2b, act2r, slope2r) = rest[:10]
    (mine, other, w2, w1, out, taps2, taps1, first_m, second_m, table, buf) = rest[10:]
    height, breadth, groups, limits = dims
    pitch = groups * 16
    step = 2 * pitch
    width = act1.shape[1]
    blocks = width // BLOCK
    packed = table.shape[1] - EXTRA
    table[place[0]] = mine[...]
    table[1 - place[0]] = other[...]
    means = []
    for layer, ref in enumerate((first_m, second_m)):
        for n, (i, j) in enumerate(pairs(width)):
            block = table[layer, n * BLOCK : (n + 1) * BLOCK, :]
            ref[i * BLOCK : (i + 1) * BLOCK, j * BLOCK : (j + 1) * BLOCK] = block
            if i != j:
                ref[j * BLOCK : (j + 1) * BLOCK, i * BLOCK : (i + 1) * BLOCK] = block.T
        means.append(get_mean(table[layer, packed:, :], blocks, 2))
    low = 2 - place[2]
    inside2 = span(groups, low, low + limits[1])
    tiles2 = [(act2r, slope2r, 0), (act2b, slope2b, 0)]
    tiles2 += [(act2, slope2, t * pitch) for t in range(0, height - 4, 2)]
    tiles2 += [(act2b, slope2b, step), (act2r, slope2r, step)]

    def second(t):
        act, slope, at = tiles2[t]
        centred = (act[at : at + step, :] - means[1]).astype(BF)
        mask = wide(pair_mask(inside2, place, limits, 2 * t - 2), 2 * BLOCK)
        for lanes in halves(width):
            push = jnp.dot(centred, second_m[:, lanes], preferred_element_type=F32)
            grad = push * slope[at : at + step, lanes] * mask
            for r in range(2):
                write_taps(taps2, 2 * t + r, grad[r * pitch : (r + 1) * pitch], groups, lanes)

    low = 1 - place[2]
    inside1 = span(groups, low, low + limits[1])
    tiles1 = [(act1b, slope1b, 0)]
    tiles1 += [(act1, slope1, t * pitch) for t in range(0, height - 2, 2)]
    tiles1 += [(act1b, slope1b, step)]

    def first(t):
        act, slope, at = tiles1[t]
        centred = (act[at : at + step, :] - means[0]).astype(BF)
        mask = wide(pair_mask(inside1, place, limits, 2 * t - 1), 2 * BLOCK)
        for lanes in halves(width):
            flow = conv(lambda r: (taps2, 2 * t + r), w2, groups, lanes) + jnp.dot(
                centred, first_m[:, lanes], preferred_element_type=F32
            )
            grad = flow * slope[at : at + step, lanes] * mask
            for r in range(2):
                write_taps(taps1, 2 * t + r, grad[r * pitch : (r + 1) * pitch], groups, lanes)

    def last(t):
        got = conv(lambda r: (taps1, 2 * t + r), w1, groups, slice(None))
        for r in range(2):
            at = (2 * t + r) * pitch
            for p in range(buf.shape[0]):
                lanes = slice(p * BLOCK, (p + 1) * BLOCK)
                for n in range(groups):
                    part = got[r * pitch + n * 16 : r * pitch + (n + 1) * 16, lanes]
                    buf[p, pl.ds(at + n, 16, stride=groups), :] = part
                out[2 * t + r, :, lanes] = buf[p, at : at + breadth, :]

    for t in range(len(tiles2)):
        second(t)
    for t in range(len(tiles1)):
        first(t)
    for t in range(height // 2):
        last(t)


def edges(place, pool_hbm, far, near, strips, sems):
    breadth = pool_hbm.shape[1]
    ends = (0, breadth - 8)
    loads = [
        pltpu.make_async_copy(pool_hbm.at[:, pl.ds(at, 8), :], strips.at[n], sems.at[n])
        for n, at in enumerate(ends)
    ]
    for load in loads:
        load.start()
    for load in loads:
        load.wait()
    left_core = place[0] == 0
    left, right = strips[0, :, 0:REACH, :], strips[1, :, 8 - REACH :, :]
    far[...] = jnp.where(left_core, left, right).astype(BF)
    near[...] = jnp.where(left_core, right, left).astype(BF)


def bands(place, pool, far, near, even, odd, row):
    height, breadth, _ = pool.shape
    left_core = place[0] == 0
    odd_row = place[3] & 1
    for start, ref in ((1 - odd_row, even), (odd_row, odd)):
        for r in range(REACH):
            at = start * (height - REACH) + r
            one, two = far[at].astype(F32), near[at].astype(F32)
            row[0:REACH, :] = jnp.where(left_core, one, two)
            row[REACH : REACH + breadth, :] = pool[at]
            row[REACH + breadth :, :] = jnp.where(left_core, two, one)
            ref[r] = row[...].astype(BF)


def flip(weight, out):
    taps, _, width = weight.shape

    def one(t, carry):
        at = pl.multiple_of(t * width, 16)
        out[pl.ds(at, width), :] = weight[taps - 1 - t].T
        return carry

    lax.fori_loop(0, taps, one, 0)


def aim(place, targets, goal, full):
    core = place[0]
    chunk = goal.shape[0]
    for n, (i, j) in enumerate(pairs(targets.shape[1])):
        rows, cols = slice(i * BLOCK, (i + 1) * BLOCK), slice(j * BLOCK, (j + 1) * BLOCK)
        block = (targets[core, rows, cols] + targets[core, cols, rows].T) * 0.5
        full[n * BLOCK : (n + 1) * BLOCK, :] = block
    goal[...] = full[pl.ds(pl.multiple_of(place[3] * chunk, 16), chunk), :]


def call(body, ins, outs, scratch, flops=0, limit=None, far=()):
    ins = [
        pltpu.with_memory_space_constraint(x, pltpu.HBM) if n in far else x
        for n, x in enumerate(ins)
    ]
    moved = sum(x.size * x.dtype.itemsize for x in ins) + sum(
        x.size * x.dtype.itemsize for x in outs
    )
    return pl.pallas_call(
        body,
        out_shape=tuple(outs),
        in_specs=[
            HBM if n in far else SMEM if x.dtype == jnp.int32 else VMEM for n, x in enumerate(ins)
        ],
        out_specs=tuple(VMEM for _ in outs),
        scratch_shapes=scratch,
        compiler_params=pltpu.CompilerParams(vmem_limit_bytes=(limit or 8) * MIB),
        cost_estimate=pl.CostEstimate(flops=flops, bytes_accessed=moved, transcendentals=0),
    )(*ins)


def shape(dims, dtype):
    return jax.ShapeDtypeStruct(dims, dtype)


def local(pool_input, weight_first, weight_second, targets):
    height, breadth, depth = pool_input.shape
    width = weight_first.shape[3]
    groups, tiles = lax.axis_size("grp"), lax.axis_size("tile")
    chips = tiles // 2
    row, tile = lax.axis_index("grp"), lax.axis_index("tile")
    core = tile % 2
    cells = height * breadth
    positions = cells * groups * tiles
    fold = -(-(breadth + 2 * REACH) // 16)
    pitch, wider = fold * 16, (fold + 2) * 16
    blocks = width // BLOCK
    place = jnp.stack([core, row * height, tile * breadth, row]).astype(jnp.int32)
    dims = (height, breadth, fold, (height * groups, breadth * tiles))
    swap = [(i, i ^ 1) for i in range(tiles)]
    cross = [(i, i + 1) for i in range(1, tiles - 1, 2)]
    cross = cross + [(j, i) for i, j in cross]

    rim = shape((height, REACH, depth), BF)
    far, near = call(
        edges,
        [place, pool_input],
        [rim] * 2,
        [pltpu.VMEM((2, height, 8, depth), F32), pltpu.SemaphoreType.DMA((2,))],
        flops=4 * 10**9,
        far=(1,),
    )
    far = lax.ppermute(far, "tile", cross)
    near = lax.ppermute(near, "tile", swap)
    band = shape((REACH, breadth + 2 * REACH, depth), BF)
    even, odd = call(
        bands,
        [place, pool_input, far, near],
        [band] * 2,
        [pltpu.VMEM((breadth + 2 * REACH, depth), F32)],
        flops=6 * 10**9,
    )

    def couples(start):
        ways = [(i, i + 1) for i in range(start, groups - 1, 2)]
        return ways + [(j, i) for i, j in ways]

    even = lax.ppermute(even, "grp", couples(0))
    odd = lax.ppermute(odd, "grp", couples(1))

    packed = len(pairs(width)) * BLOCK
    w1 = weight_first.reshape(-1, width)
    w2 = weight_second.reshape(-1, width)
    space = (fold * 15 + fold + 2 + 7) // 8 * 8

    def maps(rows):
        return [shape((rows * pitch, width), F32)] * 2

    def cost(rows_first, rows_second):
        return 2 * 9 * width * pitch * (rows_first * depth + rows_second * width)

    taps1, taps2, act1, slope1, act2, slope2 = call(
        functools.partial(middle, dims),
        [place, pool_input, far, near, w1, w2],
        [shape((height * wider, depth), BF), shape(((height - 2) * wider, width), BF)]
        + maps(height - 2)
        + maps(height - 4),
        [pltpu.VMEM((depth // BLOCK, height * space, BLOCK), F32)],
        flops=cost(height - 2, height - 4),
        limit=24,
    )
    taps2b, act1b, slope1b, act2b, slope2b, keep, mine, sent = call(
        functools.partial(front, dims),
        [place, even, odd, taps1, taps2, act1, act2, w1, w2],
        [shape((4 * wider, width), BF)]
        + maps(4)
        + maps(4)
        + [
            shape((packed, BLOCK), F32),
            shape((8, BLOCK), F32),
            shape((packed + EXTRA, BLOCK), BF),
        ],
        [
            pltpu.VMEM((4 * wider, depth), BF),
            pltpu.VMEM((depth // BLOCK, 4 * space, BLOCK), F32),
            pltpu.VMEM((2, height * pitch, width), BF),
            pltpu.VMEM((2, 2 * EXTRA, BLOCK), F32),
        ],
        flops=cost(4, 4),
        limit=24,
    )
    act2r, slope2r = call(
        functools.partial(ring, dims),
        [place, even, odd, taps2b, w1, w2],
        maps(4),
        [
            pltpu.VMEM((4 * wider, depth), BF),
            pltpu.VMEM((4 * wider, width), BF),
            pltpu.VMEM((depth // BLOCK, 4 * space, BLOCK), F32),
        ],
        flops=cost(4, 4),
        limit=16,
    )
    chunk = packed // groups
    (goal,) = call(
        aim,
        [place, targets],
        [shape((chunk, BLOCK), F32)],
        [pltpu.VMEM((packed, BLOCK), F32)],
        flops=2 * 10**8,
    )

    def turned(weight, inner):
        (out,) = call(
            flip,
            [weight.reshape(9, inner, width)],
            [shape((9 * width, inner), BF)],
            [],
            flops=2 * 10**9,
            limit=16,
        )
        return out

    back2 = turned(w2, width)
    back1 = turned(w1, depth)

    def helpers(members):
        deep = -(-3 * members // 16) * 16
        return [
            pltpu.VMEM((packed, BLOCK), F32),
            pltpu.VMEM((deep, width), F32),
            pltpu.VMEM((deep, width), F32),
            pltpu.VMEM((EXTRA, BLOCK), F32),
        ]

    message = shape((chunk + EXTRA, BLOCK), BF)
    part, centre = shape((chunk, BLOCK), F32), shape((8, BLOCK), F32)
    got = lax.ppermute(sent, "tile", swap)
    share, mean, *sents = call(
        functools.partial(merge_pair, (cells, groups, blocks)),
        [place, keep, mine, got],
        [part, centre] + [message] * (groups - 1),
        helpers(2),
    )
    gots = [
        lax.ppermute(sents[k - 1], "grp", [(i, i ^ k) for i in range(groups)])
        for k in range(1, groups)
    ]
    share, mean, sent = call(
        functools.partial(merge_many, (2 * cells, groups, blocks), None),
        [place, share, mean] + gots,
        [part, centre, message],
        helpers(groups),
    )
    gots = [
        lax.ppermute(sent, "tile", [(i, i ^ (2 * k)) for i in range(tiles)])
        for k in range(1, chips)
    ]
    share, mean = call(
        functools.partial(merge_many, (2 * groups * cells, chips, blocks), positions),
        [place, share, mean] + gots + [goal],
        [shape((chunk, BLOCK), BF), shape((EXTRA, BLOCK), BF)],
        helpers(chips),
    )
    gots = [
        lax.ppermute(share, "grp", [(i, i ^ k) for i in range(groups)])
        for k in range(1, groups)
    ]
    table = shape((packed + EXTRA, BLOCK), BF)
    (mine,) = call(assemble, [place, share, mean] + gots, [table], [])
    other = lax.ppermute(mine, "tile", swap)
    maps_in = [act1, slope1, act1b, slope1b, act2, slope2, act2b, slope2b, act2r, slope2r]
    (out,) = call(
        functools.partial(back, dims),
        [place] + maps_in + [mine, other, back2, back1],
        [shape(pool_input.shape, F32)],
        [
            pltpu.VMEM(((height + 4) * wider, width), BF),
            pltpu.VMEM(((height + 2) * wider, width), BF),
            pltpu.VMEM((width, width), BF),
            pltpu.VMEM((width, width), BF),
            pltpu.VMEM((2, packed + EXTRA, BLOCK), BF),
            pltpu.VMEM((depth // BLOCK, height * pitch, BLOCK), F32),
        ],
        flops=2 * 9 * width * pitch * ((height + 2) * width + height * depth),
        limit=32,
    )
    return out


def solution(mesh):
    return jax.shard_map(
        local,
        mesh=mesh,
        in_specs=(P("grp", "tile", None), P(), P(), P()),
        out_specs=P("grp", "tile", None),
        check_vma=False,
    )
```

```python
import functools

import jax
import jax.numpy as jnp
from jax import lax
from jax.experimental import pallas as pl
from jax.experimental.pallas import tpu as pltpu
from jax.sharding import PartitionSpec as P


GELU_SCALE = 0.7978845608
GELU_CUBIC = 0.044715
REACH = 4
BLOCK = 128
EXTRA = 16
BF = jnp.bfloat16
F32 = jnp.float32
VMEM = pl.BlockSpec(memory_space=pltpu.VMEM)
HBM = pl.BlockSpec(memory_space=pltpu.HBM)
MIB = 2**20


def gelu_pair(values):
    square = values * values
    hyper = jnp.tanh(GELU_SCALE * (values + GELU_CUBIC * values * square))
    half = 0.5 * (1.0 + hyper)
    slope = half + 0.5 * values * (1.0 - hyper * hyper) * (
        GELU_SCALE + 3.0 * GELU_SCALE * GELU_CUBIC * square
    )
    return values * half, slope


def pairs(width):
    blocks = width // BLOCK
    return [(i, j) for i in range(blocks) for j in range(i, blocks)]


def wide(mask, width):
    return jnp.concatenate([mask] * (width // BLOCK), axis=1)


def columns(groups):
    n = lax.broadcasted_iota(jnp.int32, (groups * 16, BLOCK), 0)
    return (n & 15) * groups + (n >> 4)


def span(groups, low, high):
    col = columns(groups)
    return jnp.where((col >= low) & (col < high), 1.0, 0.0).astype(F32)


def pair_mask(inside, place, limits, row):
    parts = []
    for r in range(2):
        at = place[1] + row + r
        parts.append(inside * jnp.where((at >= 0) & (at < limits[0]), 1.0, 0.0).astype(F32))
    return jnp.concatenate(parts, axis=0)


def roll_group(value):
    return [pltpu.roll(value[n * 16 : (n + 1) * 16], 15, 0) for n in range(2)]


def write_taps(ref, row, value, groups, lanes=slice(None)):
    at, pitch = row * (groups + 2) * 16, groups * 16
    ref[at : at + pitch, lanes] = value.astype(BF)
    for n, block in enumerate(roll_group(value)):
        ref[at + pitch + n * 16 : at + pitch + (n + 1) * 16, lanes] = block.astype(BF)


def fold_row(ref, row, buf_ref, at, groups):
    base = row * (groups + 2) * 16
    for n in range(groups + 2):
        for p in range(buf_ref.shape[0]):
            ref[base + n * 16 : base + (n + 1) * 16, p * BLOCK : (p + 1) * BLOCK] = buf_ref[
                p, pl.ds(at + n, 16, stride=groups), :
            ].astype(BF)


def put_row(buf_ref, at, value):
    for p in range(buf_ref.shape[0]):
        buf_ref[p, at : at + value.shape[0], :] = value[:, p * BLOCK : (p + 1) * BLOCK]


def clear_rows(buf_ref, start, stop):
    for p in range(buf_ref.shape[0]):
        buf_ref[p, start:stop, :] = jnp.zeros((stop - start, BLOCK), F32)


def conv(find, weight_ref, groups, lanes):
    pitch, pieces = groups * 16, []
    for a in range(3):
        for b in range(3):
            both = []
            for r in range(2):
                ref, row = find(r + a)
                at = (row * (groups + 2) + b) * 16
                both.append(ref[at : at + pitch, :])
            pieces.append(jnp.concatenate(both, axis=0))
    lhs = jnp.concatenate(pieces, axis=1)
    return jnp.dot(lhs, weight_ref[:, lanes], preferred_element_type=F32)


def halves(width):
    half = 2 * BLOCK
    return [slice(n, n + half) for n in range(0, width, half)]


def first_rows(find, w1, taps_ref, row, act, slope, at, groups, mask):
    width, pitch = w1.shape[1], groups * 16
    for lanes in halves(width):
        value, tilt = gelu_pair(conv(find, w1, groups, lanes))
        value = value * wide(mask, 2 * BLOCK)
        for r in range(2):
            one = value[r * pitch : (r + 1) * pitch]
            write_taps(taps_ref, row + r, one, groups, lanes)
            if act is None:
                continue
            two = tilt[r * pitch : (r + 1) * pitch]
            base = at + r * pitch
            for ref, part in ((act, one), (slope, two)):
                ref[base : base + pitch - 32, lanes] = part[32:]
                for n, block in enumerate(roll_group(part)):
                    to = base + pitch - 32 + n * 16
                    ref[to : to + 16, lanes] = block


def second_rows(find, w2, act, slope, at, groups):
    step = groups * 32
    for lanes in halves(w2.shape[1]):
        value, tilt = gelu_pair(conv(find, w2, groups, lanes))
        act[at : at + step, lanes] = value
        slope[at : at + step, lanes] = tilt


def put_mean(rows_ref, mean, parts):
    blocks = mean.shape[1] // BLOCK
    high = mean.astype(BF).astype(F32)
    for p, row in enumerate((high, mean - high) if parts == 2 else (mean,)):
        for j in range(blocks):
            at = p * blocks + j
            rows_ref[at : at + 1, :] = row[:, j * BLOCK : (j + 1) * BLOCK]


def get_mean(rows, blocks, parts):
    rows = rows.astype(F32)
    found = rows[:blocks] + rows[blocks : 2 * blocks] if parts == 2 else rows[:blocks]
    return jnp.concatenate([found[j : j + 1] for j in range(blocks)], axis=1)


def panels(lhs, rhs, emit):
    width, n = lhs.shape[1], 0
    for i in range(0, width, BLOCK):
        panel = lax.dot_general(
            lhs[:, i : i + BLOCK],
            rhs[:, i:],
            (((0,), (0,)), ((), ())),
            preferred_element_type=F32,
        )
        for j in range(0, width - i, BLOCK):
            emit(n, panel[:, j : j + BLOCK])
            n += 1


def spread(means, count, left_ref, right_ref, emit):
    centre = means[0]
    for mean in means[1:]:
        centre = centre + mean
    centre = centre * (1.0 / len(means))
    left_ref[...] = jnp.zeros(left_ref.shape, F32)
    right_ref[...] = jnp.zeros(right_ref.shape, F32)
    for n, mean in enumerate(means):
        away = mean - centre
        high = away.astype(BF).astype(F32)
        low = away - high
        for q, (lhs, rhs) in enumerate(((high, high), (high, low), (low, high))):
            at = 3 * n + q
            left_ref[at : at + 1, :] = lhs
            right_ref[at : at + 1, :] = rhs
    lhs, rhs = left_ref[...].astype(BF), right_ref[...].astype(BF)
    panels(lhs, rhs, lambda n, block: emit(n, block * float(count)))
    return centre


def middle(dims, place, pool, far, near, w1, w2, *rest):
    taps1, taps2, act1, slope1, act2, slope2, buf = rest
    height, breadth, groups, limits = dims
    pitch = groups * 16
    left_core = place[0] == 0
    space = buf.shape[1] // height
    for r in range(height):
        at = r * space
        one, two = far[r].astype(F32), near[r].astype(F32)
        put_row(buf, at, jnp.where(left_core, one, two))
        put_row(buf, at + REACH, pool[r])
        put_row(buf, at + REACH + breadth, jnp.where(left_core, two, one))
        clear_rows(buf, at + 2 * REACH + breadth, at + space)
        fold_row(taps1, r, buf, at, groups)
    low = 3 - place[2]
    inside = span(groups, low, low + limits[1])
    for t in range(0, height - 2, 2):
        mask = pair_mask(inside, place, limits, t + 1)
        first_rows(
            lambda r: (taps1, t + r), w1, taps2, t, act1, slope1, t * pitch, groups, mask
        )
        if t >= 2:
            second_rows(
                lambda r: (taps2, t - 2 + r), w2, act2, slope2, (t - 2) * pitch, groups
            )


def rim_taps(ref, rows, place, buf, groups):
    space = buf.shape[1] // len(rows)
    even = (place[3] & 1) == 0
    for n, (one, two, r) in enumerate(rows):
        breadth = one.shape[1]
        at = n * space
        put_row(buf, at, jnp.where(even, one[r].astype(F32), two[r].astype(F32)))
        clear_rows(buf, at + breadth, at + space)
        fold_row(ref, n, buf, at, groups)


def front(dims, place, even, odd, taps1, taps2, act1, act2, w1, w2, *rest):
    (taps2b, act1b, slope1b, act2b, slope2b, keep, mine, sent) = rest[:8]
    (rim, buf, centred, stat) = rest[8:]
    height, breadth, groups, limits = dims
    pitch = groups * 16
    width = w1.shape[1]
    rows = [(odd, even, REACH - 2), (odd, even, REACH - 1), (even, odd, 0), (even, odd, 1)]
    rim_taps(rim, rows, place, buf, groups)
    low = 3 - place[2]
    inside = span(groups, low, low + limits[1])
    last = height - 2
    finds = (
        lambda r: (rim, r) if r < 2 else (taps1, r - 2),
        lambda r: (taps1, last + r) if r < 2 else (rim, r),
    )
    for n, row in enumerate((-1, height - 1)):
        mask = pair_mask(inside, place, limits, row)
        first_rows(
            finds[n], w1, taps2b, 2 * n, act1b, slope1b, 2 * n * pitch, groups, mask
        )
    last = height - 4
    finds = (
        lambda r: (taps2b, r) if r < 2 else (taps2, r - 2),
        lambda r: (taps2, last + r) if r < 2 else (taps2b, r),
    )
    for n in range(2):
        second_rows(finds[n], w2, act2b, slope2b, 2 * n * pitch, groups)
    cells = height * breadth
    first_parts = [(act1b, pitch, 2 * pitch), (act1, 0, (height - 2) * pitch)]
    second_parts = [(act2b, 0, 4 * pitch), (act2, 0, (height - 4) * pitch)]
    for layer, (parts, offset) in enumerate(((first_parts, 1), (second_parts, 2))):
        own = wide(span(groups, offset, offset + breadth), width)
        total = jnp.zeros((pitch, width), F32)
        for ref, start, count in parts:
            for at in range(start, start + count, pitch):
                total = total + ref[at : at + pitch, :]
        mean = jnp.sum(total * own, axis=0, keepdims=True) * (1.0 / cells)
        n = 0
        for ref, start, count in parts:
            for at in range(start, start + count, pitch):
                centred[layer, n : n + pitch, :] = ((ref[at : at + pitch, :] - mean) * own).astype(
                    BF
                )
                n += pitch
        stat[layer] = jnp.zeros(stat.shape[1:], F32)
        put_mean(stat.at[layer, 0:EXTRA], mean, 2)
        put_mean(stat.at[layer, EXTRA : 2 * EXTRA], mean, 1)
    rows = keep.shape[0]

    def give(n, block):
        sent[n * BLOCK : (n + 1) * BLOCK, :] = block.astype(BF)

    def hold(n, block):
        keep[n * BLOCK : (n + 1) * BLOCK, :] = block

    for layer, emit in ((1 - place[0], give), (place[0], hold)):
        panels(centred[layer], centred[layer], emit)
    mine[...] = stat[place[0], EXTRA : EXTRA + 8, :]
    sent[rows:, :] = stat[1 - place[0], 0:EXTRA, :].astype(BF)


def ring(dims, place, even, odd, taps2b, w1, w2, act2, slope2, rim, outer, buf):
    height, _, groups, limits = dims
    low = 3 - place[2]
    inside = span(groups, low, low + limits[1])
    finds = (
        lambda r: (outer, r) if r < 2 else (taps2b, r - 2),
        lambda r: (taps2b, 2 + r) if r < 2 else (outer, r),
    )
    for n, (one, two, row) in enumerate(((odd, even, -3), (even, odd, height + 1))):
        rim_taps(rim, [(one, two, r) for r in range(REACH)], place, buf, groups)
        mask = pair_mask(inside, place, limits, row)
        first_rows(lambda r: (rim, r), w1, outer, 2 * n, None, None, 0, groups, mask)
        second_rows(finds[n], w2, act2, slope2, 2 * n * groups * 16, groups)


def write_message(ref, part, rows_ref, centre):
    count = part.shape[0]
    rows_ref[...] = jnp.zeros(rows_ref.shape, F32)
    put_mean(rows_ref, centre, 2)
    ref[0:count, :] = part.astype(BF)
    ref[count:, :] = rows_ref[...].astype(BF)


def merge_pair(dims, place, keep, mine, got, share, centre_out, *rest):
    count, groups, blocks = dims
    messages, (full, left, right, rows_ref) = rest[: groups - 1], rest[groups - 1 :]
    rows = keep.shape[0]
    chunk = rows // groups

    def emit(n, product):
        at = slice(n * BLOCK, (n + 1) * BLOCK)
        full[at, :] = keep[at, :] + got[at, :].astype(F32) + product

    means = [get_mean(mine[...], blocks, 1), get_mean(got[rows:, :], blocks, 2)]
    centre = spread(means, count, left, right, emit)
    centre_out[...] = jnp.zeros(centre_out.shape, F32)
    put_mean(centre_out, centre, 1)
    for k, ref in enumerate(messages, 1):
        at = pl.multiple_of((place[3] ^ k) * chunk, 16)
        write_message(ref, full[pl.ds(at, chunk), :], rows_ref, centre)
    share[...] = full[pl.ds(pl.multiple_of(place[3] * chunk, 16), chunk), :]


def merge_many(dims, final, place, share, mine, *rest):
    count, members, blocks = dims
    gots, rest = rest[: members - 1], rest[members - 1 :]
    chunk = share.shape[0]
    full, left, right, rows_ref = rest[-4:]

    def emit(n, product):
        full[n * BLOCK : (n + 1) * BLOCK, :] = product

    means = [get_mean(mine[...], blocks, 1)]
    means += [get_mean(got[chunk:, :], blocks, 2) for got in gots]
    centre = spread(means, count, left, right, emit)
    total = share[...] + full[pl.ds(pl.multiple_of(place[3] * chunk, 16), chunk), :]
    for got in gots:
        total = total + got[0:chunk, :].astype(F32)
    if final is None:
        out, centre_out, sent = rest[:3]
        out[...] = total
        centre_out[...] = jnp.zeros(centre_out.shape, F32)
        put_mean(centre_out, centre, 1)
        write_message(sent, total, rows_ref, centre)
    else:
        goal, sent, centre_out = rest[:3]
        rows_ref[...] = jnp.zeros(rows_ref.shape, F32)
        put_mean(rows_ref, centre, 2)
        centre_out[...] = rows_ref[...].astype(BF)
        sent[...] = (total * (1.0 / final) - goal[...]).astype(BF)


def assemble(place, share, centre, *rest):
    gots, out = rest[:-1], rest[-1]
    chunk = share.shape[0]
    for k, ref in enumerate((share,) + tuple(gots)):
        out[pl.ds(pl.multiple_of((place[3] ^ k) * chunk, 16), chunk), :] = ref[...]
    rows = chunk * (len(gots) + 1)
    out[rows:, :] = centre[...]


def back(dims, place, *rest):
    (act1, slope1, act1b, slope1b, act2, slope2, act2b, slope2b, act2r, slope2r) = rest[:10]
    (mine, other, w2, w1, out, taps2, taps1, first_m, second_m, table, buf) = rest[10:]
    height, breadth, groups, limits = dims
    pitch = groups * 16
    step = 2 * pitch
    width = act1.shape[1]
    blocks = width // BLOCK
    packed = table.shape[1] - EXTRA
    table[place[0]] = mine[...]
    table[1 - place[0]] = other[...]
    means = []
    for layer, ref in enumerate((first_m, second_m)):
        for n, (i, j) in enumerate(pairs(width)):
            block = table[layer, n * BLOCK : (n + 1) * BLOCK, :]
            ref[i * BLOCK : (i + 1) * BLOCK, j * BLOCK : (j + 1) * BLOCK] = block
            if i != j:
                ref[j * BLOCK : (j + 1) * BLOCK, i * BLOCK : (i + 1) * BLOCK] = block.T
        means.append(get_mean(table[layer, packed:, :], blocks, 2))
    low = 2 - place[2]
    inside2 = span(groups, low, low + limits[1])
    tiles2 = [(act2r, slope2r, 0), (act2b, slope2b, 0)]
    tiles2 += [(act2, slope2, t * pitch) for t in range(0, height - 4, 2)]
    tiles2 += [(act2b, slope2b, step), (act2r, slope2r, step)]

    def second(t):
        act, slope, at = tiles2[t]
        centred = (act[at : at + step, :] - means[1]).astype(BF)
        mask = wide(pair_mask(inside2, place, limits, 2 * t - 2), 2 * BLOCK)
        for lanes in halves(width):
            push = jnp.dot(centred, second_m[:, lanes], preferred_element_type=F32)
            grad = push * slope[at : at + step, lanes] * mask
            for r in range(2):
                write_taps(taps2, 2 * t + r, grad[r * pitch : (r + 1) * pitch], groups, lanes)

    low = 1 - place[2]
    inside1 = span(groups, low, low + limits[1])
    tiles1 = [(act1b, slope1b, 0)]
    tiles1 += [(act1, slope1, t * pitch) for t in range(0, height - 2, 2)]
    tiles1 += [(act1b, slope1b, step)]

    def first(t):
        act, slope, at = tiles1[t]
        centred = (act[at : at + step, :] - means[0]).astype(BF)
        mask = wide(pair_mask(inside1, place, limits, 2 * t - 1), 2 * BLOCK)
        for lanes in halves(width):
            flow = conv(lambda r: (taps2, 2 * t + r), w2, groups, lanes) + jnp.dot(
                centred, first_m[:, lanes], preferred_element_type=F32
            )
            grad = flow * slope[at : at + step, lanes] * mask
            for r in range(2):
                write_taps(taps1, 2 * t + r, grad[r * pitch : (r + 1) * pitch], groups, lanes)

    def last(t):
        got = conv(lambda r: (taps1, 2 * t + r), w1, groups, slice(None))
        for r in range(2):
            at = (2 * t + r) * pitch
            for p in range(buf.shape[0]):
                lanes = slice(p * BLOCK, (p + 1) * BLOCK)
                for n in range(groups):
                    part = got[r * pitch + n * 16 : r * pitch + (n + 1) * 16, lanes]
                    buf[p, pl.ds(at + n, 16, stride=groups), :] = part
                out[2 * t + r, :, lanes] = buf[p, at : at + breadth, :]

    for t in range(len(tiles2)):
        second(t)
    for t in range(len(tiles1)):
        first(t)
    for t in range(height // 2):
        last(t)


def edges(place, pool_hbm, far, near, strips, sems):
    breadth = pool_hbm.shape[1]
    ends = (0, breadth - 8)
    loads = [
        pltpu.make_async_copy(pool_hbm.at[:, pl.ds(at, 8), :], strips.at[n], sems.at[n])
        for n, at in enumerate(ends)
    ]
    for load in loads:
        load.start()
    for load in loads:
        load.wait()
    left_core = place[0] == 0
    left, right = strips[0, :, 0:REACH, :], strips[1, :, 8 - REACH :, :]
    far[...] = jnp.where(left_core, left, right).astype(BF)
    near[...] = jnp.where(left_core, right, left).astype(BF)


def bands(place, pool, far, near, even, odd, row):
    height, breadth, _ = pool.shape
    left_core = place[0] == 0
    odd_row = place[3] & 1
    for start, ref in ((1 - odd_row, even), (odd_row, odd)):
        for r in range(REACH):
            at = start * (height - REACH) + r
            one, two = far[at].astype(F32), near[at].astype(F32)
            row[0:REACH, :] = jnp.where(left_core, one, two)
            row[REACH : REACH + breadth, :] = pool[at]
            row[REACH + breadth :, :] = jnp.where(left_core, two, one)
            ref[r] = row[...].astype(BF)


def flip(weight, out):
    taps, _, width = weight.shape

    def one(t, carry):
        at = pl.multiple_of(t * width, 16)
        out[pl.ds(at, width), :] = weight[taps - 1 - t].T
        return carry

    lax.fori_loop(0, taps, one, 0)


def aim(place, targets, goal, full):
    core = place[0]
    chunk = goal.shape[0]
    for n, (i, j) in enumerate(pairs(targets.shape[1])):
        rows, cols = slice(i * BLOCK, (i + 1) * BLOCK), slice(j * BLOCK, (j + 1) * BLOCK)
        block = (targets[core, rows, cols] + targets[core, cols, rows].T) * 0.5
        full[n * BLOCK : (n + 1) * BLOCK, :] = block
    goal[...] = full[pl.ds(pl.multiple_of(place[3] * chunk, 16), chunk), :]


def locate(height, breadth):
    row, tile = lax.axis_index("grp"), lax.axis_index("tile")
    return tile & 1, row * height, tile * breadth, row


def call(body, ins, outs, scratch, flops=0, limit=None, far=()):
    if isinstance(ins[0], tuple):
        (height, breadth), inner, ins = ins[0], body, ins[1:]

        def body(*refs):
            inner(locate(height, breadth), *refs)

    ins = [
        pltpu.with_memory_space_constraint(x, pltpu.HBM) if n in far else x
        for n, x in enumerate(ins)
    ]
    moved = sum(x.size * x.dtype.itemsize for x in ins) + sum(
        x.size * x.dtype.itemsize for x in outs
    )
    return pl.pallas_call(
        body,
        out_shape=tuple(outs),
        in_specs=[HBM if n in far else VMEM for n in range(len(ins))],
        out_specs=tuple(VMEM for _ in outs),
        scratch_shapes=scratch,
        compiler_params=pltpu.CompilerParams(vmem_limit_bytes=(limit or 8) * MIB),
        cost_estimate=pl.CostEstimate(flops=flops, bytes_accessed=moved, transcendentals=0),
    )(*ins)


def shape(dims, dtype):
    return jax.ShapeDtypeStruct(dims, dtype)


def local(pool_input, weight_first, weight_second, targets):
    height, breadth, depth = pool_input.shape
    width = weight_first.shape[3]
    groups, tiles = lax.axis_size("grp"), lax.axis_size("tile")
    chips = tiles // 2
    cells = height * breadth
    positions = cells * groups * tiles
    fold = -(-(breadth + 2 * REACH) // 16)
    pitch, wider = fold * 16, (fold + 2) * 16
    blocks = width // BLOCK
    place = (height, breadth)
    dims = (height, breadth, fold, (height * groups, breadth * tiles))
    swap = [(i, i ^ 1) for i in range(tiles)]
    cross = [(i, i + 1) for i in range(1, tiles - 1, 2)]
    cross = cross + [(j, i) for i, j in cross]

    rim = shape((height, REACH, depth), BF)
    far, near = call(
        edges,
        [place, pool_input],
        [rim] * 2,
        [pltpu.VMEM((2, height, 8, depth), F32), pltpu.SemaphoreType.DMA((2,))],
        flops=4 * 10**9,
        far=(0,),
    )
    far = lax.ppermute(far, "tile", cross)
    near = lax.ppermute(near, "tile", swap)
    band = shape((REACH, breadth + 2 * REACH, depth), BF)
    even, odd = call(
        bands,
        [place, pool_input, far, near],
        [band] * 2,
        [pltpu.VMEM((breadth + 2 * REACH, depth), F32)],
        flops=6 * 10**9,
    )

    def couples(start):
        ways = [(i, i + 1) for i in range(start, groups - 1, 2)]
        return ways + [(j, i) for i, j in ways]

    even = lax.ppermute(even, "grp", couples(0))
    odd = lax.ppermute(odd, "grp", couples(1))

    packed = len(pairs(width)) * BLOCK
    w1 = weight_first.reshape(-1, width)
    w2 = weight_second.reshape(-1, width)
    space = (fold * 15 + fold + 2 + 7) // 8 * 8

    def maps(rows):
        return [shape((rows * pitch, width), F32)] * 2

    def cost(rows_first, rows_second):
        return 2 * 9 * width * pitch * (rows_first * depth + rows_second * width)

    taps1, taps2, act1, slope1, act2, slope2 = call(
        functools.partial(middle, dims),
        [place, pool_input, far, near, w1, w2],
        [shape((height * wider, depth), BF), shape(((height - 2) * wider, width), BF)]
        + maps(height - 2)
        + maps(height - 4),
        [pltpu.VMEM((depth // BLOCK, height * space, BLOCK), F32)],
        flops=cost(height - 2, height - 4),
        limit=24,
    )
    taps2b, act1b, slope1b, act2b, slope2b, keep, mine, sent = call(
        functools.partial(front, dims),
        [place, even, odd, taps1, taps2, act1, act2, w1, w2],
        [shape((4 * wider, width), BF)]
        + maps(4)
        + maps(4)
        + [
            shape((packed, BLOCK), F32),
            shape((8, BLOCK), F32),
            shape((packed + EXTRA, BLOCK), BF),
        ],
        [
            pltpu.VMEM((4 * wider, depth), BF),
            pltpu.VMEM((depth // BLOCK, 4 * space, BLOCK), F32),
            pltpu.VMEM((2, height * pitch, width), BF),
            pltpu.VMEM((2, 2 * EXTRA, BLOCK), F32),
        ],
        flops=cost(4, 4),
        limit=24,
    )
    act2r, slope2r = call(
        functools.partial(ring, dims),
        [place, even, odd, taps2b, w1, w2],
        maps(4),
        [
            pltpu.VMEM((4 * wider, depth), BF),
            pltpu.VMEM((4 * wider, width), BF),
            pltpu.VMEM((depth // BLOCK, 4 * space, BLOCK), F32),
        ],
        flops=cost(4, 4),
        limit=16,
    )
    chunk = packed // groups
    (goal,) = call(
        aim,
        [place, targets],
        [shape((chunk, BLOCK), F32)],
        [pltpu.VMEM((packed, BLOCK), F32)],
        flops=2 * 10**8,
    )

    def turned(weight, inner):
        (out,) = call(
            flip,
            [weight.reshape(9, inner, width)],
            [shape((9 * width, inner), BF)],
            [],
            flops=2 * 10**9,
            limit=16,
        )
        return out

    back2 = turned(w2, width)
    back1 = turned(w1, depth)

    def helpers(members):
        deep = -(-3 * members // 16) * 16
        return [
            pltpu.VMEM((packed, BLOCK), F32),
            pltpu.VMEM((deep, width), F32),
            pltpu.VMEM((deep, width), F32),
            pltpu.VMEM((EXTRA, BLOCK), F32),
        ]

    message = shape((chunk + EXTRA, BLOCK), BF)
    part, centre = shape((chunk, BLOCK), F32), shape((8, BLOCK), F32)
    got = lax.ppermute(sent, "tile", swap)
    share, mean, *sents = call(
        functools.partial(merge_pair, (cells, groups, blocks)),
        [place, keep, mine, got],
        [part, centre] + [message] * (groups - 1),
        helpers(2),
    )
    gots = [
        lax.ppermute(sents[k - 1], "grp", [(i, i ^ k) for i in range(groups)])
        for k in range(1, groups)
    ]
    share, mean, sent = call(
        functools.partial(merge_many, (2 * cells, groups, blocks), None),
        [place, share, mean] + gots,
        [part, centre, message],
        helpers(groups),
    )
    gots = [
        lax.ppermute(sent, "tile", [(i, i ^ (2 * k)) for i in range(tiles)])
        for k in range(1, chips)
    ]
    share, mean = call(
        functools.partial(merge_many, (2 * groups * cells, chips, blocks), positions),
        [place, share, mean] + gots + [goal],
        [shape((chunk, BLOCK), BF), shape((EXTRA, BLOCK), BF)],
        helpers(chips),
    )
    gots = [
        lax.ppermute(share, "grp", [(i, i ^ k) for i in range(groups)])
        for k in range(1, groups)
    ]
    table = shape((packed + EXTRA, BLOCK), BF)
    (mine,) = call(assemble, [place, share, mean] + gots, [table], [])
    other = lax.ppermute(mine, "tile", swap)
    maps_in = [act1, slope1, act1b, slope1b, act2, slope2, act2b, slope2b, act2r, slope2r]
    (out,) = call(
        functools.partial(back, dims),
        [place] + maps_in + [mine, other, back2, back1],
        [shape(pool_input.shape, F32)],
        [
            pltpu.VMEM(((height + 4) * wider, width), BF),
            pltpu.VMEM(((height + 2) * wider, width), BF),
            pltpu.VMEM((width, width), BF),
            pltpu.VMEM((width, width), BF),
            pltpu.VMEM((2, packed + EXTRA, BLOCK), BF),
            pltpu.VMEM((depth // BLOCK, height * pitch, BLOCK), F32),
        ],
        flops=2 * 9 * width * pitch * ((height + 2) * width + height * depth),
        limit=32,
    )
    return out


def solution(mesh):
    return jax.shard_map(
        local,
        mesh=mesh,
        in_specs=(P("grp", "tile", None), P(), P(), P()),
        out_specs=P("grp", "tile", None),
        check_vma=False,
    )
```

```python
import functools

import jax
import jax.numpy as jnp
from jax import lax
from jax.experimental import pallas as pl
from jax.experimental.pallas import tpu as pltpu
from jax.sharding import PartitionSpec as P


GELU_SCALE = 0.7978845608
GELU_CUBIC = 0.044715
REACH = 4
BLOCK = 128
EXTRA = 16
BF = jnp.bfloat16
F32 = jnp.float32
VMEM = pl.BlockSpec(memory_space=pltpu.VMEM)
HBM = pl.BlockSpec(memory_space=pltpu.HBM)
MIB = 2**20


def gelu_pair(values):
    square = values * values
    hyper = jnp.tanh(GELU_SCALE * (values + GELU_CUBIC * values * square))
    half = 0.5 * (1.0 + hyper)
    slope = half + 0.5 * values * (1.0 - hyper * hyper) * (
        GELU_SCALE + 3.0 * GELU_SCALE * GELU_CUBIC * square
    )
    return values * half, slope


def pairs(width):
    blocks = width // BLOCK
    return [(i, j) for i in range(blocks) for j in range(i + 1, blocks)]


def packed_rows(width, groups):
    return (len(pairs(width)) + width // BLOCK // 2) * BLOCK + 16 * groups


def corners():
    row = lax.broadcasted_iota(jnp.int32, (BLOCK, BLOCK), 0)
    return row, lax.broadcasted_iota(jnp.int32, (BLOCK, BLOCK), 1)


def packer(width, rows, put):
    places, held, lines = pairs(width), {}, []
    row, col = corners()

    def emit(i, j, block):
        if i != j:
            put(places.index((i, j)) * BLOCK, block)
        elif i % 2 == 0:
            held[i] = block
        else:
            both = jnp.where(row <= col, held[i - 1], block)
            put((len(places) + i // 2) * BLOCK, both)
            lines.append(jnp.sum(jnp.where(row == col, block, 0.0), axis=0, keepdims=True))

    def finish():
        start = (len(places) + len(lines)) * BLOCK
        at = lax.broadcasted_iota(jnp.int32, (rows - start, BLOCK), 0)
        value = jnp.zeros((rows - start, BLOCK), F32)
        for n, line in enumerate(lines):
            value = jnp.where(at == n, line, value)
        put(start, value)

    return emit, finish


def wide(mask, width):
    return jnp.concatenate([mask] * (width // BLOCK), axis=1)


def columns(groups):
    n = lax.broadcasted_iota(jnp.int32, (groups * 16, BLOCK), 0)
    return (n & 15) * groups + (n >> 4)


def span(groups, low, high):
    col = columns(groups)
    return jnp.where((col >= low) & (col < high), 1.0, 0.0).astype(F32)


def pair_mask(inside, place, limits, row):
    parts = []
    for r in range(2):
        at = place[1] + row + r
        parts.append(inside * jnp.where((at >= 0) & (at < limits[0]), 1.0, 0.0).astype(F32))
    return jnp.concatenate(parts, axis=0)


def roll_group(value):
    return [pltpu.roll(value[n * 16 : (n + 1) * 16], 15, 0) for n in range(2)]


def write_taps(ref, row, value, groups, lanes=slice(None)):
    at, pitch = row * (groups + 2) * 16, groups * 16
    ref[at : at + pitch, lanes] = value.astype(BF)
    for n, block in enumerate(roll_group(value)):
        ref[at + pitch + n * 16 : at + pitch + (n + 1) * 16, lanes] = block.astype(BF)


def fold_row(ref, row, buf_ref, at, groups):
    base = row * (groups + 2) * 16
    for n in range(groups + 2):
        for p in range(buf_ref.shape[0]):
            ref[base + n * 16 : base + (n + 1) * 16, p * BLOCK : (p + 1) * BLOCK] = buf_ref[
                p, pl.ds(at + n, 16, stride=groups), :
            ].astype(BF)


def put_row(buf_ref, at, value):
    for p in range(buf_ref.shape[0]):
        buf_ref[p, at : at + value.shape[0], :] = value[:, p * BLOCK : (p + 1) * BLOCK]


def clear_rows(buf_ref, start, stop):
    for p in range(buf_ref.shape[0]):
        buf_ref[p, start:stop, :] = jnp.zeros((stop - start, BLOCK), F32)


def conv(find, weight_ref, groups, lanes):
    pitch, pieces = groups * 16, []
    for a in range(3):
        for b in range(3):
            both = []
            for r in range(2):
                ref, row = find(r + a)
                at = (row * (groups + 2) + b) * 16
                both.append(ref[at : at + pitch, :])
            pieces.append(jnp.concatenate(both, axis=0))
    lhs = jnp.concatenate(pieces, axis=1)
    return jnp.dot(lhs, weight_ref[:, lanes], preferred_element_type=F32)


def halves(width):
    half = 2 * BLOCK
    return [slice(n, n + half) for n in range(0, width, half)]


def first_rows(find, w1, taps_ref, row, act, slope, at, groups, mask):
    width, pitch = w1.shape[1], groups * 16
    for lanes in halves(width):
        value, tilt = gelu_pair(conv(find, w1, groups, lanes))
        value = value * wide(mask, 2 * BLOCK)
        for r in range(2):
            one = value[r * pitch : (r + 1) * pitch]
            write_taps(taps_ref, row + r, one, groups, lanes)
            if act is None:
                continue
            two = tilt[r * pitch : (r + 1) * pitch]
            base = at + r * pitch
            for ref, part in ((act, one), (slope, two)):
                ref[base : base + pitch - 32, lanes] = part[32:]
                for n, block in enumerate(roll_group(part)):
                    to = base + pitch - 32 + n * 16
                    ref[to : to + 16, lanes] = block


def second_rows(find, w2, act, slope, at, groups):
    step = groups * 32
    for lanes in halves(w2.shape[1]):
        value, tilt = gelu_pair(conv(find, w2, groups, lanes))
        act[at : at + step, lanes] = value
        slope[at : at + step, lanes] = tilt


def put_mean(rows_ref, mean, parts):
    blocks = mean.shape[1] // BLOCK
    high = mean.astype(BF).astype(F32)
    for p, row in enumerate((high, mean - high) if parts == 2 else (mean,)):
        for j in range(blocks):
            at = p * blocks + j
            rows_ref[at : at + 1, :] = row[:, j * BLOCK : (j + 1) * BLOCK]


def get_mean(rows, blocks, parts):
    rows = rows.astype(F32)
    found = rows[:blocks] + rows[blocks : 2 * blocks] if parts == 2 else rows[:blocks]
    return jnp.concatenate([found[j : j + 1] for j in range(blocks)], axis=1)


def panels(lhs, rhs, emit):
    width = lhs.shape[1]
    for i in range(0, width, BLOCK):
        panel = lax.dot_general(
            lhs[:, i : i + BLOCK],
            rhs[:, i:],
            (((0,), (0,)), ((), ())),
            preferred_element_type=F32,
        )
        for j in range(0, width - i, BLOCK):
            emit(i // BLOCK, (i + j) // BLOCK, panel[:, j : j + BLOCK])


def spread(means, count, left_ref, right_ref, rows, put):
    centre = means[0]
    for mean in means[1:]:
        centre = centre + mean
    centre = centre * (1.0 / len(means))
    left_ref[...] = jnp.zeros(left_ref.shape, F32)
    right_ref[...] = jnp.zeros(right_ref.shape, F32)
    for n, mean in enumerate(means):
        away = mean - centre
        high = away.astype(BF).astype(F32)
        low = away - high
        for q, (lhs, rhs) in enumerate(((high, high), (high, low), (low, high))):
            at = 3 * n + q
            left_ref[at : at + 1, :] = lhs
            right_ref[at : at + 1, :] = rhs
    lhs, rhs = left_ref[...].astype(BF), right_ref[...].astype(BF)
    emit, finish = packer(lhs.shape[1], rows, lambda at, value: put(at, value * float(count)))
    panels(lhs, rhs, emit)
    finish()
    return centre


def middle(dims, place, pool, far, near, w1, w2, *rest):
    taps1, taps2, act1, slope1, act2, slope2, buf = rest
    height, breadth, groups, limits = dims
    pitch = groups * 16
    left_core = place[0] == 0
    space = buf.shape[1] // height
    for r in range(height):
        at = r * space
        one, two = far[r].astype(F32), near[r].astype(F32)
        put_row(buf, at, jnp.where(left_core, one, two))
        put_row(buf, at + REACH, pool[r])
        put_row(buf, at + REACH + breadth, jnp.where(left_core, two, one))
        clear_rows(buf, at + 2 * REACH + breadth, at + space)
        fold_row(taps1, r, buf, at, groups)
    low = 3 - place[2]
    inside = span(groups, low, low + limits[1])
    for t in range(0, height - 2, 2):
        mask = pair_mask(inside, place, limits, t + 1)
        first_rows(
            lambda r: (taps1, t + r), w1, taps2, t, act1, slope1, t * pitch, groups, mask
        )
        if t >= 2:
            second_rows(
                lambda r: (taps2, t - 2 + r), w2, act2, slope2, (t - 2) * pitch, groups
            )


def rim_taps(ref, rows, place, buf, groups):
    space = buf.shape[1] // len(rows)
    even = (place[3] & 1) == 0
    for n, (one, two, r) in enumerate(rows):
        breadth = one.shape[1]
        at = n * space
        put_row(buf, at, jnp.where(even, one[r].astype(F32), two[r].astype(F32)))
        clear_rows(buf, at + breadth, at + space)
        fold_row(ref, n, buf, at, groups)


def front(dims, place, even, odd, taps1, taps2, act1, act2, w1, w2, *rest):
    (taps2b, act1b, slope1b, act2b, slope2b, keep, mine, sent) = rest[:8]
    (rim, buf, centred, stat) = rest[8:]
    height, breadth, groups, limits = dims
    pitch = groups * 16
    width = w1.shape[1]
    rows = [(odd, even, REACH - 2), (odd, even, REACH - 1), (even, odd, 0), (even, odd, 1)]
    rim_taps(rim, rows, place, buf, groups)
    low = 3 - place[2]
    inside = span(groups, low, low + limits[1])
    last = height - 2
    finds = (
        lambda r: (rim, r) if r < 2 else (taps1, r - 2),
        lambda r: (taps1, last + r) if r < 2 else (rim, r),
    )
    for n, row in enumerate((-1, height - 1)):
        mask = pair_mask(inside, place, limits, row)
        first_rows(
            finds[n], w1, taps2b, 2 * n, act1b, slope1b, 2 * n * pitch, groups, mask
        )
    last = height - 4
    finds = (
        lambda r: (taps2b, r) if r < 2 else (taps2, r - 2),
        lambda r: (taps2, last + r) if r < 2 else (taps2b, r),
    )
    for n in range(2):
        second_rows(finds[n], w2, act2b, slope2b, 2 * n * pitch, groups)
    cells = height * breadth
    first_parts = [(act1b, pitch, 2 * pitch), (act1, 0, (height - 2) * pitch)]
    second_parts = [(act2b, 0, 4 * pitch), (act2, 0, (height - 4) * pitch)]
    for layer, (parts, offset) in enumerate(((first_parts, 1), (second_parts, 2))):
        own = wide(span(groups, offset, offset + breadth), width)
        total = jnp.zeros((pitch, width), F32)
        for ref, start, count in parts:
            for at in range(start, start + count, pitch):
                total = total + ref[at : at + pitch, :]
        mean = jnp.sum(total * own, axis=0, keepdims=True) * (1.0 / cells)
        n = 0
        for ref, start, count in parts:
            for at in range(start, start + count, pitch):
                centred[layer, n : n + pitch, :] = ((ref[at : at + pitch, :] - mean) * own).astype(
                    BF
                )
                n += pitch
        stat[layer] = jnp.zeros(stat.shape[1:], F32)
        put_mean(stat.at[layer, 0:EXTRA], mean, 2)
        put_mean(stat.at[layer, EXTRA : 2 * EXTRA], mean, 1)
    rows = keep.shape[0]

    def give(at, value):
        sent[at : at + value.shape[0], :] = value.astype(BF)

    def hold(at, value):
        keep[at : at + value.shape[0], :] = value

    for layer, put in ((1 - place[0], give), (place[0], hold)):
        emit, finish = packer(width, rows, put)
        panels(centred[layer], centred[layer], emit)
        finish()
    mine[...] = stat[place[0], EXTRA : EXTRA + 8, :]
    sent[rows:, :] = stat[1 - place[0], 0:EXTRA, :].astype(BF)


def ring(dims, place, even, odd, taps2b, w1, w2, act2, slope2, rim, outer, buf):
    height, _, groups, limits = dims
    low = 3 - place[2]
    inside = span(groups, low, low + limits[1])
    finds = (
        lambda r: (outer, r) if r < 2 else (taps2b, r - 2),
        lambda r: (taps2b, 2 + r) if r < 2 else (outer, r),
    )
    for n, (one, two, row) in enumerate(((odd, even, -3), (even, odd, height + 1))):
        rim_taps(rim, [(one, two, r) for r in range(REACH)], place, buf, groups)
        mask = pair_mask(inside, place, limits, row)
        first_rows(lambda r: (rim, r), w1, outer, 2 * n, None, None, 0, groups, mask)
        second_rows(finds[n], w2, act2, slope2, 2 * n * groups * 16, groups)


def write_message(ref, part, rows_ref, centre):
    count = part.shape[0]
    rows_ref[...] = jnp.zeros(rows_ref.shape, F32)
    put_mean(rows_ref, centre, 2)
    ref[0:count, :] = part.astype(BF)
    ref[count:, :] = rows_ref[...].astype(BF)


def merge_pair(dims, place, keep, mine, got, share, centre_out, *rest):
    count, groups, blocks = dims
    messages, (full, left, right, rows_ref) = rest[: groups - 1], rest[groups - 1 :]
    rows = keep.shape[0]
    chunk = rows // groups

    def put(start, value):
        at = slice(start, start + value.shape[0])
        full[at, :] = keep[at, :] + got[at, :].astype(F32) + value

    means = [get_mean(mine[...], blocks, 1), get_mean(got[rows:, :], blocks, 2)]
    centre = spread(means, count, left, right, rows, put)
    centre_out[...] = jnp.zeros(centre_out.shape, F32)
    put_mean(centre_out, centre, 1)
    for k, ref in enumerate(messages, 1):
        at = pl.multiple_of((place[3] ^ k) * chunk, 16)
        write_message(ref, full[pl.ds(at, chunk), :], rows_ref, centre)
    share[...] = full[pl.ds(pl.multiple_of(place[3] * chunk, 16), chunk), :]


def merge_many(dims, final, place, share, mine, *rest):
    count, members, blocks = dims
    gots, rest = rest[: members - 1], rest[members - 1 :]
    chunk = share.shape[0]
    full, left, right, rows_ref = rest[-4:]

    def put(start, value):
        full[start : start + value.shape[0], :] = value

    means = [get_mean(mine[...], blocks, 1)]
    means += [get_mean(got[chunk:, :], blocks, 2) for got in gots]
    centre = spread(means, count, left, right, full.shape[0], put)
    total = share[...] + full[pl.ds(pl.multiple_of(place[3] * chunk, 16), chunk), :]
    for got in gots:
        total = total + got[0:chunk, :].astype(F32)
    if final is None:
        out, centre_out, sent = rest[:3]
        out[...] = total
        centre_out[...] = jnp.zeros(centre_out.shape, F32)
        put_mean(centre_out, centre, 1)
        write_message(sent, total, rows_ref, centre)
    else:
        goal, sent, centre_out = rest[:3]
        rows_ref[...] = jnp.zeros(rows_ref.shape, F32)
        put_mean(rows_ref, centre, 2)
        centre_out[...] = rows_ref[...].astype(BF)
        sent[...] = (total * (1.0 / final) - goal[...]).astype(BF)


def assemble(place, share, centre, *rest):
    gots, out = rest[:-1], rest[-1]
    chunk = share.shape[0]
    for k, ref in enumerate((share,) + tuple(gots)):
        out[pl.ds(pl.multiple_of((place[3] ^ k) * chunk, 16), chunk), :] = ref[...]
    rows = chunk * (len(gots) + 1)
    out[rows:, :] = centre[...]


def back(dims, place, *rest):
    (act1, slope1, act1b, slope1b, act2, slope2, act2b, slope2b, act2r, slope2r) = rest[:10]
    (mine, other, w2, w1, out, taps2, taps1, first_m, second_m, table, buf) = rest[10:]
    height, breadth, groups, limits = dims
    pitch = groups * 16
    step = 2 * pitch
    width = act1.shape[1]
    blocks = width // BLOCK
    packed = table.shape[1] - EXTRA
    table[place[0]] = mine[...]
    table[1 - place[0]] = other[...]
    means, (row, col) = [], corners()
    for layer, ref in enumerate((first_m, second_m)):
        for n, (i, j) in enumerate(pairs(width)):
            block = table[layer, n * BLOCK : (n + 1) * BLOCK, :]
            ref[i * BLOCK : (i + 1) * BLOCK, j * BLOCK : (j + 1) * BLOCK] = block
            ref[j * BLOCK : (j + 1) * BLOCK, i * BLOCK : (i + 1) * BLOCK] = block.T
        for n in range(blocks // 2):
            at = (len(pairs(width)) + n) * BLOCK
            both = table[layer, at : at + BLOCK, :].astype(F32)
            at = (len(pairs(width)) + blocks // 2) * BLOCK
            line = table[layer, at : at + 16, :].astype(F32)[n : n + 1]
            turned = both.T
            one = jnp.where(row <= col, both, turned)
            two = jnp.where(row > col, both, jnp.where(row == col, line, turned))
            for i, block in ((2 * n, one), (2 * n + 1, two)):
                at = slice(i * BLOCK, (i + 1) * BLOCK)
                ref[at, at] = block.astype(BF)
        means.append(get_mean(table[layer, packed:, :], blocks, 2))
    low = 2 - place[2]
    inside2 = span(groups, low, low + limits[1])
    tiles2 = [(act2r, slope2r, 0), (act2b, slope2b, 0)]
    tiles2 += [(act2, slope2, t * pitch) for t in range(0, height - 4, 2)]
    tiles2 += [(act2b, slope2b, step), (act2r, slope2r, step)]

    def second(t):
        act, slope, at = tiles2[t]
        centred = (act[at : at + step, :] - means[1]).astype(BF)
        mask = wide(pair_mask(inside2, place, limits, 2 * t - 2), 2 * BLOCK)
        for lanes in halves(width):
            push = jnp.dot(centred, second_m[:, lanes], preferred_element_type=F32)
            grad = push * slope[at : at + step, lanes] * mask
            for r in range(2):
                write_taps(taps2, 2 * t + r, grad[r * pitch : (r + 1) * pitch], groups, lanes)

    low = 1 - place[2]
    inside1 = span(groups, low, low + limits[1])
    tiles1 = [(act1b, slope1b, 0)]
    tiles1 += [(act1, slope1, t * pitch) for t in range(0, height - 2, 2)]
    tiles1 += [(act1b, slope1b, step)]

    def first(t):
        act, slope, at = tiles1[t]
        centred = (act[at : at + step, :] - means[0]).astype(BF)
        mask = wide(pair_mask(inside1, place, limits, 2 * t - 1), 2 * BLOCK)
        for lanes in halves(width):
            flow = conv(lambda r: (taps2, 2 * t + r), w2, groups, lanes) + jnp.dot(
                centred, first_m[:, lanes], preferred_element_type=F32
            )
            grad = flow * slope[at : at + step, lanes] * mask
            for r in range(2):
                write_taps(taps1, 2 * t + r, grad[r * pitch : (r + 1) * pitch], groups, lanes)

    def last(t):
        got = conv(lambda r: (taps1, 2 * t + r), w1, groups, slice(None))
        for r in range(2):
            at = (2 * t + r) * pitch
            for p in range(buf.shape[0]):
                lanes = slice(p * BLOCK, (p + 1) * BLOCK)
                for n in range(groups):
                    part = got[r * pitch + n * 16 : r * pitch + (n + 1) * 16, lanes]
                    buf[p, pl.ds(at + n, 16, stride=groups), :] = part
                out[2 * t + r, :, lanes] = buf[p, at : at + breadth, :]

    for t in range(len(tiles2)):
        second(t)
    for t in range(len(tiles1)):
        first(t)
    for t in range(height // 2):
        last(t)


def edges(place, pool_hbm, far, near, strips, sems):
    breadth = pool_hbm.shape[1]
    ends = (0, breadth - 8)
    loads = [
        pltpu.make_async_copy(pool_hbm.at[:, pl.ds(at, 8), :], strips.at[n], sems.at[n])
        for n, at in enumerate(ends)
    ]
    for load in loads:
        load.start()
    for load in loads:
        load.wait()
    left_core = place[0] == 0
    left, right = strips[0, :, 0:REACH, :], strips[1, :, 8 - REACH :, :]
    far[...] = jnp.where(left_core, left, right).astype(BF)
    near[...] = jnp.where(left_core, right, left).astype(BF)


def bands(place, pool, far, near, even, odd, row):
    height, breadth, _ = pool.shape
    left_core = place[0] == 0
    odd_row = place[3] & 1
    for start, ref in ((1 - odd_row, even), (odd_row, odd)):
        for r in range(REACH):
            at = start * (height - REACH) + r
            one, two = far[at].astype(F32), near[at].astype(F32)
            row[0:REACH, :] = jnp.where(left_core, one, two)
            row[REACH : REACH + breadth, :] = pool[at]
            row[REACH + breadth :, :] = jnp.where(left_core, two, one)
            ref[r] = row[...].astype(BF)


def flip(weight, out):
    taps, _, width = weight.shape

    def one(t, carry):
        at = pl.multiple_of(t * width, 16)
        out[pl.ds(at, width), :] = weight[taps - 1 - t].T
        return carry

    lax.fori_loop(0, taps, one, 0)


def aim(place, targets, goal, full):
    core = place[0]
    chunk = goal.shape[0]

    def put(start, value):
        full[start : start + value.shape[0], :] = value

    blocks = targets.shape[1] // BLOCK
    emit, finish = packer(targets.shape[1], full.shape[0], put)
    for i in range(blocks):
        for j in range(i, blocks):
            rows, cols = slice(i * BLOCK, (i + 1) * BLOCK), slice(j * BLOCK, (j + 1) * BLOCK)
            emit(i, j, (targets[core, rows, cols] + targets[core, cols, rows].T) * 0.5)
    finish()
    goal[...] = full[pl.ds(pl.multiple_of(place[3] * chunk, 16), chunk), :]


def locate(height, breadth):
    row, tile = lax.axis_index("grp"), lax.axis_index("tile")
    return tile & 1, row * height, tile * breadth, row


def call(body, ins, outs, scratch, flops=0, limit=None, far=()):
    if isinstance(ins[0], tuple):
        (height, breadth), inner, ins = ins[0], body, ins[1:]

        def body(*refs):
            inner(locate(height, breadth), *refs)

    ins = [
        pltpu.with_memory_space_constraint(x, pltpu.HBM) if n in far else x
        for n, x in enumerate(ins)
    ]
    moved = sum(x.size * x.dtype.itemsize for x in ins) + sum(
        x.size * x.dtype.itemsize for x in outs
    )
    return pl.pallas_call(
        body,
        out_shape=tuple(outs),
        in_specs=[HBM if n in far else VMEM for n in range(len(ins))],
        out_specs=tuple(VMEM for _ in outs),
        scratch_shapes=scratch,
        compiler_params=pltpu.CompilerParams(vmem_limit_bytes=(limit or 8) * MIB),
        cost_estimate=pl.CostEstimate(flops=flops, bytes_accessed=moved, transcendentals=0),
    )(*ins)


def shape(dims, dtype):
    return jax.ShapeDtypeStruct(dims, dtype)


def local(pool_input, weight_first, weight_second, targets):
    height, breadth, depth = pool_input.shape
    width = weight_first.shape[3]
    groups, tiles = lax.axis_size("grp"), lax.axis_size("tile")
    chips = tiles // 2
    cells = height * breadth
    positions = cells * groups * tiles
    fold = -(-(breadth + 2 * REACH) // 16)
    pitch, wider = fold * 16, (fold + 2) * 16
    blocks = width // BLOCK
    place = (height, breadth)
    dims = (height, breadth, fold, (height * groups, breadth * tiles))
    swap = [(i, i ^ 1) for i in range(tiles)]
    cross = [(i, i + 1) for i in range(1, tiles - 1, 2)]
    cross = cross + [(j, i) for i, j in cross]

    rim = shape((height, REACH, depth), BF)
    far, near = call(
        edges,
        [place, pool_input],
        [rim] * 2,
        [pltpu.VMEM((2, height, 8, depth), F32), pltpu.SemaphoreType.DMA((2,))],
        flops=4 * 10**9,
        far=(0,),
    )
    far = lax.ppermute(far, "tile", cross)
    near = lax.ppermute(near, "tile", swap)
    band = shape((REACH, breadth + 2 * REACH, depth), BF)
    even, odd = call(
        bands,
        [place, pool_input, far, near],
        [band] * 2,
        [pltpu.VMEM((breadth + 2 * REACH, depth), F32)],
        flops=6 * 10**9,
    )

    def couples(start):
        ways = [(i, i + 1) for i in range(start, groups - 1, 2)]
        return ways + [(j, i) for i, j in ways]

    even = lax.ppermute(even, "grp", couples(0))
    odd = lax.ppermute(odd, "grp", couples(1))

    packed = packed_rows(width, groups)
    w1 = weight_first.reshape(-1, width)
    w2 = weight_second.reshape(-1, width)
    space = (fold * 15 + fold + 2 + 7) // 8 * 8

    def maps(rows):
        return [shape((rows * pitch, width), F32)] * 2

    def cost(rows_first, rows_second):
        return 2 * 9 * width * pitch * (rows_first * depth + rows_second * width)

    taps1, taps2, act1, slope1, act2, slope2 = call(
        functools.partial(middle, dims),
        [place, pool_input, far, near, w1, w2],
        [shape((height * wider, depth), BF), shape(((height - 2) * wider, width), BF)]
        + maps(height - 2)
        + maps(height - 4),
        [pltpu.VMEM((depth // BLOCK, height * space, BLOCK), F32)],
        flops=cost(height - 2, height - 4),
        limit=24,
    )
    taps2b, act1b, slope1b, act2b, slope2b, keep, mine, sent = call(
        functools.partial(front, dims),
        [place, even, odd, taps1, taps2, act1, act2, w1, w2],
        [shape((4 * wider, width), BF)]
        + maps(4)
        + maps(4)
        + [
            shape((packed, BLOCK), F32),
            shape((8, BLOCK), F32),
            shape((packed + EXTRA, BLOCK), BF),
        ],
        [
            pltpu.VMEM((4 * wider, depth), BF),
            pltpu.VMEM((depth // BLOCK, 4 * space, BLOCK), F32),
            pltpu.VMEM((2, height * pitch, width), BF),
            pltpu.VMEM((2, 2 * EXTRA, BLOCK), F32),
        ],
        flops=cost(4, 4),
        limit=24,
    )
    act2r, slope2r = call(
        functools.partial(ring, dims),
        [place, even, odd, taps2b, w1, w2],
        maps(4),
        [
            pltpu.VMEM((4 * wider, depth), BF),
            pltpu.VMEM((4 * wider, width), BF),
            pltpu.VMEM((depth // BLOCK, 4 * space, BLOCK), F32),
        ],
        flops=cost(4, 4),
        limit=16,
    )
    chunk = packed // groups
    (goal,) = call(
        aim,
        [place, targets],
        [shape((chunk, BLOCK), F32)],
        [pltpu.VMEM((packed, BLOCK), F32)],
        flops=2 * 10**8,
    )

    def turned(weight, inner):
        (out,) = call(
            flip,
            [weight.reshape(9, inner, width)],
            [shape((9 * width, inner), BF)],
            [],
            flops=2 * 10**9,
            limit=16,
        )
        return out

    back2 = turned(w2, width)
    back1 = turned(w1, depth)

    def helpers(members):
        deep = -(-3 * members // 16) * 16
        return [
            pltpu.VMEM((packed, BLOCK), F32),
            pltpu.VMEM((deep, width), F32),
            pltpu.VMEM((deep, width), F32),
            pltpu.VMEM((EXTRA, BLOCK), F32),
        ]

    message = shape((chunk + EXTRA, BLOCK), BF)
    part, centre = shape((chunk, BLOCK), F32), shape((8, BLOCK), F32)
    got = lax.ppermute(sent, "tile", swap)
    share, mean, *sents = call(
        functools.partial(merge_pair, (cells, groups, blocks)),
        [place, keep, mine, got],
        [part, centre] + [message] * (groups - 1),
        helpers(2),
    )
    gots = [
        lax.ppermute(sents[k - 1], "grp", [(i, i ^ k) for i in range(groups)])
        for k in range(1, groups)
    ]
    share, mean, sent = call(
        functools.partial(merge_many, (2 * cells, groups, blocks), None),
        [place, share, mean] + gots,
        [part, centre, message],
        helpers(groups),
    )
    gots = [
        lax.ppermute(sent, "tile", [(i, i ^ (2 * k)) for i in range(tiles)])
        for k in range(1, chips)
    ]
    share, mean = call(
        functools.partial(merge_many, (2 * groups * cells, chips, blocks), positions),
        [place, share, mean] + gots + [goal],
        [shape((chunk, BLOCK), BF), shape((EXTRA, BLOCK), BF)],
        helpers(chips),
    )
    gots = [
        lax.ppermute(share, "grp", [(i, i ^ k) for i in range(groups)])
        for k in range(1, groups)
    ]
    table = shape((packed + EXTRA, BLOCK), BF)
    (mine,) = call(assemble, [place, share, mean] + gots, [table], [])
    other = lax.ppermute(mine, "tile", swap)
    maps_in = [act1, slope1, act1b, slope1b, act2, slope2, act2b, slope2b, act2r, slope2r]
    (out,) = call(
        functools.partial(back, dims),
        [place] + maps_in + [mine, other, back2, back1],
        [shape(pool_input.shape, F32)],
        [
            pltpu.VMEM(((height + 4) * wider, width), BF),
            pltpu.VMEM(((height + 2) * wider, width), BF),
            pltpu.VMEM((width, width), BF),
            pltpu.VMEM((width, width), BF),
            pltpu.VMEM((2, packed + EXTRA, BLOCK), BF),
            pltpu.VMEM((depth // BLOCK, height * pitch, BLOCK), F32),
        ],
        flops=2 * 9 * width * pitch * ((height + 2) * width + height * depth),
        limit=32,
    )
    return out


def solution(mesh):
    return jax.shard_map(
        local,
        mesh=mesh,
        in_specs=(P("grp", "tile", None), P(), P(), P()),
        out_specs=P("grp", "tile", None),
        check_vma=False,
    )
```

```python
import functools

import jax
import jax.numpy as jnp
from jax import lax
from jax.experimental import pallas as pl
from jax.experimental.pallas import tpu as pltpu
from jax.sharding import PartitionSpec as P


GELU_SCALE = 0.7978845608
GELU_CUBIC = 0.044715
REACH = 4
BLOCK = 128
EXTRA = 16
BF = jnp.bfloat16
F32 = jnp.float32
VMEM = pl.BlockSpec(memory_space=pltpu.VMEM)
HBM = pl.BlockSpec(memory_space=pltpu.HBM)
MIB = 2**20


def gelu_pair(values):
    square = values * values
    hyper = jnp.tanh(GELU_SCALE * (values + GELU_CUBIC * values * square))
    half = 0.5 * (1.0 + hyper)
    slope = half + 0.5 * values * (1.0 - hyper * hyper) * (
        GELU_SCALE + 3.0 * GELU_SCALE * GELU_CUBIC * square
    )
    return values * half, slope


def pairs(width):
    blocks = width // BLOCK
    return [(i, j) for i in range(blocks) for j in range(i + 1, blocks)]


def packed_rows(width, groups):
    return (len(pairs(width)) + width // BLOCK // 2) * BLOCK + 16 * groups


def corners():
    row = lax.broadcasted_iota(jnp.int32, (BLOCK, BLOCK), 0)
    return row, lax.broadcasted_iota(jnp.int32, (BLOCK, BLOCK), 1)


def packer(width, rows, put):
    places, held, lines = pairs(width), {}, []
    row, col = corners()

    def emit(i, j, block):
        if i != j:
            put(places.index((i, j)) * BLOCK, block)
        elif i % 2 == 0:
            held[i] = block
        else:
            both = jnp.where(row <= col, held[i - 1], block)
            put((len(places) + i // 2) * BLOCK, both)
            lines.append(jnp.sum(jnp.where(row == col, block, 0.0), axis=0, keepdims=True))

    def finish():
        start = (len(places) + len(lines)) * BLOCK
        at = lax.broadcasted_iota(jnp.int32, (rows - start, BLOCK), 0)
        value = jnp.zeros((rows - start, BLOCK), F32)
        for n, line in enumerate(lines):
            value = jnp.where(at == n, line, value)
        put(start, value)

    return emit, finish


def wide(mask, width):
    return jnp.concatenate([mask] * (width // BLOCK), axis=1)


def columns(groups):
    n = lax.broadcasted_iota(jnp.int32, (groups * 16, BLOCK), 0)
    return (n & 15) * groups + (n >> 4)


def span(groups, low, high):
    col = columns(groups)
    return jnp.where((col >= low) & (col < high), 1.0, 0.0).astype(F32)


def pair_mask(inside, place, limits, row):
    parts = []
    for r in range(2):
        at = place[1] + row + r
        parts.append(inside * jnp.where((at >= 0) & (at < limits[0]), 1.0, 0.0).astype(F32))
    return jnp.concatenate(parts, axis=0)


def roll_group(value):
    return [pltpu.roll(value[n * 16 : (n + 1) * 16], 15, 0) for n in range(2)]


def write_taps(ref, row, value, groups, lanes=slice(None)):
    at, pitch = row * (groups + 2) * 16, groups * 16
    ref[at : at + pitch, lanes] = value.astype(BF)
    for n, block in enumerate(roll_group(value)):
        ref[at + pitch + n * 16 : at + pitch + (n + 1) * 16, lanes] = block.astype(BF)


def fold_row(ref, row, buf_ref, at, groups):
    base = row * (groups + 2) * 16
    for n in range(groups + 2):
        for p in range(buf_ref.shape[0]):
            ref[base + n * 16 : base + (n + 1) * 16, p * BLOCK : (p + 1) * BLOCK] = buf_ref[
                p, pl.ds(at + n, 16, stride=groups), :
            ].astype(BF)


def put_row(buf_ref, at, value):
    for p in range(buf_ref.shape[0]):
        buf_ref[p, at : at + value.shape[0], :] = value[:, p * BLOCK : (p + 1) * BLOCK]


def clear_rows(buf_ref, start, stop):
    for p in range(buf_ref.shape[0]):
        buf_ref[p, start:stop, :] = jnp.zeros((stop - start, BLOCK), F32)


def conv(find, weight_ref, groups, lanes):
    pitch, pieces = groups * 16, []
    for a in range(3):
        for b in range(3):
            both = []
            for r in range(2):
                ref, row = find(r + a)
                at = (row * (groups + 2) + b) * 16
                both.append(ref[at : at + pitch, :])
            pieces.append(jnp.concatenate(both, axis=0))
    lhs = jnp.concatenate(pieces, axis=1)
    return jnp.dot(lhs, weight_ref[:, lanes], preferred_element_type=F32)


def halves(width):
    half = 2 * BLOCK
    return [slice(n, n + half) for n in range(0, width, half)]


def first_rows(find, w1, taps_ref, row, act, slope, at, groups, mask):
    width, pitch = w1.shape[1], groups * 16
    for lanes in halves(width):
        value, tilt = gelu_pair(conv(find, w1, groups, lanes))
        value = value * wide(mask, 2 * BLOCK)
        for r in range(2):
            one = value[r * pitch : (r + 1) * pitch]
            write_taps(taps_ref, row + r, one, groups, lanes)
            if act is None:
                continue
            two = tilt[r * pitch : (r + 1) * pitch]
            base = at + r * pitch
            for ref, part in ((act, one), (slope, two)):
                ref[base : base + pitch - 32, lanes] = part[32:]
                for n, block in enumerate(roll_group(part)):
                    to = base + pitch - 32 + n * 16
                    ref[to : to + 16, lanes] = block


def second_rows(find, w2, act, slope, at, groups):
    step = groups * 32
    for lanes in halves(w2.shape[1]):
        value, tilt = gelu_pair(conv(find, w2, groups, lanes))
        act[at : at + step, lanes] = value
        slope[at : at + step, lanes] = tilt


def put_mean(rows_ref, mean, parts):
    blocks = mean.shape[1] // BLOCK
    high = mean.astype(BF).astype(F32)
    for p, row in enumerate((high, mean - high) if parts == 2 else (mean,)):
        for j in range(blocks):
            at = p * blocks + j
            rows_ref[at : at + 1, :] = row[:, j * BLOCK : (j + 1) * BLOCK]


def get_mean(rows, blocks, parts):
    rows = rows.astype(F32)
    found = rows[:blocks] + rows[blocks : 2 * blocks] if parts == 2 else rows[:blocks]
    return jnp.concatenate([found[j : j + 1] for j in range(blocks)], axis=1)


def panels(lhs, rhs, emit):
    width = lhs.shape[1]
    for i in range(0, width, BLOCK):
        panel = lax.dot_general(
            lhs[:, i : i + BLOCK],
            rhs[:, i:],
            (((0,), (0,)), ((), ())),
            preferred_element_type=F32,
        )
        for j in range(0, width - i, BLOCK):
            emit(i // BLOCK, (i + j) // BLOCK, panel[:, j : j + BLOCK])


def spread(means, count, left_ref, right_ref, rows, put):
    centre = means[0]
    for mean in means[1:]:
        centre = centre + mean
    centre = centre * (1.0 / len(means))
    left_ref[...] = jnp.zeros(left_ref.shape, F32)
    right_ref[...] = jnp.zeros(right_ref.shape, F32)
    for n, mean in enumerate(means):
        away = mean - centre
        high = away.astype(BF).astype(F32)
        low = away - high
        for q, (lhs, rhs) in enumerate(((high, high), (high, low), (low, high))):
            at = 3 * n + q
            left_ref[at : at + 1, :] = lhs
            right_ref[at : at + 1, :] = rhs
    lhs, rhs = left_ref[...].astype(BF), right_ref[...].astype(BF)
    emit, finish = packer(lhs.shape[1], rows, lambda at, value: put(at, value * float(count)))
    panels(lhs, rhs, emit)
    finish()
    return centre


def middle(dims, place, pool, far, near, w1, w2, *rest):
    taps1, taps2, act1, slope1, act2, slope2, buf = rest
    height, breadth, groups, limits = dims
    pitch = groups * 16
    left_core = place[0] == 0
    space = buf.shape[1] // height
    for r in range(height):
        at = r * space
        one, two = far[r].astype(F32), near[r].astype(F32)
        put_row(buf, at, jnp.where(left_core, one, two))
        put_row(buf, at + REACH, pool[r])
        put_row(buf, at + REACH + breadth, jnp.where(left_core, two, one))
        clear_rows(buf, at + 2 * REACH + breadth, at + space)
        fold_row(taps1, r, buf, at, groups)
    low = 3 - place[2]
    inside = span(groups, low, low + limits[1])
    for t in range(0, height - 2, 2):
        mask = pair_mask(inside, place, limits, t + 1)
        first_rows(
            lambda r: (taps1, t + r), w1, taps2, t, act1, slope1, t * pitch, groups, mask
        )
        if t >= 2:
            second_rows(
                lambda r: (taps2, t - 2 + r), w2, act2, slope2, (t - 2) * pitch, groups
            )


def rim_taps(ref, rows, place, buf, groups):
    space = buf.shape[1] // len(rows)
    even = (place[3] & 1) == 0
    for n, (one, two, r) in enumerate(rows):
        breadth = one.shape[1]
        at = n * space
        put_row(buf, at, jnp.where(even, one[r].astype(F32), two[r].astype(F32)))
        clear_rows(buf, at + breadth, at + space)
        fold_row(ref, n, buf, at, groups)


def front(dims, place, even, odd, taps1, taps2, act1, act2, w1, w2, *rest):
    (taps2b, act1b, slope1b, act2b, slope2b, centred, mine, sent) = rest[:8]
    (rim, buf, stat) = rest[8:]
    height, breadth, groups, limits = dims
    pitch = groups * 16
    width = w1.shape[1]
    rows = [(odd, even, REACH - 2), (odd, even, REACH - 1), (even, odd, 0), (even, odd, 1)]
    rim_taps(rim, rows, place, buf, groups)
    low = 3 - place[2]
    inside = span(groups, low, low + limits[1])
    last = height - 2
    finds = (
        lambda r: (rim, r) if r < 2 else (taps1, r - 2),
        lambda r: (taps1, last + r) if r < 2 else (rim, r),
    )
    for n, row in enumerate((-1, height - 1)):
        mask = pair_mask(inside, place, limits, row)
        first_rows(
            finds[n], w1, taps2b, 2 * n, act1b, slope1b, 2 * n * pitch, groups, mask
        )
    last = height - 4
    finds = (
        lambda r: (taps2b, r) if r < 2 else (taps2, r - 2),
        lambda r: (taps2, last + r) if r < 2 else (taps2b, r),
    )
    for n in range(2):
        second_rows(finds[n], w2, act2b, slope2b, 2 * n * pitch, groups)
    cells = height * breadth
    first_parts = [(act1b, pitch, 2 * pitch), (act1, 0, (height - 2) * pitch)]
    second_parts = [(act2b, 0, 4 * pitch), (act2, 0, (height - 4) * pitch)]
    for layer, (parts, offset) in enumerate(((first_parts, 1), (second_parts, 2))):
        own = wide(span(groups, offset, offset + breadth), width)
        total = jnp.zeros((pitch, width), F32)
        for ref, start, count in parts:
            for at in range(start, start + count, pitch):
                total = total + ref[at : at + pitch, :]
        mean = jnp.sum(total * own, axis=0, keepdims=True) * (1.0 / cells)
        n = 0
        for ref, start, count in parts:
            for at in range(start, start + count, pitch):
                centred[layer, n : n + pitch, :] = ((ref[at : at + pitch, :] - mean) * own).astype(
                    BF
                )
                n += pitch
        stat[layer] = jnp.zeros(stat.shape[1:], F32)
        put_mean(stat.at[layer, 0:EXTRA], mean, 2)
        put_mean(stat.at[layer, EXTRA : 2 * EXTRA], mean, 1)
    rows = sent.shape[0] - EXTRA

    def put(at, value):
        sent[at : at + value.shape[0], :] = value.astype(BF)

    emit, finish = packer(width, rows, put)
    other = centred[1 - place[0]]
    panels(other, other, emit)
    finish()
    mine[...] = stat[place[0], EXTRA : EXTRA + 8, :]
    sent[rows:, :] = stat[1 - place[0], 0:EXTRA, :].astype(BF)


def hold(place, centred, keep):
    def put(at, value):
        keep[at : at + value.shape[0], :] = value

    own = centred[place[0]]
    emit, finish = packer(own.shape[1], keep.shape[0], put)
    panels(own, own, emit)
    finish()


def ring(dims, place, even, odd, taps2b, w1, w2, act2, slope2, rim, outer, buf):
    height, _, groups, limits = dims
    low = 3 - place[2]
    inside = span(groups, low, low + limits[1])
    finds = (
        lambda r: (outer, r) if r < 2 else (taps2b, r - 2),
        lambda r: (taps2b, 2 + r) if r < 2 else (outer, r),
    )
    for n, (one, two, row) in enumerate(((odd, even, -3), (even, odd, height + 1))):
        rim_taps(rim, [(one, two, r) for r in range(REACH)], place, buf, groups)
        mask = pair_mask(inside, place, limits, row)
        first_rows(lambda r: (rim, r), w1, outer, 2 * n, None, None, 0, groups, mask)
        second_rows(finds[n], w2, act2, slope2, 2 * n * groups * 16, groups)


def write_message(ref, part, rows_ref, centre):
    count = part.shape[0]
    rows_ref[...] = jnp.zeros(rows_ref.shape, F32)
    put_mean(rows_ref, centre, 2)
    ref[0:count, :] = part.astype(BF)
    ref[count:, :] = rows_ref[...].astype(BF)


def merge_pair(dims, place, keep, mine, got, share, centre_out, *rest):
    count, groups, blocks = dims
    messages, (full, left, right, rows_ref) = rest[: groups - 1], rest[groups - 1 :]
    rows = keep.shape[0]
    chunk = rows // groups

    def put(start, value):
        at = slice(start, start + value.shape[0])
        full[at, :] = keep[at, :] + got[at, :].astype(F32) + value

    means = [get_mean(mine[...], blocks, 1), get_mean(got[rows:, :], blocks, 2)]
    centre = spread(means, count, left, right, rows, put)
    centre_out[...] = jnp.zeros(centre_out.shape, F32)
    put_mean(centre_out, centre, 1)
    for k, ref in enumerate(messages, 1):
        at = pl.multiple_of((place[3] ^ k) * chunk, 16)
        write_message(ref, full[pl.ds(at, chunk), :], rows_ref, centre)
    share[...] = full[pl.ds(pl.multiple_of(place[3] * chunk, 16), chunk), :]


def merge_many(dims, final, place, share, mine, *rest):
    count, members, blocks = dims
    gots, rest = rest[: members - 1], rest[members - 1 :]
    chunk = share.shape[0]
    full, left, right, rows_ref = rest[-4:]

    def put(start, value):
        full[start : start + value.shape[0], :] = value

    means = [get_mean(mine[...], blocks, 1)]
    means += [get_mean(got[chunk:, :], blocks, 2) for got in gots]
    centre = spread(means, count, left, right, full.shape[0], put)
    total = share[...] + full[pl.ds(pl.multiple_of(place[3] * chunk, 16), chunk), :]
    for got in gots:
        total = total + got[0:chunk, :].astype(F32)
    if final is None:
        out, centre_out, sent = rest[:3]
        out[...] = total
        centre_out[...] = jnp.zeros(centre_out.shape, F32)
        put_mean(centre_out, centre, 1)
        write_message(sent, total, rows_ref, centre)
    else:
        goal, sent, centre_out = rest[:3]
        rows_ref[...] = jnp.zeros(rows_ref.shape, F32)
        put_mean(rows_ref, centre, 2)
        centre_out[...] = rows_ref[...].astype(BF)
        sent[...] = (total * (1.0 / final) - goal[...]).astype(BF)


def assemble(place, share, centre, *rest):
    gots, out = rest[:-1], rest[-1]
    chunk = share.shape[0]
    for k, ref in enumerate((share,) + tuple(gots)):
        out[pl.ds(pl.multiple_of((place[3] ^ k) * chunk, 16), chunk), :] = ref[...]
    rows = chunk * (len(gots) + 1)
    out[rows:, :] = centre[...]


def back(dims, place, *rest):
    (act1, slope1, act1b, slope1b, act2, slope2, act2b, slope2b, act2r, slope2r) = rest[:10]
    (mine, other, w2, w1, out, taps2, taps1, first_m, second_m, table, buf) = rest[10:]
    height, breadth, groups, limits = dims
    pitch = groups * 16
    step = 2 * pitch
    width = act1.shape[1]
    blocks = width // BLOCK
    packed = table.shape[1] - EXTRA
    table[place[0]] = mine[...]
    table[1 - place[0]] = other[...]
    means, (row, col) = [], corners()
    for layer, ref in enumerate((first_m, second_m)):
        for n, (i, j) in enumerate(pairs(width)):
            block = table[layer, n * BLOCK : (n + 1) * BLOCK, :]
            ref[i * BLOCK : (i + 1) * BLOCK, j * BLOCK : (j + 1) * BLOCK] = block
            ref[j * BLOCK : (j + 1) * BLOCK, i * BLOCK : (i + 1) * BLOCK] = block.T
        for n in range(blocks // 2):
            at = (len(pairs(width)) + n) * BLOCK
            both = table[layer, at : at + BLOCK, :].astype(F32)
            at = (len(pairs(width)) + blocks // 2) * BLOCK
            line = table[layer, at : at + 16, :].astype(F32)[n : n + 1]
            turned = both.T
            one = jnp.where(row <= col, both, turned)
            two = jnp.where(row > col, both, jnp.where(row == col, line, turned))
            for i, block in ((2 * n, one), (2 * n + 1, two)):
                at = slice(i * BLOCK, (i + 1) * BLOCK)
                ref[at, at] = block.astype(BF)
        means.append(get_mean(table[layer, packed:, :], blocks, 2))
    low = 2 - place[2]
    inside2 = span(groups, low, low + limits[1])
    tiles2 = [(act2r, slope2r, 0), (act2b, slope2b, 0)]
    tiles2 += [(act2, slope2, t * pitch) for t in range(0, height - 4, 2)]
    tiles2 += [(act2b, slope2b, step), (act2r, slope2r, step)]

    def second(t):
        act, slope, at = tiles2[t]
        centred = (act[at : at + step, :] - means[1]).astype(BF)
        mask = wide(pair_mask(inside2, place, limits, 2 * t - 2), 2 * BLOCK)
        for lanes in halves(width):
            push = jnp.dot(centred, second_m[:, lanes], preferred_element_type=F32)
            grad = push * slope[at : at + step, lanes] * mask
            for r in range(2):
                write_taps(taps2, 2 * t + r, grad[r * pitch : (r + 1) * pitch], groups, lanes)

    low = 1 - place[2]
    inside1 = span(groups, low, low + limits[1])
    tiles1 = [(act1b, slope1b, 0)]
    tiles1 += [(act1, slope1, t * pitch) for t in range(0, height - 2, 2)]
    tiles1 += [(act1b, slope1b, step)]

    def first(t):
        act, slope, at = tiles1[t]
        centred = (act[at : at + step, :] - means[0]).astype(BF)
        mask = wide(pair_mask(inside1, place, limits, 2 * t - 1), 2 * BLOCK)
        for lanes in halves(width):
            flow = conv(lambda r: (taps2, 2 * t + r), w2, groups, lanes) + jnp.dot(
                centred, first_m[:, lanes], preferred_element_type=F32
            )
            grad = flow * slope[at : at + step, lanes] * mask
            for r in range(2):
                write_taps(taps1, 2 * t + r, grad[r * pitch : (r + 1) * pitch], groups, lanes)

    def last(t):
        got = conv(lambda r: (taps1, 2 * t + r), w1, groups, slice(None))
        for r in range(2):
            at = (2 * t + r) * pitch
            for p in range(buf.shape[0]):
                lanes = slice(p * BLOCK, (p + 1) * BLOCK)
                for n in range(groups):
                    part = got[r * pitch + n * 16 : r * pitch + (n + 1) * 16, lanes]
                    buf[p, pl.ds(at + n, 16, stride=groups), :] = part
                out[2 * t + r, :, lanes] = buf[p, at : at + breadth, :]

    for t in range(len(tiles2)):
        second(t)
    for t in range(len(tiles1)):
        first(t)
    for t in range(height // 2):
        last(t)


def edges(place, pool_hbm, far, near, strips, sems):
    breadth = pool_hbm.shape[1]
    ends = (0, breadth - 8)
    loads = [
        pltpu.make_async_copy(pool_hbm.at[:, pl.ds(at, 8), :], strips.at[n], sems.at[n])
        for n, at in enumerate(ends)
    ]
    for load in loads:
        load.start()
    for load in loads:
        load.wait()
    left_core = place[0] == 0
    left, right = strips[0, :, 0:REACH, :], strips[1, :, 8 - REACH :, :]
    far[...] = jnp.where(left_core, left, right).astype(BF)
    near[...] = jnp.where(left_core, right, left).astype(BF)


def bands(place, pool, far, near, even, odd, row):
    height, breadth, _ = pool.shape
    left_core = place[0] == 0
    odd_row = place[3] & 1
    for start, ref in ((1 - odd_row, even), (odd_row, odd)):
        for r in range(REACH):
            at = start * (height - REACH) + r
            one, two = far[at].astype(F32), near[at].astype(F32)
            row[0:REACH, :] = jnp.where(left_core, one, two)
            row[REACH : REACH + breadth, :] = pool[at]
            row[REACH + breadth :, :] = jnp.where(left_core, two, one)
            ref[r] = row[...].astype(BF)


def flip(weight, out):
    taps, _, width = weight.shape

    def one(t, carry):
        at = pl.multiple_of(t * width, 16)
        out[pl.ds(at, width), :] = weight[taps - 1 - t].T
        return carry

    lax.fori_loop(0, taps, one, 0)


def aim(place, targets, goal, full):
    core = place[0]
    chunk = goal.shape[0]

    def put(start, value):
        full[start : start + value.shape[0], :] = value

    blocks = targets.shape[1] // BLOCK
    emit, finish = packer(targets.shape[1], full.shape[0], put)
    for i in range(blocks):
        for j in range(i, blocks):
            rows, cols = slice(i * BLOCK, (i + 1) * BLOCK), slice(j * BLOCK, (j + 1) * BLOCK)
            emit(i, j, (targets[core, rows, cols] + targets[core, cols, rows].T) * 0.5)
    finish()
    goal[...] = full[pl.ds(pl.multiple_of(place[3] * chunk, 16), chunk), :]


def locate(height, breadth):
    row, tile = lax.axis_index("grp"), lax.axis_index("tile")
    return tile & 1, row * height, tile * breadth, row


def call(body, ins, outs, scratch, flops=0, limit=None, far=()):
    if isinstance(ins[0], tuple):
        (height, breadth), inner, ins = ins[0], body, ins[1:]

        def body(*refs):
            inner(locate(height, breadth), *refs)

    ins = [
        pltpu.with_memory_space_constraint(x, pltpu.HBM) if n in far else x
        for n, x in enumerate(ins)
    ]
    moved = sum(x.size * x.dtype.itemsize for x in ins) + sum(
        x.size * x.dtype.itemsize for x in outs
    )
    return pl.pallas_call(
        body,
        out_shape=tuple(outs),
        in_specs=[HBM if n in far else VMEM for n in range(len(ins))],
        out_specs=tuple(VMEM for _ in outs),
        scratch_shapes=scratch,
        compiler_params=pltpu.CompilerParams(vmem_limit_bytes=(limit or 8) * MIB),
        cost_estimate=pl.CostEstimate(flops=flops, bytes_accessed=moved, transcendentals=0),
    )(*ins)


def shape(dims, dtype):
    return jax.ShapeDtypeStruct(dims, dtype)


def local(pool_input, weight_first, weight_second, targets):
    height, breadth, depth = pool_input.shape
    width = weight_first.shape[3]
    groups, tiles = lax.axis_size("grp"), lax.axis_size("tile")
    chips = tiles // 2
    cells = height * breadth
    positions = cells * groups * tiles
    fold = -(-(breadth + 2 * REACH) // 16)
    pitch, wider = fold * 16, (fold + 2) * 16
    blocks = width // BLOCK
    place = (height, breadth)
    dims = (height, breadth, fold, (height * groups, breadth * tiles))
    swap = [(i, i ^ 1) for i in range(tiles)]
    cross = [(i, i + 1) for i in range(1, tiles - 1, 2)]
    cross = cross + [(j, i) for i, j in cross]

    rim = shape((height, REACH, depth), BF)
    far, near = call(
        edges,
        [place, pool_input],
        [rim] * 2,
        [pltpu.VMEM((2, height, 8, depth), F32), pltpu.SemaphoreType.DMA((2,))],
        flops=4 * 10**9,
        far=(0,),
    )
    far = lax.ppermute(far, "tile", cross)
    near = lax.ppermute(near, "tile", swap)
    band = shape((REACH, breadth + 2 * REACH, depth), BF)
    even, odd = call(
        bands,
        [place, pool_input, far, near],
        [band] * 2,
        [pltpu.VMEM((breadth + 2 * REACH, depth), F32)],
        flops=6 * 10**9,
    )

    def couples(start):
        ways = [(i, i + 1) for i in range(start, groups - 1, 2)]
        return ways + [(j, i) for i, j in ways]

    even = lax.ppermute(even, "grp", couples(0))
    odd = lax.ppermute(odd, "grp", couples(1))

    packed = packed_rows(width, groups)
    w1 = weight_first.reshape(-1, width)
    w2 = weight_second.reshape(-1, width)
    space = (fold * 15 + fold + 2 + 7) // 8 * 8

    def maps(rows):
        return [shape((rows * pitch, width), F32)] * 2

    def cost(rows_first, rows_second):
        return 2 * 9 * width * pitch * (rows_first * depth + rows_second * width)

    taps1, taps2, act1, slope1, act2, slope2 = call(
        functools.partial(middle, dims),
        [place, pool_input, far, near, w1, w2],
        [shape((height * wider, depth), BF), shape(((height - 2) * wider, width), BF)]
        + maps(height - 2)
        + maps(height - 4),
        [pltpu.VMEM((depth // BLOCK, height * space, BLOCK), F32)],
        flops=cost(height - 2, height - 4),
        limit=24,
    )
    taps2b, act1b, slope1b, act2b, slope2b, centred, mine, sent = call(
        functools.partial(front, dims),
        [place, even, odd, taps1, taps2, act1, act2, w1, w2],
        [shape((4 * wider, width), BF)]
        + maps(4)
        + maps(4)
        + [
            shape((2, height * pitch, width), BF),
            shape((8, BLOCK), F32),
            shape((packed + EXTRA, BLOCK), BF),
        ],
        [
            pltpu.VMEM((4 * wider, depth), BF),
            pltpu.VMEM((depth // BLOCK, 4 * space, BLOCK), F32),
            pltpu.VMEM((2, 2 * EXTRA, BLOCK), F32),
        ],
        flops=cost(4, 4),
        limit=24,
    )
    act2r, slope2r = call(
        functools.partial(ring, dims),
        [place, even, odd, taps2b, w1, w2],
        maps(4),
        [
            pltpu.VMEM((4 * wider, depth), BF),
            pltpu.VMEM((4 * wider, width), BF),
            pltpu.VMEM((depth // BLOCK, 4 * space, BLOCK), F32),
        ],
        flops=cost(4, 4),
        limit=16,
    )
    chunk = packed // groups
    (goal,) = call(
        aim,
        [place, targets],
        [shape((chunk, BLOCK), F32)],
        [pltpu.VMEM((packed, BLOCK), F32)],
        flops=2 * 10**8,
    )

    def turned(weight, inner):
        (out,) = call(
            flip,
            [weight.reshape(9, inner, width)],
            [shape((9 * width, inner), BF)],
            [],
            flops=2 * 10**9,
            limit=16,
        )
        return out

    back2 = turned(w2, width)
    back1 = turned(w1, depth)

    def helpers(members):
        deep = -(-3 * members // 16) * 16
        return [
            pltpu.VMEM((packed, BLOCK), F32),
            pltpu.VMEM((deep, width), F32),
            pltpu.VMEM((deep, width), F32),
            pltpu.VMEM((EXTRA, BLOCK), F32),
        ]

    message = shape((chunk + EXTRA, BLOCK), BF)
    part, centre = shape((chunk, BLOCK), F32), shape((8, BLOCK), F32)
    got = lax.ppermute(sent, "tile", swap)
    (keep,) = call(
        hold,
        [place, centred],
        [shape((packed, BLOCK), F32)],
        [],
        flops=2 * width * width * height * pitch,
    )
    share, mean, *sents = call(
        functools.partial(merge_pair, (cells, groups, blocks)),
        [place, keep, mine, got],
        [part, centre] + [message] * (groups - 1),
        helpers(2),
    )
    gots = [
        lax.ppermute(sents[k - 1], "grp", [(i, i ^ k) for i in range(groups)])
        for k in range(1, groups)
    ]
    share, mean, sent = call(
        functools.partial(merge_many, (2 * cells, groups, blocks), None),
        [place, share, mean] + gots,
        [part, centre, message],
        helpers(groups),
    )
    gots = [
        lax.ppermute(sent, "tile", [(i, i ^ (2 * k)) for i in range(tiles)])
        for k in range(1, chips)
    ]
    share, mean = call(
        functools.partial(merge_many, (2 * groups * cells, chips, blocks), positions),
        [place, share, mean] + gots + [goal],
        [shape((chunk, BLOCK), BF), shape((EXTRA, BLOCK), BF)],
        helpers(chips),
    )
    gots = [
        lax.ppermute(share, "grp", [(i, i ^ k) for i in range(groups)])
        for k in range(1, groups)
    ]
    table = shape((packed + EXTRA, BLOCK), BF)
    (mine,) = call(assemble, [place, share, mean] + gots, [table], [])
    other = lax.ppermute(mine, "tile", swap)
    maps_in = [act1, slope1, act1b, slope1b, act2, slope2, act2b, slope2b, act2r, slope2r]
    (out,) = call(
        functools.partial(back, dims),
        [place] + maps_in + [mine, other, back2, back1],
        [shape(pool_input.shape, F32)],
        [
            pltpu.VMEM(((height + 4) * wider, width), BF),
            pltpu.VMEM(((height + 2) * wider, width), BF),
            pltpu.VMEM((width, width), BF),
            pltpu.VMEM((width, width), BF),
            pltpu.VMEM((2, packed + EXTRA, BLOCK), BF),
            pltpu.VMEM((depth // BLOCK, height * pitch, BLOCK), F32),
        ],
        flops=2 * 9 * width * pitch * ((height + 2) * width + height * depth),
        limit=32,
    )
    return out


def solution(mesh):
    return jax.shard_map(
        local,
        mesh=mesh,
        in_specs=(P("grp", "tile", None), P(), P(), P()),
        out_specs=P("grp", "tile", None),
        check_vma=False,
    )
```

```python
import functools

import jax
import jax.numpy as jnp
from jax import lax
from jax.experimental import pallas as pl
from jax.experimental.pallas import tpu as pltpu
from jax.sharding import PartitionSpec as P


GELU_SCALE = 0.7978845608
GELU_CUBIC = 0.044715
REACH = 4
BLOCK = 128
EXTRA = 16
BF = jnp.bfloat16
F32 = jnp.float32
VMEM = pl.BlockSpec(memory_space=pltpu.VMEM)
HBM = pl.BlockSpec(memory_space=pltpu.HBM)
MIB = 2**20


def gelu_pair(values):
    square = values * values
    hyper = jnp.tanh(GELU_SCALE * (values + GELU_CUBIC * values * square))
    half = 0.5 * (1.0 + hyper)
    slope = half + 0.5 * values * (1.0 - hyper * hyper) * (
        GELU_SCALE + 3.0 * GELU_SCALE * GELU_CUBIC * square
    )
    return values * half, slope


def pairs(width):
    blocks = width // BLOCK
    return [(i, j) for i in range(blocks) for j in range(i + 1, blocks)]


def packed_rows(width, groups):
    return (len(pairs(width)) + width // BLOCK // 2) * BLOCK + 16 * groups


def corners():
    row = lax.broadcasted_iota(jnp.int32, (BLOCK, BLOCK), 0)
    return row, lax.broadcasted_iota(jnp.int32, (BLOCK, BLOCK), 1)


def packer(width, rows, put):
    places, held, lines = pairs(width), {}, []
    row, col = corners()

    def emit(i, j, block):
        if i != j:
            put(places.index((i, j)) * BLOCK, block)
        elif i % 2 == 0:
            held[i] = block
        else:
            both = jnp.where(row <= col, held[i - 1], block)
            put((len(places) + i // 2) * BLOCK, both)
            lines.append(jnp.sum(jnp.where(row == col, block, 0.0), axis=0, keepdims=True))

    def finish():
        start = (len(places) + len(lines)) * BLOCK
        at = lax.broadcasted_iota(jnp.int32, (rows - start, BLOCK), 0)
        value = jnp.zeros((rows - start, BLOCK), F32)
        for n, line in enumerate(lines):
            value = jnp.where(at == n, line, value)
        put(start, value)

    return emit, finish


def wide(mask, width):
    return jnp.concatenate([mask] * (width // BLOCK), axis=1)


def columns(groups):
    n = lax.broadcasted_iota(jnp.int32, (groups * 16, BLOCK), 0)
    return (n & 15) * groups + (n >> 4)


def span(groups, low, high):
    col = columns(groups)
    return jnp.where((col >= low) & (col < high), 1.0, 0.0).astype(F32)


def pair_mask(inside, place, limits, row):
    parts = []
    for r in range(2):
        at = place[1] + row + r
        parts.append(inside * jnp.where((at >= 0) & (at < limits[0]), 1.0, 0.0).astype(F32))
    return jnp.concatenate(parts, axis=0)


def roll_group(value):
    return [pltpu.roll(value[n * 16 : (n + 1) * 16], 15, 0) for n in range(2)]


def write_taps(ref, row, value, groups, lanes=slice(None)):
    at, pitch = row * (groups + 2) * 16, groups * 16
    ref[at : at + pitch, lanes] = value.astype(BF)
    for n, block in enumerate(roll_group(value)):
        ref[at + pitch + n * 16 : at + pitch + (n + 1) * 16, lanes] = block.astype(BF)


def fold_row(ref, row, buf_ref, at, groups):
    base = row * (groups + 2) * 16
    for n in range(groups + 2):
        for p in range(buf_ref.shape[0]):
            ref[base + n * 16 : base + (n + 1) * 16, p * BLOCK : (p + 1) * BLOCK] = buf_ref[
                p, pl.ds(at + n, 16, stride=groups), :
            ].astype(BF)


def put_row(buf_ref, at, value):
    for p in range(buf_ref.shape[0]):
        buf_ref[p, at : at + value.shape[0], :] = value[:, p * BLOCK : (p + 1) * BLOCK]


def clear_rows(buf_ref, start, stop):
    for p in range(buf_ref.shape[0]):
        buf_ref[p, start:stop, :] = jnp.zeros((stop - start, BLOCK), F32)


def conv(find, weight_ref, groups, lanes):
    pitch, pieces = groups * 16, []
    for a in range(3):
        for b in range(3):
            both = []
            for r in range(2):
                ref, row = find(r + a)
                at = (row * (groups + 2) + b) * 16
                both.append(ref[at : at + pitch, :])
            pieces.append(jnp.concatenate(both, axis=0))
    lhs = jnp.concatenate(pieces, axis=1)
    return jnp.dot(lhs, weight_ref[:, lanes], preferred_element_type=F32)


def halves(width):
    half = 2 * BLOCK
    return [slice(n, n + half) for n in range(0, width, half)]


def first_rows(find, w1, taps_ref, row, act, slope, at, groups, mask):
    width, pitch = w1.shape[1], groups * 16
    for lanes in halves(width):
        value, tilt = gelu_pair(conv(find, w1, groups, lanes))
        value = value * wide(mask, 2 * BLOCK)
        for r in range(2):
            one = value[r * pitch : (r + 1) * pitch]
            write_taps(taps_ref, row + r, one, groups, lanes)
            if act is None:
                continue
            two = tilt[r * pitch : (r + 1) * pitch]
            base = at + r * pitch
            for ref, part in ((act, one), (slope, two)):
                ref[base : base + pitch - 32, lanes] = part[32:]
                for n, block in enumerate(roll_group(part)):
                    to = base + pitch - 32 + n * 16
                    ref[to : to + 16, lanes] = block


def second_rows(find, w2, act, slope, at, groups):
    step = groups * 32
    for lanes in halves(w2.shape[1]):
        value, tilt = gelu_pair(conv(find, w2, groups, lanes))
        act[at : at + step, lanes] = value
        slope[at : at + step, lanes] = tilt


def put_mean(rows_ref, mean, parts):
    blocks = mean.shape[1] // BLOCK
    high = mean.astype(BF).astype(F32)
    for p, row in enumerate((high, mean - high) if parts == 2 else (mean,)):
        for j in range(blocks):
            at = p * blocks + j
            rows_ref[at : at + 1, :] = row[:, j * BLOCK : (j + 1) * BLOCK]


def get_mean(rows, blocks, parts):
    rows = rows.astype(F32)
    found = rows[:blocks] + rows[blocks : 2 * blocks] if parts == 2 else rows[:blocks]
    return jnp.concatenate([found[j : j + 1] for j in range(blocks)], axis=1)


def panels(lhs, rhs, emit):
    width = lhs.shape[1]
    for i in range(0, width, BLOCK):
        panel = lax.dot_general(
            lhs[:, i : i + BLOCK],
            rhs[:, i:],
            (((0,), (0,)), ((), ())),
            preferred_element_type=F32,
        )
        for j in range(0, width - i, BLOCK):
            emit(i // BLOCK, (i + j) // BLOCK, panel[:, j : j + BLOCK])


def spread(means, count, left_ref, right_ref, rows, put):
    centre = means[0]
    for mean in means[1:]:
        centre = centre + mean
    centre = centre * (1.0 / len(means))
    left_ref[...] = jnp.zeros(left_ref.shape, F32)
    right_ref[...] = jnp.zeros(right_ref.shape, F32)
    for n, mean in enumerate(means):
        away = mean - centre
        high = away.astype(BF).astype(F32)
        low = away - high
        for q, (lhs, rhs) in enumerate(((high, high), (high, low), (low, high))):
            at = 3 * n + q
            left_ref[at : at + 1, :] = lhs
            right_ref[at : at + 1, :] = rhs
    lhs, rhs = left_ref[...].astype(BF), right_ref[...].astype(BF)
    emit, finish = packer(lhs.shape[1], rows, lambda at, value: put(at, value * float(count)))
    panels(lhs, rhs, emit)
    finish()
    return centre


def middle(dims, place, pool, far, near, w1, w2, *rest):
    taps1, taps2, act1, slope1, act2, slope2, buf = rest
    height, breadth, groups, limits = dims
    pitch = groups * 16
    left_core = place[0] == 0
    space = buf.shape[1] // height
    for r in range(height):
        at = r * space
        one, two = far[r].astype(F32), near[r].astype(F32)
        put_row(buf, at, jnp.where(left_core, one, two))
        put_row(buf, at + REACH, pool[r])
        put_row(buf, at + REACH + breadth, jnp.where(left_core, two, one))
        clear_rows(buf, at + 2 * REACH + breadth, at + space)
        fold_row(taps1, r, buf, at, groups)
    low = 3 - place[2]
    inside = span(groups, low, low + limits[1])
    for t in range(0, height - 2, 2):
        mask = pair_mask(inside, place, limits, t + 1)
        first_rows(
            lambda r: (taps1, t + r), w1, taps2, t, act1, slope1, t * pitch, groups, mask
        )
        if t >= 2:
            second_rows(
                lambda r: (taps2, t - 2 + r), w2, act2, slope2, (t - 2) * pitch, groups
            )


def rim_taps(ref, rows, place, buf, groups):
    space = buf.shape[1] // len(rows)
    even = (place[3] & 1) == 0
    for n, (one, two, r) in enumerate(rows):
        breadth = one.shape[1]
        at = n * space
        put_row(buf, at, jnp.where(even, one[r].astype(F32), two[r].astype(F32)))
        clear_rows(buf, at + breadth, at + space)
        fold_row(ref, n, buf, at, groups)


def front(dims, place, even, odd, taps1, taps2, act1, act2, w1, w2, *rest):
    (taps2b, act1b, slope1b, act2b, slope2b, centred, mine, sent) = rest[:8]
    (rim, buf, stat) = rest[8:]
    height, breadth, groups, limits = dims
    pitch = groups * 16
    width = w1.shape[1]
    rows = [(odd, even, REACH - 2), (odd, even, REACH - 1), (even, odd, 0), (even, odd, 1)]
    rim_taps(rim, rows, place, buf, groups)
    low = 3 - place[2]
    inside = span(groups, low, low + limits[1])
    last = height - 2
    finds = (
        lambda r: (rim, r) if r < 2 else (taps1, r - 2),
        lambda r: (taps1, last + r) if r < 2 else (rim, r),
    )
    for n, row in enumerate((-1, height - 1)):
        mask = pair_mask(inside, place, limits, row)
        first_rows(
            finds[n], w1, taps2b, 2 * n, act1b, slope1b, 2 * n * pitch, groups, mask
        )
    last = height - 4
    finds = (
        lambda r: (taps2b, r) if r < 2 else (taps2, r - 2),
        lambda r: (taps2, last + r) if r < 2 else (taps2b, r),
    )
    for n in range(2):
        second_rows(finds[n], w2, act2b, slope2b, 2 * n * pitch, groups)
    cells = height * breadth
    first_parts = [(act1b, pitch, 2 * pitch), (act1, 0, (height - 2) * pitch)]
    second_parts = [(act2b, 0, 4 * pitch), (act2, 0, (height - 4) * pitch)]
    for layer, (parts, offset) in enumerate(((first_parts, 1), (second_parts, 2))):
        own = wide(span(groups, offset, offset + breadth), width)
        total = jnp.zeros((pitch, width), F32)
        for ref, start, count in parts:
            for at in range(start, start + count, pitch):
                total = total + ref[at : at + pitch, :]
        mean = jnp.sum(total * own, axis=0, keepdims=True) * (1.0 / cells)
        n = 0
        for ref, start, count in parts:
            for at in range(start, start + count, pitch):
                centred[layer, n : n + pitch, :] = ((ref[at : at + pitch, :] - mean) * own).astype(
                    BF
                )
                n += pitch
        stat[layer] = jnp.zeros(stat.shape[1:], F32)
        put_mean(stat.at[layer, 0:EXTRA], mean, 2)
        put_mean(stat.at[layer, EXTRA : 2 * EXTRA], mean, 1)
    rows = sent.shape[0] - EXTRA

    def put(at, value):
        sent[at : at + value.shape[0], :] = value.astype(BF)

    emit, finish = packer(width, rows, put)
    other = centred[1 - place[0]]
    panels(other, other, emit)
    finish()
    mine[...] = stat[place[0], EXTRA : EXTRA + 8, :]
    sent[rows:, :] = stat[1 - place[0], 0:EXTRA, :].astype(BF)


def hold(place, centred, keep):
    def put(at, value):
        keep[at : at + value.shape[0], :] = value

    own = centred[place[0]]
    emit, finish = packer(own.shape[1], keep.shape[0], put)
    panels(own, own, emit)
    finish()


def ring(dims, place, even, odd, taps2b, w1, w2, act2, slope2, rim, outer, buf):
    height, _, groups, limits = dims
    low = 3 - place[2]
    inside = span(groups, low, low + limits[1])
    finds = (
        lambda r: (outer, r) if r < 2 else (taps2b, r - 2),
        lambda r: (taps2b, 2 + r) if r < 2 else (outer, r),
    )
    for n, (one, two, row) in enumerate(((odd, even, -3), (even, odd, height + 1))):
        rim_taps(rim, [(one, two, r) for r in range(REACH)], place, buf, groups)
        mask = pair_mask(inside, place, limits, row)
        first_rows(lambda r: (rim, r), w1, outer, 2 * n, None, None, 0, groups, mask)
        second_rows(finds[n], w2, act2, slope2, 2 * n * groups * 16, groups)


def write_message(ref, part, rows_ref, centre):
    count = part.shape[0]
    rows_ref[...] = jnp.zeros(rows_ref.shape, F32)
    put_mean(rows_ref, centre, 2)
    ref[0:count, :] = part.astype(BF)
    ref[count:, :] = rows_ref[...].astype(BF)


def merge_pair(dims, place, keep, mine, got, share, centre_out, *rest):
    count, groups, blocks = dims
    messages, (full, left, right, rows_ref) = rest[: groups - 1], rest[groups - 1 :]
    rows = keep.shape[0]
    chunk = rows // groups

    def put(start, value):
        at = slice(start, start + value.shape[0])
        full[at, :] = keep[at, :] + got[at, :].astype(F32) + value

    means = [get_mean(mine[...], blocks, 1), get_mean(got[rows:, :], blocks, 2)]
    centre = spread(means, count, left, right, rows, put)
    centre_out[...] = jnp.zeros(centre_out.shape, F32)
    put_mean(centre_out, centre, 1)
    for k, ref in enumerate(messages, 1):
        at = pl.multiple_of((place[3] ^ k) * chunk, 16)
        write_message(ref, full[pl.ds(at, chunk), :], rows_ref, centre)
    share[...] = full[pl.ds(pl.multiple_of(place[3] * chunk, 16), chunk), :]


def merge_many(dims, final, place, share, mine, *rest):
    count, members, blocks = dims
    gots, rest = rest[: members - 1], rest[members - 1 :]
    chunk = share.shape[0]
    full, left, right, rows_ref = rest[-4:]

    def put(start, value):
        full[start : start + value.shape[0], :] = value

    means = [get_mean(mine[...], blocks, 1)]
    means += [get_mean(got[chunk:, :], blocks, 2) for got in gots]
    centre = spread(means, count, left, right, full.shape[0], put)
    total = share[...] + full[pl.ds(pl.multiple_of(place[3] * chunk, 16), chunk), :]
    for got in gots:
        total = total + got[0:chunk, :].astype(F32)
    if final is None:
        out, centre_out, sent = rest[:3]
        out[...] = total
        centre_out[...] = jnp.zeros(centre_out.shape, F32)
        put_mean(centre_out, centre, 1)
        write_message(sent, total, rows_ref, centre)
    else:
        goal, sent, both = rest[:3]
        part = total * (1.0 / final) - goal[...]
        sent[...] = part.astype(BF)
        write_message(both, part, rows_ref, centre)


def back(dims, members, place, *rest):
    (act1, slope1, act1b, slope1b, act2, slope2, act2b, slope2b, act2r, slope2r) = rest[:10]
    pieces, rest = rest[10 : 10 + 2 * members], rest[10 + 2 * members :]
    (w2, w1, out, taps2, taps1, first_m, second_m, table, buf) = rest
    height, breadth, groups, limits = dims
    pitch = groups * 16
    step = 2 * pitch
    width = act1.shape[1]
    blocks = width // BLOCK
    packed = table.shape[1] - EXTRA
    chunk = packed // members
    for n, ref in enumerate(pieces):
        core = place[0] if n < members else 1 - place[0]
        at = pl.multiple_of((place[3] ^ (n % members)) * chunk, 16)
        table[core, pl.ds(at, chunk), :] = ref[0:chunk, :]
        if n % members == 0:
            table[core, packed:, :] = ref[chunk:, :]
    means, (row, col) = [], corners()
    for layer, ref in enumerate((first_m, second_m)):
        for n, (i, j) in enumerate(pairs(width)):
            block = table[layer, n * BLOCK : (n + 1) * BLOCK, :]
            ref[i * BLOCK : (i + 1) * BLOCK, j * BLOCK : (j + 1) * BLOCK] = block
            ref[j * BLOCK : (j + 1) * BLOCK, i * BLOCK : (i + 1) * BLOCK] = block.T
        for n in range(blocks // 2):
            at = (len(pairs(width)) + n) * BLOCK
            both = table[layer, at : at + BLOCK, :].astype(F32)
            at = (len(pairs(width)) + blocks // 2) * BLOCK
            line = table[layer, at : at + 16, :].astype(F32)[n : n + 1]
            turned = both.T
            one = jnp.where(row <= col, both, turned)
            two = jnp.where(row > col, both, jnp.where(row == col, line, turned))
            for i, block in ((2 * n, one), (2 * n + 1, two)):
                at = slice(i * BLOCK, (i + 1) * BLOCK)
                ref[at, at] = block.astype(BF)
        means.append(get_mean(table[layer, packed:, :], blocks, 2))
    low = 2 - place[2]
    inside2 = span(groups, low, low + limits[1])
    tiles2 = [(act2r, slope2r, 0), (act2b, slope2b, 0)]
    tiles2 += [(act2, slope2, t * pitch) for t in range(0, height - 4, 2)]
    tiles2 += [(act2b, slope2b, step), (act2r, slope2r, step)]

    def second(t):
        act, slope, at = tiles2[t]
        centred = (act[at : at + step, :] - means[1]).astype(BF)
        mask = wide(pair_mask(inside2, place, limits, 2 * t - 2), 2 * BLOCK)
        for lanes in halves(width):
            push = jnp.dot(centred, second_m[:, lanes], preferred_element_type=F32)
            grad = push * slope[at : at + step, lanes] * mask
            for r in range(2):
                write_taps(taps2, 2 * t + r, grad[r * pitch : (r + 1) * pitch], groups, lanes)

    low = 1 - place[2]
    inside1 = span(groups, low, low + limits[1])
    tiles1 = [(act1b, slope1b, 0)]
    tiles1 += [(act1, slope1, t * pitch) for t in range(0, height - 2, 2)]
    tiles1 += [(act1b, slope1b, step)]

    def first(t):
        act, slope, at = tiles1[t]
        centred = (act[at : at + step, :] - means[0]).astype(BF)
        mask = wide(pair_mask(inside1, place, limits, 2 * t - 1), 2 * BLOCK)
        for lanes in halves(width):
            flow = conv(lambda r: (taps2, 2 * t + r), w2, groups, lanes) + jnp.dot(
                centred, first_m[:, lanes], preferred_element_type=F32
            )
            grad = flow * slope[at : at + step, lanes] * mask
            for r in range(2):
                write_taps(taps1, 2 * t + r, grad[r * pitch : (r + 1) * pitch], groups, lanes)

    def last(t):
        got = conv(lambda r: (taps1, 2 * t + r), w1, groups, slice(None))
        for r in range(2):
            at = (2 * t + r) * pitch
            for p in range(buf.shape[0]):
                lanes = slice(p * BLOCK, (p + 1) * BLOCK)
                for n in range(groups):
                    part = got[r * pitch + n * 16 : r * pitch + (n + 1) * 16, lanes]
                    buf[p, pl.ds(at + n, 16, stride=groups), :] = part
                out[2 * t + r, :, lanes] = buf[p, at : at + breadth, :]

    for t in range(len(tiles2)):
        second(t)
    for t in range(len(tiles1)):
        first(t)
    for t in range(height // 2):
        last(t)


def edges(place, pool_hbm, far, near, strips, sems):
    breadth = pool_hbm.shape[1]
    ends = (0, breadth - 8)
    loads = [
        pltpu.make_async_copy(pool_hbm.at[:, pl.ds(at, 8), :], strips.at[n], sems.at[n])
        for n, at in enumerate(ends)
    ]
    for load in loads:
        load.start()
    for load in loads:
        load.wait()
    left_core = place[0] == 0
    left, right = strips[0, :, 0:REACH, :], strips[1, :, 8 - REACH :, :]
    far[...] = jnp.where(left_core, left, right).astype(BF)
    near[...] = jnp.where(left_core, right, left).astype(BF)


def bands(place, pool, far, near, even, odd, row):
    height, breadth, _ = pool.shape
    left_core = place[0] == 0
    odd_row = place[3] & 1
    for start, ref in ((1 - odd_row, even), (odd_row, odd)):
        for r in range(REACH):
            at = start * (height - REACH) + r
            one, two = far[at].astype(F32), near[at].astype(F32)
            row[0:REACH, :] = jnp.where(left_core, one, two)
            row[REACH : REACH + breadth, :] = pool[at]
            row[REACH + breadth :, :] = jnp.where(left_core, two, one)
            ref[r] = row[...].astype(BF)


def flip(weight, out):
    taps, _, width = weight.shape

    def one(t, carry):
        at = pl.multiple_of(t * width, 16)
        out[pl.ds(at, width), :] = weight[taps - 1 - t].T
        return carry

    lax.fori_loop(0, taps, one, 0)


def aim(place, targets, goal, full):
    core = place[0]
    chunk = goal.shape[0]

    def put(start, value):
        full[start : start + value.shape[0], :] = value

    blocks = targets.shape[1] // BLOCK
    emit, finish = packer(targets.shape[1], full.shape[0], put)
    for i in range(blocks):
        for j in range(i, blocks):
            rows, cols = slice(i * BLOCK, (i + 1) * BLOCK), slice(j * BLOCK, (j + 1) * BLOCK)
            emit(i, j, (targets[core, rows, cols] + targets[core, cols, rows].T) * 0.5)
    finish()
    goal[...] = full[pl.ds(pl.multiple_of(place[3] * chunk, 16), chunk), :]


def locate(height, breadth):
    row, tile = lax.axis_index("grp"), lax.axis_index("tile")
    return tile & 1, row * height, tile * breadth, row


def call(body, ins, outs, scratch, flops=0, limit=None, far=()):
    if isinstance(ins[0], tuple):
        (height, breadth), inner, ins = ins[0], body, ins[1:]

        def body(*refs):
            inner(locate(height, breadth), *refs)

    ins = [
        pltpu.with_memory_space_constraint(x, pltpu.HBM) if n in far else x
        for n, x in enumerate(ins)
    ]
    moved = sum(x.size * x.dtype.itemsize for x in ins) + sum(
        x.size * x.dtype.itemsize for x in outs
    )
    return pl.pallas_call(
        body,
        out_shape=tuple(outs),
        in_specs=[HBM if n in far else VMEM for n in range(len(ins))],
        out_specs=tuple(VMEM for _ in outs),
        scratch_shapes=scratch,
        compiler_params=pltpu.CompilerParams(vmem_limit_bytes=(limit or 8) * MIB),
        cost_estimate=pl.CostEstimate(flops=flops, bytes_accessed=moved, transcendentals=0),
    )(*ins)


def shape(dims, dtype):
    return jax.ShapeDtypeStruct(dims, dtype)


def local(pool_input, weight_first, weight_second, targets):
    height, breadth, depth = pool_input.shape
    width = weight_first.shape[3]
    groups, tiles = lax.axis_size("grp"), lax.axis_size("tile")
    chips = tiles // 2
    cells = height * breadth
    positions = cells * groups * tiles
    fold = -(-(breadth + 2 * REACH) // 16)
    pitch, wider = fold * 16, (fold + 2) * 16
    blocks = width // BLOCK
    place = (height, breadth)
    dims = (height, breadth, fold, (height * groups, breadth * tiles))
    swap = [(i, i ^ 1) for i in range(tiles)]
    cross = [(i, i + 1) for i in range(1, tiles - 1, 2)]
    cross = cross + [(j, i) for i, j in cross]

    rim = shape((height, REACH, depth), BF)
    far, near = call(
        edges,
        [place, pool_input],
        [rim] * 2,
        [pltpu.VMEM((2, height, 8, depth), F32), pltpu.SemaphoreType.DMA((2,))],
        flops=4 * 10**9,
        far=(0,),
    )
    far = lax.ppermute(far, "tile", cross)
    near = lax.ppermute(near, "tile", swap)
    band = shape((REACH, breadth + 2 * REACH, depth), BF)
    even, odd = call(
        bands,
        [place, pool_input, far, near],
        [band] * 2,
        [pltpu.VMEM((breadth + 2 * REACH, depth), F32)],
        flops=6 * 10**9,
    )

    def couples(start):
        ways = [(i, i + 1) for i in range(start, groups - 1, 2)]
        return ways + [(j, i) for i, j in ways]

    even = lax.ppermute(even, "grp", couples(0))
    odd = lax.ppermute(odd, "grp", couples(1))

    packed = packed_rows(width, groups)
    w1 = weight_first.reshape(-1, width)
    w2 = weight_second.reshape(-1, width)
    space = (fold * 15 + fold + 2 + 7) // 8 * 8

    def maps(rows):
        return [shape((rows * pitch, width), F32)] * 2

    def cost(rows_first, rows_second):
        return 2 * 9 * width * pitch * (rows_first * depth + rows_second * width)

    taps1, taps2, act1, slope1, act2, slope2 = call(
        functools.partial(middle, dims),
        [place, pool_input, far, near, w1, w2],
        [shape((height * wider, depth), BF), shape(((height - 2) * wider, width), BF)]
        + maps(height - 2)
        + maps(height - 4),
        [pltpu.VMEM((depth // BLOCK, height * space, BLOCK), F32)],
        flops=cost(height - 2, height - 4),
        limit=24,
    )
    taps2b, act1b, slope1b, act2b, slope2b, centred, mine, sent = call(
        functools.partial(front, dims),
        [place, even, odd, taps1, taps2, act1, act2, w1, w2],
        [shape((4 * wider, width), BF)]
        + maps(4)
        + maps(4)
        + [
            shape((2, height * pitch, width), BF),
            shape((8, BLOCK), F32),
            shape((packed + EXTRA, BLOCK), BF),
        ],
        [
            pltpu.VMEM((4 * wider, depth), BF),
            pltpu.VMEM((depth // BLOCK, 4 * space, BLOCK), F32),
            pltpu.VMEM((2, 2 * EXTRA, BLOCK), F32),
        ],
        flops=cost(4, 4),
        limit=24,
    )
    act2r, slope2r = call(
        functools.partial(ring, dims),
        [place, even, odd, taps2b, w1, w2],
        maps(4),
        [
            pltpu.VMEM((4 * wider, depth), BF),
            pltpu.VMEM((4 * wider, width), BF),
            pltpu.VMEM((depth // BLOCK, 4 * space, BLOCK), F32),
        ],
        flops=cost(4, 4),
        limit=16,
    )
    chunk = packed // groups
    (goal,) = call(
        aim,
        [place, targets],
        [shape((chunk, BLOCK), F32)],
        [pltpu.VMEM((packed, BLOCK), F32)],
        flops=2 * 10**8,
    )

    def turned(weight, inner):
        (out,) = call(
            flip,
            [weight.reshape(9, inner, width)],
            [shape((9 * width, inner), BF)],
            [],
            flops=2 * 10**9,
            limit=16,
        )
        return out

    back2 = turned(w2, width)
    back1 = turned(w1, depth)

    def helpers(members):
        deep = -(-3 * members // 16) * 16
        return [
            pltpu.VMEM((packed, BLOCK), F32),
            pltpu.VMEM((deep, width), F32),
            pltpu.VMEM((deep, width), F32),
            pltpu.VMEM((EXTRA, BLOCK), F32),
        ]

    message = shape((chunk + EXTRA, BLOCK), BF)
    part, centre = shape((chunk, BLOCK), F32), shape((8, BLOCK), F32)
    got = lax.ppermute(sent, "tile", swap)
    (keep,) = call(
        hold,
        [place, centred],
        [shape((packed, BLOCK), F32)],
        [],
        flops=2 * width * width * height * pitch,
    )
    share, mean, *sents = call(
        functools.partial(merge_pair, (cells, groups, blocks)),
        [place, keep, mine, got],
        [part, centre] + [message] * (groups - 1),
        helpers(2),
    )
    gots = [
        lax.ppermute(sents[k - 1], "grp", [(i, i ^ k) for i in range(groups)])
        for k in range(1, groups)
    ]
    share, mean, sent = call(
        functools.partial(merge_many, (2 * cells, groups, blocks), None),
        [place, share, mean] + gots,
        [part, centre, message],
        helpers(groups),
    )
    gots = [
        lax.ppermute(sent, "tile", [(i, i ^ (2 * k)) for i in range(tiles)])
        for k in range(1, chips)
    ]
    share, both = call(
        functools.partial(merge_many, (2 * groups * cells, chips, blocks), positions),
        [place, share, mean] + gots + [goal],
        [shape((chunk, BLOCK), BF), message],
        helpers(chips),
    )
    gots = [
        lax.ppermute(share, "grp", [(i, i ^ k) for i in range(groups)])
        for k in range(1, groups)
    ]
    mine = [both] + gots
    other = [lax.ppermute(piece, "tile", swap) for piece in mine]
    maps_in = [act1, slope1, act1b, slope1b, act2, slope2, act2b, slope2b, act2r, slope2r]
    (out,) = call(
        functools.partial(back, dims, groups),
        [place] + maps_in + mine + other + [back2, back1],
        [shape(pool_input.shape, F32)],
        [
            pltpu.VMEM(((height + 4) * wider, width), BF),
            pltpu.VMEM(((height + 2) * wider, width), BF),
            pltpu.VMEM((width, width), BF),
            pltpu.VMEM((width, width), BF),
            pltpu.VMEM((2, packed + EXTRA, BLOCK), BF),
            pltpu.VMEM((depth // BLOCK, height * pitch, BLOCK), F32),
        ],
        flops=2 * 9 * width * pitch * ((height + 2) * width + height * depth),
        limit=32,
    )
    return out


def solution(mesh):
    return jax.shard_map(
        local,
        mesh=mesh,
        in_specs=(P("grp", "tile", None), P(), P(), P()),
        out_specs=P("grp", "tile", None),
        check_vma=False,
    )
```

```python
import functools

import jax
import jax.numpy as jnp
from jax import lax
from jax.experimental import pallas as pl
from jax.experimental.pallas import tpu as pltpu
from jax.sharding import PartitionSpec as P


GELU_SCALE = 0.7978845608
GELU_CUBIC = 0.044715
REACH = 4
BLOCK = 128
EXTRA = 16
BF = jnp.bfloat16
F32 = jnp.float32
VMEM = pl.BlockSpec(memory_space=pltpu.VMEM)
HBM = pl.BlockSpec(memory_space=pltpu.HBM)
MIB = 2**20


def gelu_pair(values):
    square = values * values
    hyper = jnp.tanh(GELU_SCALE * (values + GELU_CUBIC * values * square))
    half = 0.5 * (1.0 + hyper)
    slope = half + 0.5 * values * (1.0 - hyper * hyper) * (
        GELU_SCALE + 3.0 * GELU_SCALE * GELU_CUBIC * square
    )
    return values * half, slope


def pairs(width):
    blocks = width // BLOCK
    return [(i, j) for i in range(blocks) for j in range(i + 1, blocks)]


def packed_rows(width, groups):
    return (len(pairs(width)) + width // BLOCK // 2) * BLOCK + 16 * groups


def corners():
    row = lax.broadcasted_iota(jnp.int32, (BLOCK, BLOCK), 0)
    return row, lax.broadcasted_iota(jnp.int32, (BLOCK, BLOCK), 1)


def packer(width, rows, put):
    places, held, lines = pairs(width), {}, []
    row, col = corners()

    def emit(i, j, block):
        if i != j:
            put(places.index((i, j)) * BLOCK, block)
        elif i % 2 == 0:
            held[i] = block
        else:
            both = jnp.where(row <= col, held[i - 1], block)
            put((len(places) + i // 2) * BLOCK, both)
            lines.append(jnp.sum(jnp.where(row == col, block, 0.0), axis=0, keepdims=True))

    def finish():
        start = (len(places) + len(lines)) * BLOCK
        at = lax.broadcasted_iota(jnp.int32, (rows - start, BLOCK), 0)
        value = jnp.zeros((rows - start, BLOCK), F32)
        for n, line in enumerate(lines):
            value = jnp.where(at == n, line, value)
        put(start, value)

    return emit, finish


def wide(mask, width):
    return jnp.concatenate([mask] * (width // BLOCK), axis=1)


def columns(groups):
    n = lax.broadcasted_iota(jnp.int32, (groups * 16, BLOCK), 0)
    return (n & 15) * groups + (n >> 4)


def span(groups, low, high):
    col = columns(groups)
    return jnp.where((col >= low) & (col < high), 1.0, 0.0).astype(F32)


def pair_mask(inside, place, limits, row):
    parts = []
    for r in range(2):
        at = place[1] + row + r
        parts.append(inside * jnp.where((at >= 0) & (at < limits[0]), 1.0, 0.0).astype(F32))
    return jnp.concatenate(parts, axis=0)


def roll_group(value):
    return [pltpu.roll(value[n * 16 : (n + 1) * 16], 15, 0) for n in range(2)]


def write_taps(ref, row, value, groups, lanes=slice(None)):
    at, pitch = row * (groups + 2) * 16, groups * 16
    ref[at : at + pitch, lanes] = value.astype(BF)
    for n, block in enumerate(roll_group(value)):
        ref[at + pitch + n * 16 : at + pitch + (n + 1) * 16, lanes] = block.astype(BF)


def fold_row(ref, row, buf_ref, at, groups):
    base = row * (groups + 2) * 16
    for n in range(groups + 2):
        for p in range(buf_ref.shape[0]):
            ref[base + n * 16 : base + (n + 1) * 16, p * BLOCK : (p + 1) * BLOCK] = buf_ref[
                p, pl.ds(at + n, 16, stride=groups), :
            ].astype(BF)


def put_row(buf_ref, at, value):
    for p in range(buf_ref.shape[0]):
        buf_ref[p, at : at + value.shape[0], :] = value[:, p * BLOCK : (p + 1) * BLOCK]


def clear_rows(buf_ref, start, stop):
    for p in range(buf_ref.shape[0]):
        buf_ref[p, start:stop, :] = jnp.zeros((stop - start, BLOCK), F32)


def conv(find, weight_ref, groups, lanes):
    pitch, pieces = groups * 16, []
    for a in range(3):
        for b in range(3):
            both = []
            for r in range(2):
                ref, row = find(r + a)
                at = (row * (groups + 2) + b) * 16
                both.append(ref[at : at + pitch, :])
            pieces.append(jnp.concatenate(both, axis=0))
    lhs = jnp.concatenate(pieces, axis=1)
    return jnp.dot(lhs, weight_ref[:, lanes], preferred_element_type=F32)


def halves(width):
    half = 2 * BLOCK
    return [slice(n, n + half) for n in range(0, width, half)]


def first_rows(find, w1, taps_ref, row, act, slope, at, groups, mask):
    width, pitch = w1.shape[1], groups * 16
    for lanes in halves(width):
        value, tilt = gelu_pair(conv(find, w1, groups, lanes))
        value = value * wide(mask, 2 * BLOCK)
        for r in range(2):
            one = value[r * pitch : (r + 1) * pitch]
            write_taps(taps_ref, row + r, one, groups, lanes)
            if act is None:
                continue
            two = tilt[r * pitch : (r + 1) * pitch]
            base = at + r * pitch
            for ref, part in ((act, one), (slope, two)):
                ref[base : base + pitch - 32, lanes] = part[32:]
                for n, block in enumerate(roll_group(part)):
                    to = base + pitch - 32 + n * 16
                    ref[to : to + 16, lanes] = block


def second_rows(find, w2, act, slope, at, groups):
    step = groups * 32
    for lanes in halves(w2.shape[1]):
        value, tilt = gelu_pair(conv(find, w2, groups, lanes))
        act[at : at + step, lanes] = value
        slope[at : at + step, lanes] = tilt


def put_mean(rows_ref, mean, parts):
    blocks = mean.shape[1] // BLOCK
    high = mean.astype(BF).astype(F32)
    for p, row in enumerate((high, mean - high) if parts == 2 else (mean,)):
        for j in range(blocks):
            at = p * blocks + j
            rows_ref[at : at + 1, :] = row[:, j * BLOCK : (j + 1) * BLOCK]


def get_mean(rows, blocks, parts):
    rows = rows.astype(F32)
    found = rows[:blocks] + rows[blocks : 2 * blocks] if parts == 2 else rows[:blocks]
    return jnp.concatenate([found[j : j + 1] for j in range(blocks)], axis=1)


def panels(lhs, rhs, emit):
    width = lhs.shape[1]
    for i in range(0, width, BLOCK):
        panel = lax.dot_general(
            lhs[:, i : i + BLOCK],
            rhs[:, i:],
            (((0,), (0,)), ((), ())),
            preferred_element_type=F32,
        )
        for j in range(0, width - i, BLOCK):
            emit(i // BLOCK, (i + j) // BLOCK, panel[:, j : j + BLOCK])


def spread(means, count, left_ref, right_ref, rows, put):
    centre = means[0]
    for mean in means[1:]:
        centre = centre + mean
    centre = centre * (1.0 / len(means))
    left_ref[...] = jnp.zeros(left_ref.shape, F32)
    right_ref[...] = jnp.zeros(right_ref.shape, F32)
    for n, mean in enumerate(means):
        away = mean - centre
        high = away.astype(BF).astype(F32)
        low = away - high
        for q, (lhs, rhs) in enumerate(((high, high), (high, low), (low, high))):
            at = 3 * n + q
            left_ref[at : at + 1, :] = lhs
            right_ref[at : at + 1, :] = rhs
    lhs, rhs = left_ref[...].astype(BF), right_ref[...].astype(BF)
    emit, finish = packer(lhs.shape[1], rows, lambda at, value: put(at, value * float(count)))
    panels(lhs, rhs, emit)
    finish()
    return centre


def middle(dims, place, pool, far, near, w1, w2, *rest):
    taps1, taps2, act1, slope1, act2, slope2, buf = rest
    height, breadth, groups, limits = dims
    pitch = groups * 16
    left_core = place[0] == 0
    space = buf.shape[1] // height
    for r in range(height):
        at = r * space
        one, two = far[r].astype(F32), near[r].astype(F32)
        put_row(buf, at, jnp.where(left_core, one, two))
        put_row(buf, at + REACH, pool[r])
        put_row(buf, at + REACH + breadth, jnp.where(left_core, two, one))
        clear_rows(buf, at + 2 * REACH + breadth, at + space)
        fold_row(taps1, r, buf, at, groups)
    low = 3 - place[2]
    inside = span(groups, low, low + limits[1])
    for t in range(0, height - 2, 2):
        mask = pair_mask(inside, place, limits, t + 1)
        first_rows(
            lambda r: (taps1, t + r), w1, taps2, t, act1, slope1, t * pitch, groups, mask
        )
        if t >= 2:
            second_rows(
                lambda r: (taps2, t - 2 + r), w2, act2, slope2, (t - 2) * pitch, groups
            )


def rim_taps(ref, rows, place, buf, groups):
    space = buf.shape[1] // len(rows)
    even = (place[3] & 1) == 0
    for n, (one, two, r) in enumerate(rows):
        breadth = one.shape[1]
        at = n * space
        put_row(buf, at, jnp.where(even, one[r].astype(F32), two[r].astype(F32)))
        clear_rows(buf, at + breadth, at + space)
        fold_row(ref, n, buf, at, groups)


def cell_parts(act1b, act1, act2b, act2, height, pitch):
    return (
        ([(act1b, pitch, 2 * pitch), (act1, 0, (height - 2) * pitch)], 1),
        ([(act2b, 0, 4 * pitch), (act2, 0, (height - 4) * pitch)], 2),
    )


def centre_cells(layers, which, mean, breadth, groups, out):
    pitch = groups * 16
    for layer, (parts, offset) in enumerate(layers):

        @pl.when(which == layer)
        def _(parts=parts, offset=offset):
            own, n = wide(span(groups, offset, offset + breadth), out.shape[1]), 0
            for ref, start, count in parts:
                for at in range(start, start + count, pitch):
                    out[n : n + pitch, :] = ((ref[at : at + pitch, :] - mean) * own).astype(BF)
                    n += pitch


def front(dims, place, even, odd, taps1, taps2, act1, act2, w1, w2, *rest):
    (taps2b, act1b, slope1b, act2b, slope2b, mine, sent) = rest[:7]
    (rim, buf, stat, centred) = rest[7:]
    height, breadth, groups, limits = dims
    pitch = groups * 16
    width = w1.shape[1]
    blocks = width // BLOCK
    rows = [(odd, even, REACH - 2), (odd, even, REACH - 1), (even, odd, 0), (even, odd, 1)]
    rim_taps(rim, rows, place, buf, groups)
    low = 3 - place[2]
    inside = span(groups, low, low + limits[1])
    last = height - 2
    finds = (
        lambda r: (rim, r) if r < 2 else (taps1, r - 2),
        lambda r: (taps1, last + r) if r < 2 else (rim, r),
    )
    for n, row in enumerate((-1, height - 1)):
        mask = pair_mask(inside, place, limits, row)
        first_rows(
            finds[n], w1, taps2b, 2 * n, act1b, slope1b, 2 * n * pitch, groups, mask
        )
    last = height - 4
    finds = (
        lambda r: (taps2b, r) if r < 2 else (taps2, r - 2),
        lambda r: (taps2, last + r) if r < 2 else (taps2b, r),
    )
    for n in range(2):
        second_rows(finds[n], w2, act2b, slope2b, 2 * n * pitch, groups)
    cells = height * breadth
    layers = cell_parts(act1b, act1, act2b, act2, height, pitch)
    for layer, (parts, offset) in enumerate(layers):
        own = wide(span(groups, offset, offset + breadth), width)
        total = jnp.zeros((pitch, width), F32)
        for ref, start, count in parts:
            for at in range(start, start + count, pitch):
                total = total + ref[at : at + pitch, :]
        mean = jnp.sum(total * own, axis=0, keepdims=True) * (1.0 / cells)
        stat[layer] = jnp.zeros(stat.shape[1:], F32)
        put_mean(stat.at[layer, 0:EXTRA], mean, 2)
        put_mean(stat.at[layer, EXTRA : 2 * EXTRA], mean, 1)
    mean = get_mean(stat[1 - place[0], EXTRA : EXTRA + 8, :], blocks, 1)
    centre_cells(layers, 1 - place[0], mean, breadth, groups, centred)
    rows = sent.shape[0] - EXTRA

    def put(at, value):
        sent[at : at + value.shape[0], :] = value.astype(BF)

    emit, finish = packer(width, rows, put)
    panels(centred[...], centred[...], emit)
    finish()
    mine[...] = stat[place[0], EXTRA : EXTRA + 8, :]
    sent[rows:, :] = stat[1 - place[0], 0:EXTRA, :].astype(BF)


def hold(dims, place, act1b, act1, act2b, act2, mine, keep, centred):
    height, breadth, groups, _ = dims
    layers = cell_parts(act1b, act1, act2b, act2, height, groups * 16)
    mean = get_mean(mine[...], centred.shape[1] // BLOCK, 1)
    centre_cells(layers, place[0], mean, breadth, groups, centred)

    def put(at, value):
        keep[at : at + value.shape[0], :] = value

    emit, finish = packer(centred.shape[1], keep.shape[0], put)
    panels(centred[...], centred[...], emit)
    finish()


def ring(dims, place, even, odd, taps2b, w1, w2, act2, slope2, rim, outer, buf):
    height, _, groups, limits = dims
    low = 3 - place[2]
    inside = span(groups, low, low + limits[1])
    finds = (
        lambda r: (outer, r) if r < 2 else (taps2b, r - 2),
        lambda r: (taps2b, 2 + r) if r < 2 else (outer, r),
    )
    for n, (one, two, row) in enumerate(((odd, even, -3), (even, odd, height + 1))):
        rim_taps(rim, [(one, two, r) for r in range(REACH)], place, buf, groups)
        mask = pair_mask(inside, place, limits, row)
        first_rows(lambda r: (rim, r), w1, outer, 2 * n, None, None, 0, groups, mask)
        second_rows(finds[n], w2, act2, slope2, 2 * n * groups * 16, groups)


def write_message(ref, part, rows_ref, centre):
    count = part.shape[0]
    rows_ref[...] = jnp.zeros(rows_ref.shape, F32)
    put_mean(rows_ref, centre, 2)
    ref[0:count, :] = part.astype(BF)
    ref[count:, :] = rows_ref[...].astype(BF)


def merge_pair(dims, place, keep, mine, got, share, centre_out, *rest):
    count, groups, blocks = dims
    messages, (full, left, right, rows_ref) = rest[: groups - 1], rest[groups - 1 :]
    rows = keep.shape[0]
    chunk = rows // groups

    def put(start, value):
        at = slice(start, start + value.shape[0])
        full[at, :] = keep[at, :] + got[at, :].astype(F32) + value

    means = [get_mean(mine[...], blocks, 1), get_mean(got[rows:, :], blocks, 2)]
    centre = spread(means, count, left, right, rows, put)
    centre_out[...] = jnp.zeros(centre_out.shape, F32)
    put_mean(centre_out, centre, 1)
    for k, ref in enumerate(messages, 1):
        at = pl.multiple_of((place[3] ^ k) * chunk, 16)
        write_message(ref, full[pl.ds(at, chunk), :], rows_ref, centre)
    share[...] = full[pl.ds(pl.multiple_of(place[3] * chunk, 16), chunk), :]


def merge_many(dims, final, place, share, mine, *rest):
    count, members, blocks = dims
    gots, rest = rest[: members - 1], rest[members - 1 :]
    chunk = share.shape[0]
    full, left, right, rows_ref = rest[-4:]

    def put(start, value):
        full[start : start + value.shape[0], :] = value

    means = [get_mean(mine[...], blocks, 1)]
    means += [get_mean(got[chunk:, :], blocks, 2) for got in gots]
    centre = spread(means, count, left, right, full.shape[0], put)
    total = share[...] + full[pl.ds(pl.multiple_of(place[3] * chunk, 16), chunk), :]
    for got in gots:
        total = total + got[0:chunk, :].astype(F32)
    if final is None:
        out, centre_out, sent = rest[:3]
        out[...] = total
        centre_out[...] = jnp.zeros(centre_out.shape, F32)
        put_mean(centre_out, centre, 1)
        write_message(sent, total, rows_ref, centre)
    else:
        goal, sent, both = rest[:3]
        part = total * (1.0 / final) - goal[...]
        sent[...] = part.astype(BF)
        write_message(both, part, rows_ref, centre)


def back(dims, members, place, *rest):
    (act1, slope1, act1b, slope1b, act2, slope2, act2b, slope2b, act2r, slope2r) = rest[:10]
    pieces, rest = rest[10 : 10 + 2 * members], rest[10 + 2 * members :]
    (w2, w1, out, taps2, taps1, first_m, second_m, table, buf) = rest
    height, breadth, groups, limits = dims
    pitch = groups * 16
    step = 2 * pitch
    width = act1.shape[1]
    blocks = width // BLOCK
    packed = table.shape[1] - EXTRA
    chunk = packed // members
    for n, ref in enumerate(pieces):
        core = place[0] if n < members else 1 - place[0]
        at = pl.multiple_of((place[3] ^ (n % members)) * chunk, 16)
        table[core, pl.ds(at, chunk), :] = ref[0:chunk, :]
        if n % members == 0:
            table[core, packed:, :] = ref[chunk:, :]
    means, (row, col) = [], corners()
    for layer, ref in enumerate((first_m, second_m)):
        for n, (i, j) in enumerate(pairs(width)):
            block = table[layer, n * BLOCK : (n + 1) * BLOCK, :]
            ref[i * BLOCK : (i + 1) * BLOCK, j * BLOCK : (j + 1) * BLOCK] = block
            ref[j * BLOCK : (j + 1) * BLOCK, i * BLOCK : (i + 1) * BLOCK] = block.T
        for n in range(blocks // 2):
            at = (len(pairs(width)) + n) * BLOCK
            both = table[layer, at : at + BLOCK, :].astype(F32)
            at = (len(pairs(width)) + blocks // 2) * BLOCK
            line = table[layer, at : at + 16, :].astype(F32)[n : n + 1]
            turned = both.T
            one = jnp.where(row <= col, both, turned)
            two = jnp.where(row > col, both, jnp.where(row == col, line, turned))
            for i, block in ((2 * n, one), (2 * n + 1, two)):
                at = slice(i * BLOCK, (i + 1) * BLOCK)
                ref[at, at] = block.astype(BF)
        means.append(get_mean(table[layer, packed:, :], blocks, 2))
    low = 2 - place[2]
    inside2 = span(groups, low, low + limits[1])
    tiles2 = [(act2r, slope2r, 0), (act2b, slope2b, 0)]
    tiles2 += [(act2, slope2, t * pitch) for t in range(0, height - 4, 2)]
    tiles2 += [(act2b, slope2b, step), (act2r, slope2r, step)]

    def second(t):
        act, slope, at = tiles2[t]
        centred = (act[at : at + step, :] - means[1]).astype(BF)
        mask = wide(pair_mask(inside2, place, limits, 2 * t - 2), 2 * BLOCK)
        for lanes in halves(width):
            push = jnp.dot(centred, second_m[:, lanes], preferred_element_type=F32)
            grad = push * slope[at : at + step, lanes] * mask
            for r in range(2):
                write_taps(taps2, 2 * t + r, grad[r * pitch : (r + 1) * pitch], groups, lanes)

    low = 1 - place[2]
    inside1 = span(groups, low, low + limits[1])
    tiles1 = [(act1b, slope1b, 0)]
    tiles1 += [(act1, slope1, t * pitch) for t in range(0, height - 2, 2)]
    tiles1 += [(act1b, slope1b, step)]

    def first(t):
        act, slope, at = tiles1[t]
        centred = (act[at : at + step, :] - means[0]).astype(BF)
        mask = wide(pair_mask(inside1, place, limits, 2 * t - 1), 2 * BLOCK)
        for lanes in halves(width):
            flow = conv(lambda r: (taps2, 2 * t + r), w2, groups, lanes) + jnp.dot(
                centred, first_m[:, lanes], preferred_element_type=F32
            )
            grad = flow * slope[at : at + step, lanes] * mask
            for r in range(2):
                write_taps(taps1, 2 * t + r, grad[r * pitch : (r + 1) * pitch], groups, lanes)

    def last(t):
        got = conv(lambda r: (taps1, 2 * t + r), w1, groups, slice(None))
        for r in range(2):
            at = (2 * t + r) * pitch
            for p in range(buf.shape[0]):
                lanes = slice(p * BLOCK, (p + 1) * BLOCK)
                for n in range(groups):
                    part = got[r * pitch + n * 16 : r * pitch + (n + 1) * 16, lanes]
                    buf[p, pl.ds(at + n, 16, stride=groups), :] = part
                out[2 * t + r, :, lanes] = buf[p, at : at + breadth, :]

    for t in range(len(tiles2)):
        second(t)
    for t in range(len(tiles1)):
        first(t)
    for t in range(height // 2):
        last(t)


def edges(place, pool_hbm, far, near, strips, sems):
    breadth = pool_hbm.shape[1]
    ends = (0, breadth - 8)
    loads = [
        pltpu.make_async_copy(pool_hbm.at[:, pl.ds(at, 8), :], strips.at[n], sems.at[n])
        for n, at in enumerate(ends)
    ]
    for load in loads:
        load.start()
    for load in loads:
        load.wait()
    left_core = place[0] == 0
    left, right = strips[0, :, 0:REACH, :], strips[1, :, 8 - REACH :, :]
    far[...] = jnp.where(left_core, left, right).astype(BF)
    near[...] = jnp.where(left_core, right, left).astype(BF)


def bands(place, pool, far, near, even, odd, row):
    height, breadth, _ = pool.shape
    left_core = place[0] == 0
    odd_row = place[3] & 1
    for start, ref in ((1 - odd_row, even), (odd_row, odd)):
        for r in range(REACH):
            at = start * (height - REACH) + r
            one, two = far[at].astype(F32), near[at].astype(F32)
            row[0:REACH, :] = jnp.where(left_core, one, two)
            row[REACH : REACH + breadth, :] = pool[at]
            row[REACH + breadth :, :] = jnp.where(left_core, two, one)
            ref[r] = row[...].astype(BF)


def flip(weight, out):
    taps, _, width = weight.shape

    def one(t, carry):
        at = pl.multiple_of(t * width, 16)
        out[pl.ds(at, width), :] = weight[taps - 1 - t].T
        return carry

    lax.fori_loop(0, taps, one, 0)


def aim(place, targets, goal, full):
    core = place[0]
    chunk = goal.shape[0]

    def put(start, value):
        full[start : start + value.shape[0], :] = value

    blocks = targets.shape[1] // BLOCK
    emit, finish = packer(targets.shape[1], full.shape[0], put)
    for i in range(blocks):
        for j in range(i, blocks):
            rows, cols = slice(i * BLOCK, (i + 1) * BLOCK), slice(j * BLOCK, (j + 1) * BLOCK)
            emit(i, j, (targets[core, rows, cols] + targets[core, cols, rows].T) * 0.5)
    finish()
    goal[...] = full[pl.ds(pl.multiple_of(place[3] * chunk, 16), chunk), :]


def locate(height, breadth):
    row, tile = lax.axis_index("grp"), lax.axis_index("tile")
    return tile & 1, row * height, tile * breadth, row


def call(body, ins, outs, scratch, flops=0, limit=None, far=()):
    if isinstance(ins[0], tuple):
        (height, breadth), inner, ins = ins[0], body, ins[1:]

        def body(*refs):
            inner(locate(height, breadth), *refs)

    ins = [
        pltpu.with_memory_space_constraint(x, pltpu.HBM) if n in far else x
        for n, x in enumerate(ins)
    ]
    moved = sum(x.size * x.dtype.itemsize for x in ins) + sum(
        x.size * x.dtype.itemsize for x in outs
    )
    return pl.pallas_call(
        body,
        out_shape=tuple(outs),
        in_specs=[HBM if n in far else VMEM for n in range(len(ins))],
        out_specs=tuple(VMEM for _ in outs),
        scratch_shapes=scratch,
        compiler_params=pltpu.CompilerParams(vmem_limit_bytes=(limit or 8) * MIB),
        cost_estimate=pl.CostEstimate(flops=flops, bytes_accessed=moved, transcendentals=0),
    )(*ins)


def shape(dims, dtype):
    return jax.ShapeDtypeStruct(dims, dtype)


def local(pool_input, weight_first, weight_second, targets):
    height, breadth, depth = pool_input.shape
    width = weight_first.shape[3]
    groups, tiles = lax.axis_size("grp"), lax.axis_size("tile")
    chips = tiles // 2
    cells = height * breadth
    positions = cells * groups * tiles
    fold = -(-(breadth + 2 * REACH) // 16)
    pitch, wider = fold * 16, (fold + 2) * 16
    blocks = width // BLOCK
    place = (height, breadth)
    dims = (height, breadth, fold, (height * groups, breadth * tiles))
    swap = [(i, i ^ 1) for i in range(tiles)]
    cross = [(i, i + 1) for i in range(1, tiles - 1, 2)]
    cross = cross + [(j, i) for i, j in cross]

    rim = shape((height, REACH, depth), BF)
    far, near = call(
        edges,
        [place, pool_input],
        [rim] * 2,
        [pltpu.VMEM((2, height, 8, depth), F32), pltpu.SemaphoreType.DMA((2,))],
        flops=4 * 10**9,
        far=(0,),
    )
    far = lax.ppermute(far, "tile", cross)
    near = lax.ppermute(near, "tile", swap)
    band = shape((REACH, breadth + 2 * REACH, depth), BF)
    even, odd = call(
        bands,
        [place, pool_input, far, near],
        [band] * 2,
        [pltpu.VMEM((breadth + 2 * REACH, depth), F32)],
        flops=6 * 10**9,
    )

    def couples(start):
        ways = [(i, i + 1) for i in range(start, groups - 1, 2)]
        return ways + [(j, i) for i, j in ways]

    even = lax.ppermute(even, "grp", couples(0))
    odd = lax.ppermute(odd, "grp", couples(1))

    packed = packed_rows(width, groups)
    w1 = weight_first.reshape(-1, width)
    w2 = weight_second.reshape(-1, width)
    space = (fold * 15 + fold + 2 + 7) // 8 * 8

    def maps(rows):
        return [shape((rows * pitch, width), F32)] * 2

    def cost(rows_first, rows_second):
        return 2 * 9 * width * pitch * (rows_first * depth + rows_second * width)

    taps1, taps2, act1, slope1, act2, slope2 = call(
        functools.partial(middle, dims),
        [place, pool_input, far, near, w1, w2],
        [shape((height * wider, depth), BF), shape(((height - 2) * wider, width), BF)]
        + maps(height - 2)
        + maps(height - 4),
        [pltpu.VMEM((depth // BLOCK, height * space, BLOCK), F32)],
        flops=cost(height - 2, height - 4),
        limit=24,
    )
    taps2b, act1b, slope1b, act2b, slope2b, mine, sent = call(
        functools.partial(front, dims),
        [place, even, odd, taps1, taps2, act1, act2, w1, w2],
        [shape((4 * wider, width), BF)]
        + maps(4)
        + maps(4)
        + [
            shape((8, BLOCK), F32),
            shape((packed + EXTRA, BLOCK), BF),
        ],
        [
            pltpu.VMEM((4 * wider, depth), BF),
            pltpu.VMEM((depth // BLOCK, 4 * space, BLOCK), F32),
            pltpu.VMEM((2, 2 * EXTRA, BLOCK), F32),
            pltpu.VMEM((height * pitch, width), BF),
        ],
        flops=cost(4, 4),
        limit=24,
    )
    act2r, slope2r = call(
        functools.partial(ring, dims),
        [place, even, odd, taps2b, w1, w2],
        maps(4),
        [
            pltpu.VMEM((4 * wider, depth), BF),
            pltpu.VMEM((4 * wider, width), BF),
            pltpu.VMEM((depth // BLOCK, 4 * space, BLOCK), F32),
        ],
        flops=cost(4, 4),
        limit=16,
    )
    chunk = packed // groups
    (goal,) = call(
        aim,
        [place, targets],
        [shape((chunk, BLOCK), F32)],
        [pltpu.VMEM((packed, BLOCK), F32)],
        flops=2 * 10**8,
    )

    def turned(weight, inner):
        (out,) = call(
            flip,
            [weight.reshape(9, inner, width)],
            [shape((9 * width, inner), BF)],
            [],
            flops=2 * 10**9,
            limit=16,
        )
        return out

    back2 = turned(w2, width)
    back1 = turned(w1, depth)

    def helpers(members):
        deep = -(-3 * members // 16) * 16
        return [
            pltpu.VMEM((packed, BLOCK), F32),
            pltpu.VMEM((deep, width), F32),
            pltpu.VMEM((deep, width), F32),
            pltpu.VMEM((EXTRA, BLOCK), F32),
        ]

    message = shape((chunk + EXTRA, BLOCK), BF)
    part, centre = shape((chunk, BLOCK), F32), shape((8, BLOCK), F32)
    got = lax.ppermute(sent, "tile", swap)
    (keep,) = call(
        functools.partial(hold, dims),
        [place, act1b, act1, act2b, act2, mine],
        [shape((packed, BLOCK), F32)],
        [pltpu.VMEM((height * pitch, width), BF)],
        flops=2 * width * width * height * pitch,
    )
    share, mean, *sents = call(
        functools.partial(merge_pair, (cells, groups, blocks)),
        [place, keep, mine, got],
        [part, centre] + [message] * (groups - 1),
        helpers(2),
    )
    gots = [
        lax.ppermute(sents[k - 1], "grp", [(i, i ^ k) for i in range(groups)])
        for k in range(1, groups)
    ]
    share, mean, sent = call(
        functools.partial(merge_many, (2 * cells, groups, blocks), None),
        [place, share, mean] + gots,
        [part, centre, message],
        helpers(groups),
    )
    gots = [
        lax.ppermute(sent, "tile", [(i, i ^ (2 * k)) for i in range(tiles)])
        for k in range(1, chips)
    ]
    share, both = call(
        functools.partial(merge_many, (2 * groups * cells, chips, blocks), positions),
        [place, share, mean] + gots + [goal],
        [shape((chunk, BLOCK), BF), message],
        helpers(chips),
    )
    gots = [
        lax.ppermute(share, "grp", [(i, i ^ k) for i in range(groups)])
        for k in range(1, groups)
    ]
    mine = [both] + gots
    other = [lax.ppermute(piece, "tile", swap) for piece in mine]
    maps_in = [act1, slope1, act1b, slope1b, act2, slope2, act2b, slope2b, act2r, slope2r]
    (out,) = call(
        functools.partial(back, dims, groups),
        [place] + maps_in + mine + other + [back2, back1],
        [shape(pool_input.shape, F32)],
        [
            pltpu.VMEM(((height + 4) * wider, width), BF),
            pltpu.VMEM(((height + 2) * wider, width), BF),
            pltpu.VMEM((width, width), BF),
            pltpu.VMEM((width, width), BF),
            pltpu.VMEM((2, packed + EXTRA, BLOCK), BF),
            pltpu.VMEM((depth // BLOCK, height * pitch, BLOCK), F32),
        ],
        flops=2 * 9 * width * pitch * ((height + 2) * width + height * depth),
        limit=32,
    )
    return out


def solution(mesh):
    return jax.shard_map(
        local,
        mesh=mesh,
        in_specs=(P("grp", "tile", None), P(), P(), P()),
        out_specs=P("grp", "tile", None),
        check_vma=False,
    )
```
